32 devices in a mesh: batch: 16 (over z, y, core), win: 2 (over x).
Axes of the slice: x: 2, y: 2, z: 4, core: 2. Of those that a mesh axis runs over, the one named last changes fastest.
Arguments:
- images: bfloat16 [64, 28, 28, 384], P('batch', 'win'), may hold values from -6 to 6
- valid_mask: int32 [64, 28, 28], P('batch', 'win'), may hold values 0 or 1
- cotangent: bfloat16 [64, 28, 28, 384], P('batch', 'win'), may hold values from -6 to 6
- conv_param: float32 [3, 10, 384], replicated, may hold values from -1.5 to 1.5
- norm_gain: float32 [4, 384], replicated, may hold values from 0.5 to 1.5
- norm_shift: float32 [4, 384], replicated, may hold values from -1 to 1
- qkv_weight: bfloat16 [2, 384, 1152], replicated, may hold values from -0.3125 to 0.3125
- attention_bias: float32 [7, 384], replicated, may hold values from -1 to 1
- out_weight: bfloat16 [2, 384, 384], replicated, may hold values from -1.25 to 1.25
- up_weight: bfloat16 [2, 384, 1536], replicated, may hold values from -0.3125 to 0.3125
- up_bias: float32 [2, 1536], replicated, may hold values from -1 to 1
- down_weight: bfloat16 [2, 1536, 384], replicated, may hold values from -0.15625 to 0.15625
- down_bias: float32 [2, 384], replicated, may hold values from -1 to 1
Outputs:
- output: float32 [64, 28, 28, 384], P('batch', 'win')
- images_grad: float32 [64, 28, 28, 384], P('batch', 'win')
- conv_grad: float32 [3, 10, 384], replicated
- gain_grad: float32 [4, 384], replicated
- shift_grad: float32 [4, 384], replicated
- qkv_grad: float32 [2, 384, 1152], replicated
- bias_grad: float32 [7, 384], replicated
- out_grad: float32 [2, 384, 384], replicated
- up_grad: float32 [2, 384, 1536], replicated
- up_bias_grad: float32 [2, 1536], replicated
- down_grad: float32 [2, 1536, 384], replicated
- down_bias_grad: float32 [2, 384], replicated
The draws below stay inside these ranges and needn't reach their ends.
Inputs may be any that keep to these rules, and one draw needn't show every extreme that they name: `valid_mask`: 0 marks a patch left out of the channel-attention sums.
All inputs are finite; a program needn't handle non-finite values. No bound on the sum of `valid_mask` on one device may be relied on, other than what follows from the above.
Results may differ from the reference program's by a relative error of at most 0.017.
Values may be sent and summed in bfloat16 or wider, within the bound.
No kernel may reach another device: no remote copies, remote signals or barrier semaphores. Data moves between devices by JAX's collectives and lax.ppermute only.
A program may use at most 256 MiB of HBM per device.

```python
import jax
import jax.numpy as jnp
from jax import lax

D = 384
HEADS = 12
HD = 32
FF = 1536
WIN = 7
SIDE = 28
IMG_DEV = 4
IMAGES = 64


def place_ends(values, own_key, low, top_value):
    longest = values.shape.index(max(values.shape))
    spots = []
    for shift in (0, 1):
        where = [jax.random.randint(jax.random.fold_in(own_key, axis), (), 0, length) for axis, length in enumerate(values.shape)]
        where[longest] = (where[longest] + shift) % values.shape[longest]
        spots.append(tuple(where))
    return values.at[spots[0]].set(low).at[spots[1]].set(top_value)


def shard_levels(key, shape, shards, low, high):
    factor_of, own = 1.0, jax.random.fold_in(key, 6)
    for dim, blocks in shards:
        steps = jnp.exp(jax.random.uniform(jax.random.fold_in(own, dim), (blocks,), jnp.float32, low / len(shards), high / len(shards)))
        factor_of = factor_of * jnp.repeat(steps, shape[dim] // blocks).reshape([-1 if axis == dim else 1 for axis in range(len(shape))])
    return factor_of


def gaussian(key, dims, scale, bound, cuts=(), held_as=jnp.bfloat16):
    loudness = shard_levels(key, dims, cuts, -0.22, 0.18) if cuts else 1.0
    drawn = jax.random.normal(key, dims, jnp.float32) * scale * loudness
    return jnp.minimum(jnp.maximum(drawn, -bound), bound).astype(held_as)


def setup_inputs(seed: int = 0) -> dict:
    splits = jax.random.split(jax.random.key(seed), 14)
    return {
        "images": gaussian(splits[0], (IMAGES, SIDE, SIDE, D), 1.0, 6.0, ((0, 16), (1, 2))),
        "valid_mask": place_ends((jax.random.randint(splits[1], (IMAGES, SIDE, SIDE), 0, 4) < 3).astype(jnp.int32), jax.random.fold_in(splits[1], 1), 0, 1),
        "cotangent": gaussian(splits[2], (IMAGES, SIDE, SIDE, D), 1.0, 6.0, ((0, 16), (1, 2))),
        "conv_param": gaussian(splits[3], (3, 10, D), 0.3, 1.5, (), jnp.float32),
        "norm_gain": jnp.clip(1.0 + 0.1 * jax.random.normal(splits[4], (4, D), jnp.float32), 0.5, 1.5),
        "norm_shift": gaussian(splits[5], (4, D), 0.2, 1.0, (), jnp.float32),
        "qkv_weight": gaussian(splits[6], (2, D, 3 * D), D ** -0.5, 0.3125),
        "attention_bias": gaussian(splits[7], (7, D), 0.2, 1.0, (), jnp.float32),
        "out_weight": gaussian(splits[8], (2, D, D), (D // 16) ** -0.5, 1.25),
        "up_weight": gaussian(splits[9], (2, D, FF), D ** -0.5, 0.3125),
        "up_bias": gaussian(splits[10], (2, FF), 0.2, 1.0, (), jnp.float32),
        "down_weight": gaussian(splits[11], (2, FF, D), FF ** -0.5, 0.15625),
        "down_bias": gaussian(splits[12], (2, D), 0.2, 1.0, (), jnp.float32),
    }


epsilon = 1e-05

@jax.custom_vjp
def low(v):
    return lax.optimization_barrier(v.astype(jnp.bfloat16)).astype(jnp.float32)

@jax.custom_vjp
def low_back(v):
    return v

def low_keep(v):
    return (low(v), None)

def low_pass(kept, grad):
    return (grad,)

def back_keep(v):
    return (v, None)

def back_low(kept, grad):
    return (low(grad),)
low.defvjp(low_keep, low_pass)
low_back.defvjp(back_keep, back_low)

def both_ways(inputs):
    return low(low_back(inputs))

def matmul(left, right):
    return jnp.dot(left, right, precision=lax.Precision.HIGHEST, preferred_element_type=jnp.float32)

def position(volume, kernel):
    row_count, col_count = (volume.shape[1], volume.shape[2])
    padded = jnp.pad(volume, ((0, 0), (1, 1), (1, 1), (0, 0)))
    summed = volume + kernel[9]
    for tap_row in range(3):
        for tap_col in range(3):
            summed = summed + padded[:, tap_row:tap_row + row_count, tap_col:tap_col + col_count, :] * kernel[3 * tap_row + tap_col]
    return summed

def layer_norm(volume, norm_gain, norm_shift):
    center = volume - lax.optimization_barrier(jnp.mean(volume, axis=-1, keepdims=True))
    spread = lax.optimization_barrier(jnp.mean(center * center, axis=-1, keepdims=True))
    return center * lax.rsqrt(spread + epsilon) * norm_gain + norm_shift

def to_windows(volume):
    image_count, row_count, col_count, depth = volume.shape
    blocks = volume.reshape(image_count, row_count // WIN, WIN, col_count // WIN, WIN, depth)
    return blocks.transpose(0, 1, 3, 2, 4, 5).reshape(-1, WIN * WIN, depth)

def from_windows(blocks, image_count, row_count, col_count):
    depth = blocks.shape[-1]
    volume = blocks.reshape(image_count, row_count // WIN, col_count // WIN, WIN, WIN, depth)
    return volume.transpose(0, 1, 3, 2, 4, 5).reshape(image_count, row_count, col_count, depth)

def window_attention(normed, weight, offset, out_matrix, out_offset):
    image_count, row_count, col_count = (normed.shape[0], normed.shape[1], normed.shape[2])
    flat_rows = low(normed).reshape(-1, D)
    joined = both_ways(matmul(flat_rows, weight) + offset)
    blocks = to_windows(joined.reshape(image_count, row_count, col_count, 3 * D))
    window_count = blocks.shape[0]
    queries = blocks[..., :D].reshape(window_count, WIN * WIN, HEADS, HD)
    key_rows = blocks[..., D:2 * D].reshape(window_count, WIN * WIN, HEADS, HD)
    value_rows = blocks[..., 2 * D:].reshape(window_count, WIN * WIN, HEADS, HD)
    scores = low_back(jnp.einsum('wqhc,wkhc->whqk', queries, key_rows, precision=lax.Precision.HIGHEST) * HD ** (-0.5))
    attend = low(jax.nn.softmax(scores, axis=-1))
    blended = jnp.einsum('whqk,wkhc->wqhc', attend, value_rows, precision=lax.Precision.HIGHEST)
    blended = from_windows(blended.reshape(window_count, WIN * WIN, D), image_count, row_count, col_count)
    blended = both_ways(blended.reshape(-1, D))
    return low_back(matmul(blended, out_matrix) + out_offset).reshape(normed.shape)

def channel_attention(normed, mask_col, weight, offset, out_matrix, out_offset):
    image_count = normed.shape[0]
    flat_rows = low(normed).reshape(-1, D)
    joined = both_ways(matmul(flat_rows, weight) + offset).reshape(image_count, -1, 3 * D)
    queries = (joined[..., :D] * mask_col).reshape(image_count, -1, HEADS, HD)
    key_rows = joined[..., D:2 * D].reshape(image_count, -1, HEADS, HD)
    value_rows = joined[..., 2 * D:].reshape(image_count, -1, HEADS, HD)
    gram = low_back(jnp.einsum('gnhi,gnhj->ghij', queries, key_rows, precision=lax.Precision.HIGHEST) / SIDE)
    mixing = low(jax.nn.softmax(gram, axis=-1))
    blended = jnp.einsum('ghij,gnhj->gnhi', mixing, value_rows, precision=lax.Precision.HIGHEST)
    blended = both_ways(blended.reshape(-1, D))
    return low_back(matmul(blended, out_matrix) + out_offset).reshape(normed.shape)

def feed_forward(normed, up_matrix, up_offset, down_matrix, down_offset):
    flat_rows = low(normed).reshape(-1, D)
    pre_act = low_back(matmul(flat_rows, up_matrix) + up_offset)
    hidden = low(jax.nn.gelu(pre_act, approximate=False))
    return low_back(matmul(hidden, down_matrix) + down_offset).reshape(normed.shape)

def forward(params, images, mask_col):
    conv_param, norm_gain, norm_shift, qkv_weight, attention_bias, out_weight, up_weight, up_bias, down_weight, down_bias = params
    pos_one = position(images, conv_param[0])
    window_offset = jnp.concatenate([attention_bias[0], jnp.zeros_like(attention_bias[0]), attention_bias[1]])
    resid_one = pos_one + window_attention(layer_norm(pos_one, norm_gain[0], norm_shift[0]), qkv_weight[0], window_offset, out_weight[0], attention_bias[2])
    pos_two = position(resid_one, conv_param[1])
    resid_two = pos_two + feed_forward(layer_norm(pos_two, norm_gain[1], norm_shift[1]), up_weight[0], up_bias[0], down_weight[0], down_bias[0])
    pos_three = position(resid_two, conv_param[2])
    resid_three = pos_three + channel_attention(layer_norm(pos_three, norm_gain[2], norm_shift[2]), mask_col, qkv_weight[1], attention_bias[3:6].reshape(-1), out_weight[1], attention_bias[6])
    return resid_three + feed_forward(layer_norm(resid_three, norm_gain[3], norm_shift[3]), up_weight[1], up_bias[1], down_weight[1], down_bias[1])

def reference(images, valid_mask, cotangent, conv_param, norm_gain, norm_shift, qkv_weight, attention_bias, out_weight, up_weight, up_bias, down_weight, down_bias):
    params = (conv_param.astype(jnp.float32), norm_gain.astype(jnp.float32), norm_shift.astype(jnp.float32), qkv_weight.astype(jnp.float32), attention_bias.astype(jnp.float32), out_weight.astype(jnp.float32), up_weight.astype(jnp.float32), up_bias.astype(jnp.float32), down_weight.astype(jnp.float32), down_bias.astype(jnp.float32))
    group_total = IMAGES // IMG_DEV
    image_groups = images.astype(jnp.float32).reshape(group_total, IMG_DEV, SIDE, SIDE, D)
    mask_groups = valid_mask.astype(jnp.float32).reshape(group_total, IMG_DEV, SIDE * SIDE, 1)
    cot_groups = cotangent.astype(jnp.float32).reshape(group_total, IMG_DEV, SIDE, SIDE, D)

    def group_step(totals, group_data):
        group_images, group_mask, group_cot = group_data
        result, pull_back = jax.vjp(lambda weights, inputs: forward(weights, inputs, group_mask), params, group_images)
        grad_params, grad_images = pull_back(group_cot)
        return (jax.tree.map(jnp.add, totals, grad_params), (result, grad_images))
    zero_grads = jax.tree.map(jnp.zeros_like, params)
    totals, (results, image_grads) = lax.scan(group_step, zero_grads, (image_groups, mask_groups, cot_groups))
    return (results.reshape(IMAGES, SIDE, SIDE, D), image_grads.reshape(IMAGES, SIDE, SIDE, D), totals[0], totals[1], totals[2], totals[3], totals[4], totals[5], totals[6], totals[7], totals[8], totals[9])
```

```python
import functools

import jax
import jax.numpy as jnp
import numpy as np
from jax import lax
from jax.experimental import pallas as pl
from jax.experimental.pallas import tpu as pltpu
from jax.sharding import PartitionSpec as P

D = 384
HEADS = 12
HD = 32
FF = 1536
WIN = 7
COLS = 28
WIDE = 32
SLOT = 64
GROUPS = 3
LANES = 128
SIDE = 28
CHUNK = 256
EPS = 1e-05
SCALE = HD ** (-0.5)
F32 = jnp.float32
BF16 = jnp.bfloat16

STRIP = WIN * WIDE
WROWS = 4 * SLOT


def constants():
    perm = np.zeros((WROWS, STRIP), np.float32)
    for window in range(4):
        for r in range(WIN):
            for c in range(WIN):
                perm[window * SLOT + r * WIN + c, r * WIDE + window * WIN + c] = 1.0
    heads_window = np.zeros((4 * SLOT, LANES), np.float32)
    heads_channel = np.zeros((LANES, LANES), np.float32)
    for head in range(4):
        heads_window[head * SLOT : (head + 1) * SLOT, head * HD : (head + 1) * HD] = 1.0
        heads_channel[head * HD : (head + 1) * HD, head * HD : (head + 1) * HD] = 1.0
    return (
        jnp.asarray(perm, BF16),
        jnp.asarray(perm.T, BF16),
        jnp.asarray(heads_window, BF16),
        jnp.asarray(heads_channel, BF16),
    )


def dot(left, right):
    return jnp.dot(left, right, preferred_element_type=F32)


def dot_nt(left, right):
    return lax.dot_general(left, right, (((1,), (1,)), ((), ())), preferred_element_type=F32)


def dot_tn(left, right):
    return lax.dot_general(left, right, (((0,), (0,)), ((), ())), preferred_element_type=F32)


def normalized(z):
    center = z - jnp.sum(z, axis=-1, keepdims=True) * (1.0 / D)
    spread = jnp.sum(center * center, axis=-1, keepdims=True) * (1.0 / D)
    scale = lax.rsqrt(spread + EPS)
    return center * scale, scale


def normalized_back(grad, z, gain):
    xhat, scale = normalized(z)
    scaled = grad * gain
    mean_one = jnp.sum(scaled, axis=-1, keepdims=True) * (1.0 / D)
    mean_two = jnp.sum(scaled * xhat, axis=-1, keepdims=True) * (1.0 / D)
    return (scaled - mean_one - xhat * mean_two) * scale, grad * xhat


TAIL = 0.39 * 0.5**0.5
ERFC = tuple(
    0.5 * c
    for c in (
        0.2353252479818039,
        0.091388231495776,
        0.6495598567387839,
        -0.6354008448449706,
        0.886664715384384,
        -0.2275372084398586,
    )
)


def gelu_pair(x):
    bell = jnp.exp(x * x * -0.5)
    t = 1.0 / (1.0 + TAIL * jnp.abs(x))
    poly = ERFC[5] * t + ERFC[4]
    for c in (ERFC[3], ERFC[2], ERFC[1], ERFC[0]):
        poly = poly * t + c
    tail = poly * t * bell
    below = jnp.where(x >= 0, 1.0 - tail, tail)
    return x * below, below + x * bell * ((2.0 * np.pi) ** -0.5)


def column_mask(rows):
    return lax.broadcasted_iota(jnp.int32, (rows, 1), 0) % WIDE < COLS


def folded(block):
    return jnp.sum(block.reshape(block.shape[0] // 8, 8, block.shape[1]), axis=0)


def conv_row(ext, row, kernel):
    above, here, below = ext[row], ext[row + 1], ext[row + 2]
    left = kernel[0] * above + kernel[3] * here + kernel[6] * below
    center = kernel[1] * above + (1.0 + kernel[4]) * here + kernel[7] * below + kernel[9]
    right = kernel[2] * above + kernel[5] * here + kernel[8] * below
    return center + pltpu.roll(left, 1, 0) + pltpu.roll(right, WIDE - 1, 0)


def conv_row_back(ext, row, kernel):
    above, here, below = ext[row], ext[row + 1], ext[row + 2]
    left = kernel[0] * below + kernel[3] * here + kernel[6] * above
    center = kernel[1] * below + (1.0 + kernel[4]) * here + kernel[7] * above
    right = kernel[2] * below + kernel[5] * here + kernel[8] * above
    return center + pltpu.roll(left, WIDE - 1, 0) + pltpu.roll(right, 1, 0)


def tap_sums(z, ext, row, taps_ref):
    shifted = (pltpu.roll(z, 1, 0), z, pltpu.roll(z, WIDE - 1, 0))
    for a in range(3):
        grad = ext[row + 2 - a]
        for b in range(3):
            taps_ref[3 * a + b] += folded(shifted[b] * grad)
    taps_ref[9] += folded(ext[row + 1])


def taps(ref, layer):
    return [ref[layer, j : j + 1, :] for j in range(10)]


def put_halo(ext, side, halo, rows):
    ext[0] = jnp.where(side == 1, halo, 0.0)
    ext[rows + 1] = jnp.where(side == 0, halo, 0.0)


def put_border(border_ref, side, first, last):
    border_ref[0] = jnp.where(side == 0, last, first)


def first_step():
    return pl.program_id(0) == 0


def last_step():
    return pl.program_id(0) == pl.num_programs(0) - 1


def clear(*refs):
    @pl.when(first_step())
    def _():
        for ref in refs:
            ref[...] = jnp.zeros_like(ref)


def column_sum(block):
    return jnp.sum(block.astype(F32), axis=0, keepdims=True)


def pack_tiles(out_ref, start, value):
    rows = value.shape[0]
    for j in range(value.shape[1] // LANES):
        out_ref[start + j * rows : start + (j + 1) * rows, :] = value[:, j * LANES : (j + 1) * LANES].astype(BF16)


def window_scores(q, k, heads, group):
    lanes = slice(group * LANES, (group + 1) * LANES)
    spread_q = jnp.concatenate([q[:, lanes]] * 4, axis=0) * heads
    return dot_nt(k[:, lanes], spread_q), spread_q


def per_head(block, heads):
    kept = block * heads
    return kept[:SLOT] + kept[SLOT : 2 * SLOT] + kept[2 * SLOT : 3 * SLOT] + kept[3 * SLOT :]


def stage_one(side_ref, img_ref, halo_ref, conv_ref, gain_ref, shift_ref, qkv_w, bias_ref, out_w, perm_ref, back_ref, heads_ref,
              pos_ref, nw_ref, qkv_ref, att_ref, mix_ref, res_ref, border_ref, ext, nrm):
    rows = img_ref.shape[1]
    side = side_ref[0]
    load_image(img_ref, halo_ref, side, ext)
    kernel = taps(conv_ref, 0)
    gain, shift = gain_ref[0:1, :], shift_ref[0:1, :]

    @pl.loop(0, rows)
    def _(r):
        z = conv_row(ext, r, kernel)
        pos_ref[0, r] = z
        xhat, _ = normalized(z)
        nrm[pl.ds(pl.multiple_of(r * WIDE, WIDE), WIDE), :] = (xhat * gain + shift).astype(BF16)

    heads = heads_ref[...]
    heads_f = heads.astype(F32)
    real = lax.broadcasted_iota(jnp.int32, (SLOT, 1), 0) < WIN * WIN
    mask = column_mask(STRIP)

    @pl.loop(0, rows // WIN)
    def _(s):
        image_rows = pl.ds(pl.multiple_of(s * STRIP, STRIP), STRIP)
        window_rows = pl.ds(pl.multiple_of(s * WROWS, WROWS), WROWS)
        nw = dot(perm_ref[...], nrm[image_rows, :]).astype(BF16)
        nw_ref[0, window_rows, :] = nw
        for part in range(3):
            cols = slice(part * D, (part + 1) * D)
            value = dot(nw, qkv_w[0, :, cols])
            if part != 1:
                value = value + bias_ref[part // 2 : part // 2 + 1, :]
            qkv_ref[0, window_rows, cols] = value.astype(BF16)
        for window in range(4):
            slot = pl.ds(pl.multiple_of(s * WROWS + window * SLOT, SLOT), SLOT)
            q, k, v = (qkv_ref[0, slot, part * D : (part + 1) * D] for part in range(3))
            for group in range(GROUPS):
                scores, _ = window_scores(q, k, heads, group)
                scores = jnp.where(real, scores * SCALE, -1e30)
                raised = jnp.exp(scores - jnp.max(scores, axis=0, keepdims=True))
                attend = raised * (1.0 / jnp.sum(raised, axis=0, keepdims=True))
                att_ref[0, slot, group * WROWS : (group + 1) * WROWS] = attend
                lanes = slice(group * LANES, (group + 1) * LANES)
                mixed = per_head(dot_tn(attend.astype(BF16), v[:, lanes]), heads_f)
                mix_ref[0, slot, lanes] = mixed.astype(BF16)
        mixed = dot(back_ref[...], mix_ref[0, window_rows, :]).astype(BF16)
        attn = (dot(mixed, out_w[0]) + bias_ref[2:3, :]).reshape(WIN, WIDE, D)
        strip = pl.ds(s * WIN, WIN)
        value = (pos_ref[0, strip] + attn).reshape(STRIP, D)
        res_ref[0, strip] = jnp.where(mask, value, 0.0).reshape(WIN, WIDE, D)

    put_border(border_ref, side, res_ref[0, 0], res_ref[0, rows - 1])


def load_image(img_ref, halo_ref, side, ext):
    rows = img_ref.shape[1]
    ext[...] = jnp.zeros_like(ext)

    @pl.loop(0, rows)
    def _(r):
        ext[r + 1, :COLS, :] = img_ref[0, r].astype(F32)

    halo = halo_ref[0].astype(F32)
    ext[0, :COLS, :] = jnp.where(side == 1, halo, 0.0)
    ext[rows + 1, :COLS, :] = jnp.where(side == 0, halo, 0.0)


def load_rows(x_ref, halo_ref, side, ext):
    rows = x_ref.shape[1]

    @pl.loop(0, rows)
    def _(r):
        ext[r + 1] = x_ref[0, r]

    put_halo(ext, side, halo_ref[0], rows)


def stage_two(side_ref, x_ref, halo_ref, conv_ref, gain_ref, shift_ref, up_w, upb_ref, down_w, downb_ref,
              pos_ref, nrm_ref, hid_ref, der_ref, res_ref, border_ref, ext):
    rows = x_ref.shape[1]
    side = side_ref[0]
    load_rows(x_ref, halo_ref, side, ext)
    kernel = taps(conv_ref, 1)
    gain, shift = gain_ref[1:2, :], shift_ref[1:2, :]

    @pl.loop(0, rows)
    def _(r):
        z = conv_row(ext, r, kernel)
        pos_ref[0, r] = z
        xhat, _ = normalized(z)
        nrm_ref[0, pl.ds(pl.multiple_of(r * WIDE, WIDE), WIDE), :] = (xhat * gain + shift).astype(BF16)

    mask = column_mask(STRIP)

    @pl.loop(0, rows // WIN)
    def _(s):
        part = pl.ds(pl.multiple_of(s * STRIP, STRIP), STRIP)
        nrm = nrm_ref[0, part, :]
        for c in range(FF // CHUNK):
            cols = slice(c * CHUNK, (c + 1) * CHUNK)
            hidden, slope = gelu_pair(dot(nrm, up_w[0, :, cols]) + upb_ref[0:1, cols])
            hid_ref[0, part, cols] = hidden.astype(BF16)
            der_ref[0, part, cols] = slope.astype(BF16)
        out = (dot(hid_ref[0, part, :], down_w[0]) + downb_ref[0:1, :]).reshape(WIN, WIDE, D)
        strip = pl.ds(s * WIN, WIN)
        value = (pos_ref[0, strip] + out).reshape(STRIP, D)
        res_ref[0, strip] = jnp.where(mask, value, 0.0).reshape(WIN, WIDE, D)

    put_border(border_ref, side, res_ref[0, 0], res_ref[0, rows - 1])


def gram_fold(left, right, heads_f):
    full = dot_tn(left, right) * heads_f
    return full[:HD] + full[HD : 2 * HD] + full[2 * HD : 3 * HD] + full[3 * HD :]


def stage_three(side_ref, x_ref, halo_ref, conv_ref, gain_ref, shift_ref, qkv_w, bias_ref, valid_ref, heads_ref,
                pos_ref, nrm_ref, qkv_ref, gram_ref, ext):
    rows = x_ref.shape[1]
    load_rows(x_ref, halo_ref, side_ref[0], ext)
    kernel = taps(conv_ref, 2)
    gain, shift = gain_ref[2:3, :], shift_ref[2:3, :]

    @pl.loop(0, rows)
    def _(r):
        z = conv_row(ext, r, kernel)
        pos_ref[0, r] = z
        xhat, _ = normalized(z)
        nrm_ref[0, pl.ds(pl.multiple_of(r * WIDE, WIDE), WIDE), :] = (xhat * gain + shift).astype(BF16)

    @pl.loop(0, rows // WIN)
    def _(s):
        part = pl.ds(pl.multiple_of(s * STRIP, STRIP), STRIP)
        nrm = nrm_ref[0, part, :]
        valid = valid_ref[0, part, :]
        for third in range(3):
            cols = slice(third * D, (third + 1) * D)
            value = (dot(nrm, qkv_w[0, :, cols]) + bias_ref[3 + third : 4 + third, :]).astype(BF16)
            if third == 0:
                value = (value.astype(F32) * valid).astype(BF16)
            qkv_ref[0, part, cols] = value

    heads_f = heads_ref[...].astype(F32)
    for group in range(GROUPS):
        low = group * LANES
        gram_ref[0, group * HD : (group + 1) * HD, :] = gram_fold(
            qkv_ref[0, :, D + low : D + low + LANES], qkv_ref[0, :, low : low + LANES], heads_f
        )


def channel_weights(gram):
    gram = gram * (1.0 / SIDE)
    raised = jnp.exp(gram - jnp.max(gram, axis=0, keepdims=True))
    return raised / jnp.sum(raised, axis=0, keepdims=True)


def block_diagonal(block, heads):
    return jnp.concatenate([block.astype(BF16)] * 4, axis=0) * heads


def stage_four(pos_ref, qkv_ref, gram_a, gram_b, cot_ref, out_w, bias_ref, gain_ref, shift_ref, up_w, upb_ref, down_w, downb_ref,
               heads_ref,
               out_ref, gres_ref, gm_ref, gchan_ref, pack_ref, small_ref,
               mix, cotf, cotb, res, nrm, hid, gpre, gn, gb, up_acc, down_acc, out_acc, sums):
    rows = pos_ref.shape[1]
    clear(up_acc, down_acc, out_acc, sums)
    heads = heads_ref[...]
    for group in range(GROUPS):
        low = group * LANES
        gram_rows = slice(group * HD, (group + 1) * HD)
        chan = block_diagonal(channel_weights(gram_a[0, gram_rows] + gram_b[0, gram_rows]), heads)
        mix[:, low : low + LANES] = dot(qkv_ref[0, :, 2 * D + low : 2 * D + low + LANES], chan).astype(BF16)

    cotf[...] = jnp.zeros_like(cotf)

    @pl.loop(0, rows)
    def _(r):
        cotf[r, :COLS, :] = cot_ref[0, r].astype(F32)
        cotb[pl.ds(pl.multiple_of(r * WIDE, WIDE), WIDE), :] = cotf[r].astype(BF16)

    gain, shift = gain_ref[3:4, :], shift_ref[3:4, :]

    @pl.loop(0, rows // WIN)
    def _(s):
        part = pl.ds(pl.multiple_of(s * STRIP, STRIP), STRIP)
        strip = pl.ds(s * WIN, WIN)
        attn = (dot(mix[part, :], out_w[0]) + bias_ref[6:7, :]).reshape(WIN, WIDE, D)
        res[strip] = pos_ref[0, strip] + attn

    @pl.loop(0, rows)
    def _(r):
        xhat, _ = normalized(res[r])
        nrm[pl.ds(pl.multiple_of(r * WIDE, WIDE), WIDE), :] = (xhat * gain + shift).astype(BF16)

    @pl.loop(0, rows // WIN)
    def _(s):
        part = pl.ds(pl.multiple_of(s * STRIP, STRIP), STRIP)
        strip = pl.ds(s * WIN, WIN)
        normed, cot = nrm[part, :], cotb[part, :]
        for c in range(FF // CHUNK):
            cols = slice(c * CHUNK, (c + 1) * CHUNK)
            hidden, slope = gelu_pair(dot(normed, up_w[0, :, cols]) + upb_ref[1:2, cols])
            hid[part, cols] = hidden.astype(BF16)
            grad = (slope * dot_nt(cot, down_w[0, cols, :])).astype(BF16)
            gpre[part, cols] = grad
            sums[:, cols] += folded(grad.astype(F32))
        value = (dot(hid[part, :], down_w[0]) + downb_ref[1:2, :]).reshape(WIN, WIDE, D) + res[strip]
        out_ref[0, strip] = value[:, :COLS, :]
        gn[strip] = dot_nt(gpre[part, :], up_w[0]).reshape(WIN, WIDE, D)

    @pl.loop(0, rows)
    def _(r):
        grad = gn[r]
        back, gain_term = normalized_back(grad, res[r], gain)
        cot = cotf[r]
        total = cot + back
        gres_ref[0, r] = total
        low = total.astype(BF16)
        gb[pl.ds(pl.multiple_of(r * WIDE, WIDE), WIDE), :] = low
        sums[:, FF : FF + D] += folded(cot)
        sums[:, FF + D : FF + 2 * D] += folded(gain_term)
        sums[:, FF + 2 * D : FF + 3 * D] += folded(grad)
        sums[:, FF + 3 * D : FF + 4 * D] += folded(low.astype(F32))

    up_acc[...] += dot_tn(nrm[...], gpre[...])
    down_acc[...] += dot_tn(cotb[...], hid[...])
    out_acc[...] += dot_tn(mix[...], gb[...])
    gm = dot_nt(gb[...], out_w[0]).astype(BF16)
    gm_ref[0] = gm
    heads_f = heads.astype(F32)
    for group in range(GROUPS):
        low = group * LANES
        gchan_ref[0, group * HD : (group + 1) * HD, :] = gram_fold(
            qkv_ref[0, :, 2 * D + low : 2 * D + low + LANES], gm[:, low : low + LANES], heads_f
        )

    @pl.when(last_step())
    def _():
        pack_tiles(pack_ref, 0, up_acc[...])
        pack_tiles(pack_ref, FF // LANES * D, down_acc[...].T)
        pack_tiles(pack_ref, 2 * FF // LANES * D, out_acc[...])
        for j in range(FF // D + 4):
            small_ref[j : j + 1, :] = jnp.sum(sums[:, j * D : (j + 1) * D], axis=0, keepdims=True)


def stage_five(side_ref, gres_ref, pos_ref, nrm_ref, qkv_ref, gm_ref, gram_a, gram_b, gchan_a, gchan_b, valid_ref, qkv_w, gain_ref,
               heads_ref,
               gpos_ref, border_ref, pack_ref, small_ref,
               joined, gn, qkv_acc, sums):
    rows = pos_ref.shape[1]
    clear(qkv_acc, sums)
    heads = heads_ref[...]
    valid = valid_ref[0]
    for group in range(GROUPS):
        low = group * LANES
        gram_rows = slice(group * HD, (group + 1) * HD)
        chan = channel_weights(gram_a[0, gram_rows] + gram_b[0, gram_rows])
        grad_chan = gchan_a[0, gram_rows] + gchan_b[0, gram_rows]
        grad_gram = chan * (grad_chan - jnp.sum(grad_chan * chan, axis=0, keepdims=True))
        chan, grad_gram = block_diagonal(chan, heads), block_diagonal(grad_gram, heads)
        lanes = slice(low, low + LANES)
        q, k = qkv_ref[0, :, lanes], qkv_ref[0, :, D + low : D + low + LANES]
        joined[:, lanes] = (dot(k, grad_gram) * (1.0 / SIDE) * valid).astype(BF16)
        joined[:, D + low : D + low + LANES] = (dot_nt(q, grad_gram) * (1.0 / SIDE)).astype(BF16)
        joined[:, 2 * D + low : 2 * D + low + LANES] = dot_nt(gm_ref[0, :, lanes], chan).astype(BF16)
    for third in range(3):
        cols = slice(third * D, (third + 1) * D)
        block = joined[:, cols]
        sums[:, cols] += folded(block.astype(F32))
        qkv_acc[:, cols] += dot_tn(nrm_ref[0], block)
    gn[...] = dot_nt(joined[...], qkv_w[0]).reshape(gn.shape)
    gain = gain_ref[2:3, :]

    @pl.loop(0, rows)
    def _(r):
        grad = gn[r]
        back, gain_term = normalized_back(grad, pos_ref[0, r], gain)
        gpos_ref[0, r] = gres_ref[0, r] + back
        sums[:, 3 * D : 4 * D] += folded(gain_term)
        sums[:, 4 * D : 5 * D] += folded(grad)

    put_border(border_ref, side_ref[0], gpos_ref[0, 0], gpos_ref[0, rows - 1])

    @pl.when(last_step())
    def _():
        pack_tiles(pack_ref, 0, qkv_acc[...])
        for j in range(5):
            small_ref[j : j + 1, :] = jnp.sum(sums[:, j * D : (j + 1) * D], axis=0, keepdims=True)


def stage_six(side_ref, g_ref, halo_ref, x_ref, pos_ref, nrm_ref, hid_ref, der_ref, conv_ref, gain_ref, up_w, down_w,
              gpos_ref, border_ref, pack_ref, small_ref,
              ext, gres, gb, gpre, gn, up_acc, down_acc, sums, tap_acc):
    rows = pos_ref.shape[1]
    clear(up_acc, down_acc, sums, tap_acc)
    load_rows(g_ref, halo_ref, side_ref[0], ext)
    kernel = taps(conv_ref, 2)
    mask = column_mask(WIDE)

    @pl.loop(0, rows)
    def _(r):
        back = jnp.where(mask, conv_row_back(ext, r, kernel), 0.0)
        gres[r] = back
        low = back.astype(BF16)
        gb[pl.ds(pl.multiple_of(r * WIDE, WIDE), WIDE), :] = low
        sums[:, FF : FF + D] += folded(low.astype(F32))
        tap_sums(x_ref[0, r], ext, r, tap_acc)

    @pl.loop(0, rows // WIN)
    def _(s):
        part = pl.ds(pl.multiple_of(s * STRIP, STRIP), STRIP)
        grad = gb[part, :]
        for c in range(FF // CHUNK):
            cols = slice(c * CHUNK, (c + 1) * CHUNK)
            block = (der_ref[0, part, cols].astype(F32) * dot_nt(grad, down_w[0, cols, :])).astype(BF16)
            gpre[part, cols] = block
            sums[:, cols] += folded(block.astype(F32))
        gn[pl.ds(s * WIN, WIN)] = dot_nt(gpre[part, :], up_w[0]).reshape(WIN, WIDE, D)

    gain = gain_ref[1:2, :]

    @pl.loop(0, rows)
    def _(r):
        grad = gn[r]
        back, gain_term = normalized_back(grad, pos_ref[0, r], gain)
        gpos_ref[0, r] = gres[r] + back
        sums[:, FF + D : FF + 2 * D] += folded(gain_term)
        sums[:, FF + 2 * D : FF + 3 * D] += folded(grad)

    put_border(border_ref, side_ref[0], gpos_ref[0, 0], gpos_ref[0, rows - 1])
    up_acc[...] += dot_tn(nrm_ref[0], gpre[...])
    down_acc[...] += dot_tn(gb[...], hid_ref[0])

    @pl.when(last_step())
    def _():
        pack_tiles(pack_ref, 0, up_acc[...])
        pack_tiles(pack_ref, FF // LANES * D, down_acc[...].T)
        for j in range(FF // D + 3):
            small_ref[j : j + 1, :] = jnp.sum(sums[:, j * D : (j + 1) * D], axis=0, keepdims=True)
        for j in range(10):
            small_ref[8 + j : 9 + j, :] = jnp.sum(tap_acc[j], axis=0, keepdims=True)


def stage_seven(side_ref, g_ref, halo_ref, x_ref, pos_ref, img_ref, imghalo_ref, nw_ref, qkv_ref, att_ref, mix_ref, conv_ref,
                gain_ref, qkv_w, out_w, perm_ref, back_ref, heads_ref,
                gpos_ref, border_ref, pack_ref, small_ref,
                ext, gres, gb, joined, gn, qkv_acc, out_acc, sums, tap_acc, tap_one):
    rows = pos_ref.shape[1]
    side = side_ref[0]
    clear(qkv_acc, out_acc, sums, tap_acc, tap_one)
    load_rows(g_ref, halo_ref, side, ext)
    kernel = taps(conv_ref, 1)
    mask = column_mask(WIDE)

    @pl.loop(0, rows)
    def _(r):
        back = jnp.where(mask, conv_row_back(ext, r, kernel), 0.0)
        gres[r] = back
        low = back.astype(BF16)
        gb[pl.ds(pl.multiple_of(r * WIDE, WIDE), WIDE), :] = low
        sums[:, 3 * D : 4 * D] += folded(low.astype(F32))
        tap_sums(x_ref[0, r], ext, r, tap_acc)

    heads = heads_ref[...]
    heads_f = heads.astype(F32)

    @pl.loop(0, rows // WIN)
    def _(s):
        image_rows = pl.ds(pl.multiple_of(s * STRIP, STRIP), STRIP)
        window_rows = pl.ds(pl.multiple_of(s * WROWS, WROWS), WROWS)
        gbw = dot(perm_ref[...], gb[image_rows, :]).astype(BF16)
        out_acc[...] += dot_tn(mix_ref[0, window_rows, :], gbw)
        gm_all = dot_nt(gbw, out_w[0]).astype(BF16)
        for window in range(4):
            slot = pl.ds(pl.multiple_of(s * WROWS + window * SLOT, SLOT), SLOT)
            gm = gm_all[window * SLOT : (window + 1) * SLOT]
            q, k, v = (qkv_ref[0, slot, part * D : (part + 1) * D] for part in range(3))
            out_rows = slice(window * SLOT, (window + 1) * SLOT)
            for group in range(GROUPS):
                lanes = slice(group * LANES, (group + 1) * LANES)
                attend = att_ref[0, slot, group * WROWS : (group + 1) * WROWS]
                grad_att, spread_gm = window_scores(gm, v, heads, group)
                spread_q = jnp.concatenate([q[:, lanes]] * 4, axis=0) * heads
                weighted = grad_att * attend
                grad_s = (weighted - attend * jnp.sum(weighted, axis=0, keepdims=True)).astype(BF16)
                gv = dot(attend.astype(BF16), spread_gm)
                gk = dot(grad_s, spread_q) * SCALE
                gq = per_head(dot_tn(grad_s, k[:, lanes]), heads_f) * SCALE
                low = group * LANES
                joined[out_rows, low : low + LANES] = gq.astype(BF16)
                joined[out_rows, D + low : D + low + LANES] = gk.astype(BF16)
                joined[out_rows, 2 * D + low : 2 * D + low + LANES] = gv.astype(BF16)
        nw = nw_ref[0, window_rows, :]
        for third in range(3):
            cols = slice(third * D, (third + 1) * D)
            block = joined[:, cols]
            qkv_acc[:, cols] += dot_tn(nw, block)
            if third != 1:
                sums[:, cols] += folded(block.astype(F32))
        unwound = dot(back_ref[...], joined[...]).astype(BF16)
        gn[pl.ds(s * WIN, WIN)] = dot_nt(unwound, qkv_w[0]).reshape(WIN, WIDE, D)

    gain = gain_ref[0:1, :]

    @pl.loop(0, rows)
    def _(r):
        grad = gn[r]
        back, gain_term = normalized_back(grad, pos_ref[0, r], gain)
        gpos_ref[0, r] = gres[r] + back
        sums[:, D : 2 * D] += folded(gain_term)
        sums[:, 4 * D : 5 * D] += folded(grad)

    put_border(border_ref, side, gpos_ref[0, 0], gpos_ref[0, rows - 1])
    load_image(img_ref, imghalo_ref, side, ext)

    @pl.loop(0, rows)
    def _(r):
        grad = gpos_ref[0, r]
        shifted = (pltpu.roll(grad, WIDE - 1, 0), grad, pltpu.roll(grad, 1, 0))
        for a in range(3):
            z = ext[r + a]
            for b in range(3):
                tap_one[3 * a + b] += folded(shifted[b] * z)
        tap_one[9] += folded(grad)

    @pl.when(last_step())
    def _():
        pack_tiles(pack_ref, 0, qkv_acc[...])
        pack_tiles(pack_ref, 3 * D // LANES * D, out_acc[...])
        for j in range(5):
            small_ref[j : j + 1, :] = jnp.sum(sums[:, j * D : (j + 1) * D], axis=0, keepdims=True)
        for j in range(10):
            small_ref[8 + j : 9 + j, :] = jnp.sum(tap_acc[j], axis=0, keepdims=True)
            small_ref[18 + j : 19 + j, :] = jnp.sum(tap_one[j], axis=0, keepdims=True)


def stage_eight(side_ref, g_ref, halo_ref, conv_ref, out_ref, ext):
    rows = g_ref.shape[1]
    load_rows(g_ref, halo_ref, side_ref[0], ext)
    kernel = taps(conv_ref, 0)

    @pl.loop(0, rows)
    def _(r):
        out_ref[0, r] = conv_row_back(ext, r, kernel)[:COLS]


VMEM_LIMIT = 60 * 1024 * 1024


def per_image(shape):
    return pl.BlockSpec((1,) + tuple(shape[1:]), lambda i: (i,) + (0,) * (len(shape) - 1))


def whole(shape):
    return pl.BlockSpec(tuple(shape), lambda i: (0,) * len(shape))


def layer(array, index):
    shape = array.shape
    return pl.BlockSpec((1,) + tuple(shape[1:]), lambda i: (index,) + (0,) * (len(shape) - 1))


def scalar():
    return pl.BlockSpec(memory_space=pltpu.SMEM)


def call(body, images, in_specs, outs, scratch, flops, name):
    return pl.pallas_call(
        body,
        name=name,
        grid=(images,),
        in_specs=in_specs,
        out_specs=[per_image(shape) if own else whole(shape) for shape, _, own in outs],
        out_shape=[jax.ShapeDtypeStruct(shape, dtype) for shape, dtype, _ in outs],
        scratch_shapes=scratch,
        compiler_params=pltpu.CompilerParams(dimension_semantics=("arbitrary",), vmem_limit_bytes=VMEM_LIMIT),
        cost_estimate=pl.CostEstimate(flops=flops, bytes_accessed=20_000_000, transcendentals=0),
    )


def exchange(array):
    return lax.ppermute(array, "win", [(0, 1), (1, 0)])


def shards(images, valid_mask, cotangent, conv, gain, shift, qkv_w, bias, out_w, up_w, up_b, down_w, down_b):
    n, rows = images.shape[0], images.shape[1]
    side = lax.axis_index("win")
    side_arr = side.astype(jnp.int32).reshape(1)
    perm, back, heads_w, heads_c = constants()
    wide = (n, rows, WIDE, D)
    flat = rows * WIDE
    wflat = rows // WIN * WROWS
    border = (n, WIDE, D)
    valid = jnp.pad(valid_mask.astype(F32), ((0, 0), (0, 0), (0, WIDE - COLS))).reshape(n, flat, 1)
    ext = pltpu.VMEM((rows + 2, WIDE, D), F32)

    def vm(shape, dtype=F32):
        return pltpu.VMEM(shape, dtype)

    edge = jnp.where(side == 0, images[:, rows - 1], images[:, 0])
    img_halo = exchange(edge)
    small_params = [whole(conv.shape), whole(gain.shape)]

    pos_one, nw, qkv_one, att, mix_one, res_one, edge = call(
        stage_one, n,
        [scalar(), per_image(images.shape), per_image(img_halo.shape), *small_params, whole(shift.shape), layer(qkv_w, 0),
         whole(bias.shape), layer(out_w, 0), whole(perm.shape), whole(back.shape), whole(heads_w.shape)],
        [(wide, F32, True), ((n, wflat, D), BF16, True), ((n, wflat, 3 * D), BF16, True), ((n, wflat, GROUPS * WROWS), F32, True),
         ((n, wflat, D), BF16, True), (wide, F32, True), (border, F32, True)],
        [ext, vm((flat, D), BF16)], 2_000_000_000, "window_forward",
    )(side_arr, images, img_halo, conv, gain, shift, qkv_w, bias, out_w, perm, back, heads_w)

    halo = exchange(edge)
    pos_two, nrm_two, hid_one, der_one, res_two, edge = call(
        stage_two, n,
        [scalar(), per_image(wide), per_image(border), *small_params, whole(shift.shape), layer(up_w, 0), whole(up_b.shape),
         layer(down_w, 0), whole(down_b.shape)],
        [(wide, F32, True), ((n, flat, D), BF16, True), ((n, flat, FF), BF16, True), ((n, flat, FF), BF16, True), (wide, F32, True),
         (border, F32, True)],
        [ext], 4_000_000_000, "mlp_one_forward",
    )(side_arr, res_one, halo, conv, gain, shift, up_w, up_b, down_w, down_b)

    halo = exchange(edge)
    gram_shape = (n, GROUPS * HD, LANES)
    pos_three, nrm_three, qkv_two, gram = call(
        stage_three, n,
        [scalar(), per_image(wide), per_image(border), *small_params, whole(shift.shape), layer(qkv_w, 1), whole(bias.shape),
         per_image(valid.shape), whole(heads_c.shape)],
        [(wide, F32, True), ((n, flat, D), BF16, True), ((n, flat, 3 * D), BF16, True), (gram_shape, F32, True)],
        [ext], 2_000_000_000, "channel_gram",
    )(side_arr, res_two, halo, conv, gain, shift, qkv_w, bias, valid, heads_c)

    gram_other = exchange(gram)
    mlp_rows = 2 * FF // LANES * D
    out_rows = D // LANES * D
    qkv_rows = 3 * D // LANES * D
    output, gres_three, gm_two, gchan, pack_four, small_four = call(
        stage_four, n,
        [per_image(wide), per_image(qkv_two.shape), per_image(gram_shape), per_image(gram_shape), per_image(cotangent.shape),
         layer(out_w, 1), whole(bias.shape), whole(gain.shape), whole(shift.shape), layer(up_w, 1), whole(up_b.shape),
         layer(down_w, 1), whole(down_b.shape), whole(heads_c.shape)],
        [(images.shape, F32, True), (wide, F32, True), ((n, flat, D), BF16, True), (gram_shape, F32, True),
         ((mlp_rows + out_rows, LANES), BF16, False), ((8, D), F32, False)],
        [vm((flat, D), BF16), vm((rows, WIDE, D)), vm((flat, D), BF16), vm((rows, WIDE, D)), vm((flat, D), BF16),
         vm((flat, FF), BF16), vm((flat, FF), BF16), vm((rows, WIDE, D)), vm((flat, D), BF16),
         vm((D, FF)), vm((D, FF)), vm((D, D)), vm((8, FF + 4 * D))],
        12_000_000_000, "mlp_two",
    )(pos_three, qkv_two, gram, gram_other, cotangent, out_w, bias, gain, shift, up_w, up_b, down_w, down_b, heads_c)

    gchan_other = exchange(gchan)
    gpos_three, edge, pack_five, small_five = call(
        stage_five, n,
        [scalar(), per_image(wide), per_image(wide), per_image(nrm_three.shape), per_image(qkv_two.shape), per_image(gm_two.shape),
         per_image(gram_shape), per_image(gram_shape), per_image(gram_shape), per_image(gram_shape), per_image(valid.shape),
         layer(qkv_w, 1), whole(gain.shape), whole(heads_c.shape)],
        [(wide, F32, True), (border, F32, True), ((qkv_rows, LANES), BF16, False), ((8, D), F32, False)],
        [vm((flat, 3 * D), BF16), vm((rows, WIDE, D)), vm((D, 3 * D)), vm((8, 5 * D))], 3_000_000_000, "channel_backward",
    )(side_arr, gres_three, pos_three, nrm_three, qkv_two, gm_two, gram, gram_other, gchan, gchan_other, valid, qkv_w, gain,
      heads_c)

    halo = exchange(edge)
    gpos_two, edge, pack_six, small_six = call(
        stage_six, n,
        [scalar(), per_image(wide), per_image(border), per_image(wide), per_image(wide), per_image(nrm_two.shape),
         per_image(hid_one.shape), per_image(der_one.shape), *small_params, layer(up_w, 0), layer(down_w, 0)],
        [(wide, F32, True), (border, F32, True), ((mlp_rows, LANES), BF16, False), ((24, D), F32, False)],
        [ext, vm((rows, WIDE, D)), vm((flat, D), BF16), vm((flat, FF), BF16), vm((rows, WIDE, D)), vm((D, FF)), vm((D, FF)),
         vm((8, FF + 3 * D)), vm((10, 8, D))], 8_000_000_000, "mlp_one_backward",
    )(side_arr, gpos_three, halo, res_two, pos_two, nrm_two, hid_one, der_one, conv, gain, up_w, down_w)

    halo = exchange(edge)
    gpos_one, edge, pack_seven, small_seven = call(
        stage_seven, n,
        [scalar(), per_image(wide), per_image(border), per_image(wide), per_image(wide), per_image(images.shape),
         per_image(img_halo.shape), per_image(nw.shape), per_image(qkv_one.shape), per_image(att.shape), per_image(mix_one.shape),
         *small_params, layer(qkv_w, 0), layer(out_w, 0), whole(perm.shape), whole(back.shape), whole(heads_w.shape)],
        [(wide, F32, True), (border, F32, True), ((qkv_rows + out_rows, LANES), BF16, False), ((32, D), F32, False)],
        [ext, vm((rows, WIDE, D)), vm((flat, D), BF16), vm((WROWS, 3 * D), BF16), vm((rows, WIDE, D)), vm((D, 3 * D)), vm((D, D)),
         vm((8, 5 * D)), vm((10, 8, D)), vm((10, 8, D))], 5_000_000_000, "window_backward",
    )(side_arr, gpos_two, halo, res_one, pos_one, images, img_halo, nw, qkv_one, att, mix_one, conv, gain, qkv_w, out_w, perm, back,
      heads_w)

    halo = exchange(edge)
    (images_grad,) = call(
        stage_eight, n, [scalar(), per_image(wide), per_image(border), whole(conv.shape)], [(images.shape, F32, True)], [ext],
        10_000_000, "images_backward",
    )(side_arr, gpos_one, halo, conv)

    small = jnp.concatenate([small_four, small_five, small_six, small_seven], axis=0)
    small = jnp.pad(small.reshape(-1, LANES), ((0, SMALL_ROWS - 3 * 72), (0, 0))).astype(BF16)
    joined = jnp.concatenate([pack_four, pack_five, pack_six, pack_seven, small], axis=0)
    summed = all_sum(joined)
    return (output, images_grad, *unpack(summed))


SMALL_ROWS = 512


def steps_of(batch):
    bits = list(range((batch // 2).bit_length() - 1))
    one = ["w", *bits]
    two = [*bits[:1], "w", *bits[1:]]
    return list(zip(one, two))


def flip(place, win, axis):
    if axis == "w":
        return place, 1 - win
    return place ^ (2 << axis), win


def all_sum(x):
    batch = lax.axis_size("batch")
    place, win = lax.axis_index("batch"), lax.axis_index("win")
    core = place % 2

    def trade(value, axes):
        pairs = []
        for b in range(batch):
            for w in range(2):
                axis = axes[b % 2]
                to = (b ^ 1, w) if axis == "c" else flip(b, w, axis)
                pairs.append((2 * b + w, 2 * to[0] + to[1]))
        return lax.ppermute(value, ("batch", "win"), pairs)

    def bit(axis):
        if axis == "c":
            return core
        return win if axis == "w" else (place // (2 << axis)) % 2

    order = [("c", "c"), *steps_of(batch)]
    bits = [jnp.where(core == 0, bit(one), bit(two)) for one, two in order]
    for axes, mine in zip(order, bits):
        half = x.shape[0] // 2
        sent = lax.dynamic_slice_in_dim(x, (1 - mine) * half, half, 0)
        kept = lax.dynamic_slice_in_dim(x, mine * half, half, 0)
        got = trade(sent, axes)
        x = (kept.astype(F32) + got.astype(F32)).astype(BF16)
    for axes, mine in zip(order[::-1], bits[::-1]):
        got = trade(x, axes)
        x = jnp.concatenate([jnp.where(mine == 0, x, got), jnp.where(mine == 0, got, x)], axis=0)
    return x


def untile(x, start, height, width):
    n = width // LANES
    block = lax.slice_in_dim(x, start, start + n * height, axis=0).reshape(n, height, LANES)
    return block.transpose(1, 0, 2).reshape(height, width).astype(F32)


def unpack(x):
    mlp, out, qkv = 2 * FF // LANES * D, D // LANES * D, 3 * D // LANES * D
    up = FF // LANES * D
    at_five = mlp + out
    at_six = at_five + qkv
    at_seven = at_six + mlp
    at_small = at_seven + qkv + out
    up_grad = jnp.stack([untile(x, at_six, D, FF), untile(x, 0, D, FF)])
    down_grad = jnp.stack([untile(x, at_six + up, FF, D), untile(x, up, FF, D)])
    out_grad = jnp.stack([untile(x, at_seven + qkv, D, D), untile(x, mlp, D, D)])
    qkv_grad = jnp.stack([untile(x, at_seven, D, 3 * D), untile(x, at_five, D, 3 * D)])
    small = x[at_small : at_small + 216].reshape(72, D).astype(F32)
    four, five, six, seven = small[:8], small[8:16], small[16:40], small[40:72]
    conv_grad = jnp.stack([seven[18:28], seven[8:18], six[8:18]])
    gain_grad = jnp.stack([seven[1], six[5], five[3], four[5]])
    shift_grad = jnp.stack([seven[4], six[6], five[4], four[6]])
    bias_grad = jnp.stack([seven[0], seven[2], seven[3], five[0], five[1], five[2], four[7]])
    up_bias_grad = jnp.stack([six[:4].reshape(FF), four[:4].reshape(FF)])
    down_bias_grad = jnp.stack([six[4], four[4]])
    return (conv_grad, gain_grad, shift_grad, qkv_grad, bias_grad, out_grad, up_grad, up_bias_grad, down_grad, down_bias_grad)


def solution(mesh):
    split = P("batch", "win", None, None)
    in_specs = (split, P("batch", "win", None), split) + (P(),) * 10
    out_specs = (split, split) + (P(),) * 10
    return jax.shard_map(shards, mesh=mesh, in_specs=in_specs, out_specs=out_specs, check_vma=False)
```

```python
import functools

import jax
import jax.numpy as jnp
import numpy as np
from jax import lax
from jax.experimental import pallas as pl
from jax.experimental.pallas import tpu as pltpu
from jax.sharding import PartitionSpec as P

D = 384
HEADS = 12
HD = 32
FF = 1536
WIN = 7
COLS = 28
WIDE = 32
SLOT = 64
GROUPS = 3
LANES = 128
SIDE = 28
CHUNK = 256
EPS = 1e-05
SCALE = HD ** (-0.5)
F32 = jnp.float32
BF16 = jnp.bfloat16

STRIP = WIN * WIDE
WROWS = 4 * SLOT


def constants():
    perm = np.zeros((WROWS, STRIP), np.float32)
    for window in range(4):
        for r in range(WIN):
            for c in range(WIN):
                perm[window * SLOT + r * WIN + c, r * WIDE + window * WIN + c] = 1.0
    heads_window = np.zeros((4 * SLOT, LANES), np.float32)
    heads_channel = np.zeros((LANES, LANES), np.float32)
    for head in range(4):
        heads_window[head * SLOT : (head + 1) * SLOT, head * HD : (head + 1) * HD] = 1.0
        heads_channel[head * HD : (head + 1) * HD, head * HD : (head + 1) * HD] = 1.0
    return (
        jnp.asarray(perm, BF16),
        jnp.asarray(perm.T, BF16),
        jnp.asarray(heads_window, BF16),
        jnp.asarray(heads_channel, BF16),
    )


def dot(left, right):
    return jnp.dot(left, right, preferred_element_type=F32)


def dot_nt(left, right):
    return lax.dot_general(left, right, (((1,), (1,)), ((), ())), preferred_element_type=F32)


def dot_tn(left, right):
    return lax.dot_general(left, right, (((0,), (0,)), ((), ())), preferred_element_type=F32)


def normalized(z):
    center = z - jnp.sum(z, axis=-1, keepdims=True) * (1.0 / D)
    spread = jnp.sum(center * center, axis=-1, keepdims=True) * (1.0 / D)
    scale = lax.rsqrt(spread + EPS)
    return center * scale, scale


def normalized_back(grad, z, gain):
    xhat, scale = normalized(z)
    scaled = grad * gain
    mean_one = jnp.sum(scaled, axis=-1, keepdims=True) * (1.0 / D)
    mean_two = jnp.sum(scaled * xhat, axis=-1, keepdims=True) * (1.0 / D)
    return (scaled - mean_one - xhat * mean_two) * scale, grad * xhat


TAIL = 0.39 * 0.5**0.5
ERFC = tuple(
    0.5 * c
    for c in (
        0.2353252479818039,
        0.091388231495776,
        0.6495598567387839,
        -0.6354008448449706,
        0.886664715384384,
        -0.2275372084398586,
    )
)


def gelu_pair(x):
    bell = jnp.exp(x * x * -0.5)
    t = 1.0 / (1.0 + TAIL * jnp.abs(x))
    poly = ERFC[5] * t + ERFC[4]
    for c in (ERFC[3], ERFC[2], ERFC[1], ERFC[0]):
        poly = poly * t + c
    tail = poly * t * bell
    below = jnp.where(x >= 0, 1.0 - tail, tail)
    return x * below, below + x * bell * ((2.0 * np.pi) ** -0.5)


def column_mask(rows):
    return lax.broadcasted_iota(jnp.int32, (rows, 1), 0) % WIDE < COLS


def folded(block):
    return jnp.sum(block.reshape(block.shape[0] // 8, 8, block.shape[1]), axis=0)


def conv_row(ext, row, kernel):
    above, here, below = ext[row], ext[row + 1], ext[row + 2]
    left = kernel[0] * above + kernel[3] * here + kernel[6] * below
    center = kernel[1] * above + (1.0 + kernel[4]) * here + kernel[7] * below + kernel[9]
    right = kernel[2] * above + kernel[5] * here + kernel[8] * below
    return center + pltpu.roll(left, 1, 0) + pltpu.roll(right, WIDE - 1, 0)


def conv_row_back(ext, row, kernel):
    above, here, below = ext[row], ext[row + 1], ext[row + 2]
    left = kernel[0] * below + kernel[3] * here + kernel[6] * above
    center = kernel[1] * below + (1.0 + kernel[4]) * here + kernel[7] * above
    right = kernel[2] * below + kernel[5] * here + kernel[8] * above
    return center + pltpu.roll(left, WIDE - 1, 0) + pltpu.roll(right, 1, 0)


def tap_sums(z, ext, row, taps_ref):
    shifted = (pltpu.roll(z, 1, 0), z, pltpu.roll(z, WIDE - 1, 0))
    for a in range(3):
        grad = ext[row + 2 - a]
        for b in range(3):
            taps_ref[3 * a + b] += folded(shifted[b] * grad)
    taps_ref[9] += folded(ext[row + 1])


def taps(ref, layer):
    return [ref[layer, j : j + 1, :] for j in range(10)]


def put_halo(ext, side, halo, rows):
    ext[0] = jnp.where(side == 1, halo, 0.0)
    ext[rows + 1] = jnp.where(side == 0, halo, 0.0)


def put_border(border_ref, side, first, last):
    border_ref[0] = jnp.where(side == 0, last, first).astype(BF16)


def first_step():
    return pl.program_id(0) == 0


def last_step():
    return pl.program_id(0) == pl.num_programs(0) - 1


def clear(*refs):
    @pl.when(first_step())
    def _():
        for ref in refs:
            ref[...] = jnp.zeros_like(ref)


def column_sum(block):
    return jnp.sum(block.astype(F32), axis=0, keepdims=True)


def pack_tiles(pack, core, start, value):
    rows, half = value.shape[0], pack.shape[1]
    for j in range(value.shape[1] // LANES):
        tile = value[:, j * LANES : (j + 1) * LANES].astype(BF16)
        low, high = start + j * rows, start + (j + 1) * rows
        for h in range(2):
            a, b = max(low, h * half), min(high, (h + 1) * half)
            if a < b:
                pack[core ^ h, a - h * half : b - h * half, :] = tile[a - low : b - low]


def hand_out(pack, keep_ref, send_ref, sems):
    copies = [pltpu.make_async_copy(pack.at[slot], ref, sems.at[slot]) for slot, ref in enumerate((keep_ref, send_ref))]
    for copy in copies:
        copy.start()
    for copy in copies:
        copy.wait()


def window_scores(q, k, heads, group):
    lanes = slice(group * LANES, (group + 1) * LANES)
    spread_q = jnp.concatenate([q[:, lanes]] * 4, axis=0) * heads
    return dot_nt(k[:, lanes], spread_q), spread_q


def own_heads(pair):
    first = lax.broadcasted_iota(jnp.int32, (HD, LANES), 1) < SLOT
    blocks = []
    for head in range(4):
        rows, lanes = slice(head * HD, (head + 1) * HD), slice(head // 2 * LANES, (head // 2 + 1) * LANES)
        one, two = (block[rows, lanes] for block in pair)
        if head % 2:
            one = pltpu.roll(one, SLOT, 1)
        else:
            two = pltpu.roll(two, SLOT, 1)
        blocks.append(jnp.where(first, one, two))
    return jnp.concatenate(blocks, axis=0)


def over_keys(left, right, odd):
    empty = jnp.zeros_like(right)
    return dot(left, jnp.concatenate([empty, right] if odd else [right, empty], axis=0))


def stage_one(side_ref, img_ref, halo_ref, conv_ref, gain_ref, shift_ref, qkv_w, bias_ref, out_w, perm_ref, back_ref, heads_ref,
              pos_ref, nw_ref, qkv_ref, kt_ref, att_ref, mix_ref, res_ref, border_ref, ext, nrm, vt, kv_t, bias_t):
    rows = img_ref.shape[1]
    side = side_ref[0]

    @pl.when(first_step())
    def _():
        kv_t[...] = qkv_w[0, :, D:].T
        bias_t[...] = jnp.broadcast_to(bias_ref[1:2, :], (LANES, D)).T

    load_image(img_ref, halo_ref, side, ext)
    kernel = taps(conv_ref, 0)
    gain, shift = gain_ref[0:1, :], shift_ref[0:1, :]

    @pl.loop(0, rows, unroll=ROW_UNROLL)
    def _(r):
        z = conv_row(ext, r, kernel)
        pos_ref[0, r] = z
        xhat, _ = normalized(z)
        nrm[pl.ds(pl.multiple_of(r * WIDE, WIDE), WIDE), :] = (xhat * gain + shift).astype(BF16)

    heads = heads_ref[...]
    real = lax.broadcasted_iota(jnp.int32, (16, 1), 0) < WIN * WIN - 48
    mask = column_mask(STRIP)

    @pl.loop(0, rows // WIN)
    def _(s):
        image_rows = pl.ds(pl.multiple_of(s * STRIP, STRIP), STRIP)
        window_rows = pl.ds(pl.multiple_of(s * WROWS, WROWS), WROWS)
        nw = dot(perm_ref[...], nrm[image_rows, :]).astype(BF16)
        nw_ref[0, window_rows, :] = nw
        for part in range(3):
            cols = slice(part * D, (part + 1) * D)
            value = dot(nw, qkv_w[0, :, cols])
            if part != 1:
                value = value + bias_ref[part // 2 : part // 2 + 1, :]
            qkv_ref[0, window_rows, cols] = value.astype(BF16)
        kt_ref[0, s] = dot_nt(kv_t[:D, :], nw).astype(BF16)
        vt[...] = (dot_nt(kv_t[D:, :], nw) + bias_t[:, :1]).astype(BF16)
        for pair in range(2):
            columns = slice(pair * LANES, (pair + 1) * LANES)
            for group in range(GROUPS):
                lanes = slice(group * LANES, (group + 1) * LANES)
                mixed = []
                for odd in range(2):
                    slot = pl.ds(pl.multiple_of(s * WROWS + (2 * pair + odd) * SLOT, SLOT), SLOT)
                    q, k = qkv_ref[0, slot, :D], qkv_ref[0, slot, D : 2 * D]
                    scores, _ = window_scores(q, k, heads, group)
                    scores = jnp.concatenate([scores[:48], jnp.where(real, scores[48:], -1e30)], axis=0)
                    raised = jnp.exp((scores - jnp.max(scores, axis=0, keepdims=True)) * SCALE)
                    attend = raised * (1.0 / jnp.sum(raised, axis=0, keepdims=True))
                    att_ref[0, slot, group * WROWS : (group + 1) * WROWS] = attend
                    mixed.append(over_keys(vt[lanes, columns], attend.astype(BF16), odd))
                mix_ref[0, s, lanes, columns] = own_heads(mixed).astype(BF16)
        mixed = dot_nt(back_ref[...], mix_ref[0, s]).astype(BF16)
        attn = (dot(mixed, out_w[0]) + bias_ref[2:3, :]).reshape(WIN, WIDE, D)
        strip = pl.ds(s * WIN, WIN)
        value = (pos_ref[0, strip] + attn).reshape(STRIP, D)
        res_ref[0, strip] = jnp.where(mask, value, 0.0).reshape(WIN, WIDE, D)

    put_border(border_ref, side, res_ref[0, 0], res_ref[0, rows - 1])


def load_image(img_ref, halo_ref, side, ext):
    rows = img_ref.shape[1]
    ext[...] = jnp.zeros_like(ext)

    @pl.loop(0, rows, unroll=ROW_UNROLL)
    def _(r):
        ext[r + 1, :COLS, :] = img_ref[0, r].astype(F32)

    halo = halo_ref[0].astype(F32)
    ext[0, :COLS, :] = jnp.where(side == 1, halo, 0.0)
    ext[rows + 1, :COLS, :] = jnp.where(side == 0, halo, 0.0)


def load_rows(x_ref, halo_ref, side, ext):
    rows = x_ref.shape[1]

    @pl.loop(0, rows, unroll=ROW_UNROLL)
    def _(r):
        ext[r + 1] = x_ref[0, r]

    put_halo(ext, side, halo_ref[0].astype(F32), rows)


def stage_two(side_ref, x_ref, halo_ref, conv_ref, gain_ref, shift_ref, up_w, upb_ref, down_w, downb_ref,
              pos_ref, nrm_ref, hid_ref, der_ref, res_ref, border_ref, ext):
    rows = x_ref.shape[1]
    side = side_ref[0]
    load_rows(x_ref, halo_ref, side, ext)
    kernel = taps(conv_ref, 1)
    gain, shift = gain_ref[1:2, :], shift_ref[1:2, :]

    @pl.loop(0, rows, unroll=ROW_UNROLL)
    def _(r):
        z = conv_row(ext, r, kernel)
        pos_ref[0, r] = z
        xhat, _ = normalized(z)
        nrm_ref[0, pl.ds(pl.multiple_of(r * WIDE, WIDE), WIDE), :] = (xhat * gain + shift).astype(BF16)

    mask = column_mask(rows * WIDE)

    @pl.loop(0, 1)
    def _(s):
        part = slice(0, rows * WIDE)
        nrm = nrm_ref[0, part, :]
        for c in range(FF // CHUNK):
            cols = slice(c * CHUNK, (c + 1) * CHUNK)
            hidden, slope = gelu_pair(dot(nrm, up_w[0, :, cols]) + upb_ref[0:1, cols])
            hid_ref[0, part, cols] = hidden.astype(BF16)
            der_ref[0, part, cols] = slope.astype(BF16)
        out = (dot(hid_ref[0, part, :], down_w[0]) + downb_ref[0:1, :]).reshape(rows, WIDE, D)
        strip = slice(0, rows)
        value = (pos_ref[0, strip] + out).reshape(rows * WIDE, D)
        res_ref[0, strip] = jnp.where(mask, value, 0.0).reshape(rows, WIDE, D)

    put_border(border_ref, side, res_ref[0, 0], res_ref[0, rows - 1])


def gram_fold(left, right, heads_f):
    full = dot_tn(left, right) * heads_f
    return full[:HD] + full[HD : 2 * HD] + full[2 * HD : 3 * HD] + full[3 * HD :]


def stage_three(side_ref, x_ref, halo_ref, conv_ref, gain_ref, shift_ref, qkv_w, bias_ref, valid_ref, heads_ref,
                pos_ref, nrm_ref, qkv_ref, gram_ref, ext):
    rows = x_ref.shape[1]
    load_rows(x_ref, halo_ref, side_ref[0], ext)
    kernel = taps(conv_ref, 2)
    gain, shift = gain_ref[2:3, :], shift_ref[2:3, :]

    @pl.loop(0, rows, unroll=ROW_UNROLL)
    def _(r):
        z = conv_row(ext, r, kernel)
        pos_ref[0, r] = z
        xhat, _ = normalized(z)
        nrm_ref[0, pl.ds(pl.multiple_of(r * WIDE, WIDE), WIDE), :] = (xhat * gain + shift).astype(BF16)

    @pl.loop(0, rows // WIN)
    def _(s):
        part = pl.ds(pl.multiple_of(s * STRIP, STRIP), STRIP)
        nrm = nrm_ref[0, part, :]
        valid = valid_ref[0, part, :]
        for third in range(3):
            cols = slice(third * D, (third + 1) * D)
            value = (dot(nrm, qkv_w[0, :, cols]) + bias_ref[3 + third : 4 + third, :]).astype(BF16)
            if third == 0:
                value = (value.astype(F32) * valid).astype(BF16)
            qkv_ref[0, part, cols] = value

    heads_f = heads_ref[...].astype(F32)
    for group in range(GROUPS):
        low = group * LANES
        gram_ref[0, group * HD : (group + 1) * HD, :] = gram_fold(
            qkv_ref[0, :, D + low : D + low + LANES], qkv_ref[0, :, low : low + LANES], heads_f
        )


def channel_weights(gram):
    gram = gram * (1.0 / SIDE)
    raised = jnp.exp(gram - jnp.max(gram, axis=0, keepdims=True))
    return raised / jnp.sum(raised, axis=0, keepdims=True)


def block_diagonal(block, heads):
    return jnp.concatenate([block.astype(BF16)] * 4, axis=0) * heads


def stage_four(core_ref, pos_ref, qkv_ref, gram_a, gram_b, cot_ref, out_w, bias_ref, gain_ref, shift_ref, up_w, upb_ref, down_w, downb_ref,
               heads_ref,
               out_ref, gres_ref, gm_ref, gchan_ref, keep_ref, send_ref, small_ref,
               pack, sems, mix, cotf, cotb, res, nrm, hid, gpre, gn, gb, up_acc, down_acc, out_acc, sums):
    rows = pos_ref.shape[1]
    clear(up_acc, down_acc, out_acc, sums)
    heads = heads_ref[...]
    for group in range(GROUPS):
        low = group * LANES
        gram_rows = slice(group * HD, (group + 1) * HD)
        chan = block_diagonal(channel_weights(gram_a[0, gram_rows] + gram_b[0, gram_rows]), heads)
        mix[:, low : low + LANES] = dot(qkv_ref[0, :, 2 * D + low : 2 * D + low + LANES], chan).astype(BF16)

    cotf[...] = jnp.zeros_like(cotf)

    @pl.loop(0, rows, unroll=ROW_UNROLL)
    def _(r):
        cotf[r, :COLS, :] = cot_ref[0, r].astype(F32)
        cotb[pl.ds(pl.multiple_of(r * WIDE, WIDE), WIDE), :] = cotf[r].astype(BF16)

    gain, shift = gain_ref[3:4, :], shift_ref[3:4, :]

    @pl.loop(0, 1)
    def _(s):
        part = slice(0, rows * WIDE)
        strip = slice(0, rows)
        attn = (dot(mix[part, :], out_w[0]) + bias_ref[6:7, :]).reshape(rows, WIDE, D)
        res[strip] = pos_ref[0, strip] + attn

    @pl.loop(0, rows, unroll=ROW_UNROLL)
    def _(r):
        xhat, _ = normalized(res[r])
        nrm[pl.ds(pl.multiple_of(r * WIDE, WIDE), WIDE), :] = (xhat * gain + shift).astype(BF16)

    @pl.loop(0, 1)
    def _(s):
        part = slice(0, rows * WIDE)
        strip = slice(0, rows)
        normed, cot = nrm[part, :], cotb[part, :]
        for c in range(FF // CHUNK):
            cols = slice(c * CHUNK, (c + 1) * CHUNK)
            hidden, slope = gelu_pair(dot(normed, up_w[0, :, cols]) + upb_ref[1:2, cols])
            hid[part, cols] = hidden.astype(BF16)
            grad = (slope * dot_nt(cot, down_w[0, cols, :])).astype(BF16)
            gpre[part, cols] = grad
            sums[:, cols] += folded(grad.astype(F32))
        value = (dot(hid[part, :], down_w[0]) + downb_ref[1:2, :]).reshape(rows, WIDE, D) + res[strip]
        for r in range(rows):
            out_ref[r, :, pl.ds(pl.program_id(0), 1), :] = value[r, :COLS, :].reshape(COLS, 1, D)
        gn[strip] = dot_nt(gpre[part, :], up_w[0]).reshape(rows, WIDE, D)

    @pl.loop(0, rows, unroll=ROW_UNROLL)
    def _(r):
        grad = gn[r]
        back, gain_term = normalized_back(grad, res[r], gain)
        cot = cotf[r]
        total = cot + back
        gres_ref[0, r] = total
        low = total.astype(BF16)
        gb[pl.ds(pl.multiple_of(r * WIDE, WIDE), WIDE), :] = low
        sums[:, FF : FF + D] += folded(cot)
        sums[:, FF + D : FF + 2 * D] += folded(gain_term)
        sums[:, FF + 2 * D : FF + 3 * D] += folded(grad)
        sums[:, FF + 3 * D : FF + 4 * D] += folded(low.astype(F32))

    up_acc[...] += dot_tn(nrm[...], gpre[...])
    down_acc[...] += dot_tn(cotb[...], hid[...])
    out_acc[...] += dot_tn(mix[...], gb[...])
    gm = dot_nt(gb[...], out_w[0]).astype(BF16)
    gm_ref[0] = gm
    heads_f = heads.astype(F32)
    for group in range(GROUPS):
        low = group * LANES
        gchan_ref[0, group * HD : (group + 1) * HD, :] = gram_fold(
            qkv_ref[0, :, 2 * D + low : 2 * D + low + LANES], gm[:, low : low + LANES], heads_f
        )

    @pl.when(last_step())
    def _():
        core = core_ref[0]
        pack_tiles(pack, core, 0, up_acc[...])
        pack_tiles(pack, core, MATRIX["up"], down_acc[...].T)
        pack_tiles(pack, core, 2 * MATRIX["up"], out_acc[...])
        hand_out(pack, keep_ref, send_ref, sems)
        for j in range(FF // D + 4):
            small_ref[j : j + 1, :] = jnp.sum(sums[:, j * D : (j + 1) * D], axis=0, keepdims=True)


def stage_five(side_ref, core_ref, gres_ref, pos_ref, nrm_ref, qkv_ref, gm_ref, gram_a, gram_b, gchan_a, gchan_b, valid_ref, qkv_w, gain_ref,
               heads_ref,
               gpos_ref, border_ref, keep_ref, send_ref, small_ref,
               pack, sems, joined, gn, qkv_acc, sums):
    rows = pos_ref.shape[1]
    clear(qkv_acc, sums)
    heads = heads_ref[...]
    valid = valid_ref[0]
    for group in range(GROUPS):
        low = group * LANES
        gram_rows = slice(group * HD, (group + 1) * HD)
        chan = channel_weights(gram_a[0, gram_rows] + gram_b[0, gram_rows])
        grad_chan = gchan_a[0, gram_rows] + gchan_b[0, gram_rows]
        grad_gram = chan * (grad_chan - jnp.sum(grad_chan * chan, axis=0, keepdims=True))
        chan, grad_gram = block_diagonal(chan, heads), block_diagonal(grad_gram, heads)
        lanes = slice(low, low + LANES)
        q, k = qkv_ref[0, :, lanes], qkv_ref[0, :, D + low : D + low + LANES]
        joined[:, lanes] = (dot(k, grad_gram) * (1.0 / SIDE) * valid).astype(BF16)
        joined[:, D + low : D + low + LANES] = (dot_nt(q, grad_gram) * (1.0 / SIDE)).astype(BF16)
        joined[:, 2 * D + low : 2 * D + low + LANES] = dot_nt(gm_ref[0, :, lanes], chan).astype(BF16)
    for third in range(3):
        cols = slice(third * D, (third + 1) * D)
        block = joined[:, cols]
        sums[:, cols] += folded(block.astype(F32))
        qkv_acc[:, cols] += dot_tn(nrm_ref[0], block)
    gn[...] = dot_nt(joined[...], qkv_w[0]).reshape(gn.shape)
    gain = gain_ref[2:3, :]

    @pl.loop(0, rows, unroll=ROW_UNROLL)
    def _(r):
        grad = gn[r]
        back, gain_term = normalized_back(grad, pos_ref[0, r], gain)
        gpos_ref[0, r] = gres_ref[0, r] + back
        sums[:, 3 * D : 4 * D] += folded(gain_term)
        sums[:, 4 * D : 5 * D] += folded(grad)

    put_border(border_ref, side_ref[0], gpos_ref[0, 0], gpos_ref[0, rows - 1])

    @pl.when(last_step())
    def _():
        pack_tiles(pack, core_ref[0], 0, qkv_acc[...])
        hand_out(pack, keep_ref, send_ref, sems)
        for j in range(5):
            small_ref[j : j + 1, :] = jnp.sum(sums[:, j * D : (j + 1) * D], axis=0, keepdims=True)


def stage_six(side_ref, core_ref, g_ref, halo_ref, x_ref, pos_ref, nrm_ref, hid_ref, der_ref, conv_ref, gain_ref, up_w, down_w,
              gpos_ref, border_ref, keep_ref, send_ref, small_ref,
              pack, sems, ext, gres, gb, gpre, gn, up_acc, down_acc, sums, tap_acc):
    rows = pos_ref.shape[1]
    clear(up_acc, down_acc, sums, tap_acc)
    load_rows(g_ref, halo_ref, side_ref[0], ext)
    kernel = taps(conv_ref, 2)
    mask = column_mask(WIDE)

    @pl.loop(0, rows, unroll=ROW_UNROLL)
    def _(r):
        back = jnp.where(mask, conv_row_back(ext, r, kernel), 0.0)
        gres[r] = back
        low = back.astype(BF16)
        gb[pl.ds(pl.multiple_of(r * WIDE, WIDE), WIDE), :] = low
        sums[:, FF : FF + D] += folded(low.astype(F32))
        tap_sums(x_ref[0, r], ext, r, tap_acc)

    @pl.loop(0, 1)
    def _(s):
        part = slice(0, rows * WIDE)
        grad = gb[part, :]
        for c in range(FF // CHUNK):
            cols = slice(c * CHUNK, (c + 1) * CHUNK)
            block = (der_ref[0, part, cols].astype(F32) * dot_nt(grad, down_w[0, cols, :])).astype(BF16)
            gpre[part, cols] = block
            sums[:, cols] += folded(block.astype(F32))
        gn[slice(0, rows)] = dot_nt(gpre[part, :], up_w[0]).reshape(rows, WIDE, D)

    gain = gain_ref[1:2, :]

    @pl.loop(0, rows, unroll=ROW_UNROLL)
    def _(r):
        grad = gn[r]
        back, gain_term = normalized_back(grad, pos_ref[0, r], gain)
        gpos_ref[0, r] = gres[r] + back
        sums[:, FF + D : FF + 2 * D] += folded(gain_term)
        sums[:, FF + 2 * D : FF + 3 * D] += folded(grad)

    put_border(border_ref, side_ref[0], gpos_ref[0, 0], gpos_ref[0, rows - 1])
    up_acc[...] += dot_tn(nrm_ref[0], gpre[...])
    down_acc[...] += dot_tn(gb[...], hid_ref[0])

    @pl.when(last_step())
    def _():
        pack_tiles(pack, core_ref[0], 0, up_acc[...])
        pack_tiles(pack, core_ref[0], FF // LANES * D, down_acc[...].T)
        hand_out(pack, keep_ref, send_ref, sems)
        for j in range(FF // D + 3):
            small_ref[j : j + 1, :] = jnp.sum(sums[:, j * D : (j + 1) * D], axis=0, keepdims=True)
        for j in range(10):
            small_ref[8 + j : 9 + j, :] = jnp.sum(tap_acc[j], axis=0, keepdims=True)


def stage_seven(side_ref, core_ref, small_four, small_five, small_six, g_ref, halo_ref, x_ref, pos_ref, img_ref, imghalo_ref, nw_ref, qkv_ref, kt_ref, att_ref, mix_ref, conv_ref,
                gain_ref, qkv_w, out_w, perm_ref, back_ref, heads_ref,
                gpos_ref, border_ref, keep_ref, send_ref,
                pack, sems, ext, gres, gb, joined, gqt, gn, q_acc, kv_acc, out_acc, sums, tap_acc, tap_one, small):
    rows = pos_ref.shape[1]
    side = side_ref[0]
    clear(q_acc, kv_acc, out_acc, sums, tap_acc, tap_one)
    load_rows(g_ref, halo_ref, side, ext)
    kernel = taps(conv_ref, 1)
    mask = column_mask(WIDE)

    @pl.loop(0, rows, unroll=ROW_UNROLL)
    def _(r):
        back = jnp.where(mask, conv_row_back(ext, r, kernel), 0.0)
        gres[r] = back
        low = back.astype(BF16)
        gb[pl.ds(pl.multiple_of(r * WIDE, WIDE), WIDE), :] = low
        sums[:, 3 * D : 4 * D] += folded(low.astype(F32))
        tap_sums(x_ref[0, r], ext, r, tap_acc)

    heads = heads_ref[...]

    @pl.loop(0, rows // WIN)
    def _(s):
        image_rows = pl.ds(pl.multiple_of(s * STRIP, STRIP), STRIP)
        window_rows = pl.ds(pl.multiple_of(s * WROWS, WROWS), WROWS)
        gbw = dot(perm_ref[...], gb[image_rows, :]).astype(BF16)
        out_acc[...] += dot(mix_ref[0, s], gbw)
        gm_all = dot_nt(gbw, out_w[0]).astype(BF16)
        for pair in range(2):
            columns = slice(pair * LANES, (pair + 1) * LANES)
            for group in range(GROUPS):
                low = group * LANES
                lanes = slice(low, low + LANES)
                queries = []
                for odd in range(2):
                    window = 2 * pair + odd
                    slot = pl.ds(pl.multiple_of(s * WROWS + window * SLOT, SLOT), SLOT)
                    out_rows = slice(window * SLOT, (window + 1) * SLOT)
                    q, v = qkv_ref[0, slot, :D], qkv_ref[0, slot, 2 * D :]
                    attend = att_ref[0, slot, group * WROWS : (group + 1) * WROWS]
                    grad_att, spread_gm = window_scores(gm_all[out_rows], v, heads, group)
                    spread_q = jnp.concatenate([q[:, lanes]] * 4, axis=0) * heads
                    weighted = grad_att * attend
                    grad_s = (weighted - attend * jnp.sum(weighted, axis=0, keepdims=True)).astype(BF16)
                    joined[out_rows, lanes] = (dot(grad_s, spread_q) * SCALE).astype(BF16)
                    joined[out_rows, D + low : D + low + LANES] = dot(attend.astype(BF16), spread_gm).astype(BF16)
                    queries.append(over_keys(kt_ref[0, s, lanes, columns], grad_s, odd))
                gqt[lanes, columns] = (own_heads(queries) * SCALE).astype(BF16)
        nw = nw_ref[0, window_rows, :]
        q_acc[...] += dot(gqt[...], nw)
        kv_acc[...] += dot_tn(nw, joined[...])
        unwound = dot_nt(back_ref[...], gqt[...]).astype(BF16)
        sums[:, :D] += folded(unwound.astype(F32))
        total = dot_nt(unwound, qkv_w[0, :, :D])
        unwound = dot(back_ref[...], joined[...]).astype(BF16)
        sums[:, 2 * D : 3 * D] += folded(unwound[:, D:].astype(F32))
        gn[pl.ds(s * WIN, WIN)] = (total + dot_nt(unwound, qkv_w[0, :, D:])).reshape(WIN, WIDE, D)

    gain = gain_ref[0:1, :]

    @pl.loop(0, rows, unroll=ROW_UNROLL)
    def _(r):
        grad = gn[r]
        back, gain_term = normalized_back(grad, pos_ref[0, r], gain)
        gpos_ref[0, r] = gres[r] + back
        sums[:, D : 2 * D] += folded(gain_term)
        sums[:, 4 * D : 5 * D] += folded(grad)

    put_border(border_ref, side, gpos_ref[0, 0], gpos_ref[0, rows - 1])
    load_image(img_ref, imghalo_ref, side, ext)

    @pl.loop(0, rows, unroll=ROW_UNROLL)
    def _(r):
        grad = gpos_ref[0, r]
        shifted = (pltpu.roll(grad, WIDE - 1, 0), grad, pltpu.roll(grad, 1, 0))
        for a in range(3):
            z = ext[r + a]
            for b in range(3):
                tap_one[3 * a + b] += folded(shifted[b] * z)
        tap_one[9] += folded(grad)

    @pl.when(last_step())
    def _():
        core = core_ref[0]
        pack_tiles(pack, core, 0, q_acc[...].T)
        pack_tiles(pack, core, D // LANES * D, kv_acc[...])
        pack_tiles(pack, core, 3 * D // LANES * D, out_acc[...])
        small[...] = jnp.zeros_like(small)
        small[0:8] = small_four[...]
        small[8:16] = small_five[...]
        small[16:40] = small_six[...]
        for j in range(5):
            small[40 + j : 41 + j, :] = jnp.sum(sums[:, j * D : (j + 1) * D], axis=0, keepdims=True)
        for j in range(10):
            small[48 + j : 49 + j, :] = jnp.sum(tap_acc[j], axis=0, keepdims=True)
            small[58 + j : 59 + j, :] = jnp.sum(tap_one[j], axis=0, keepdims=True)
        pack_tiles(pack, core, 4 * D // LANES * D, small[...])
        hand_out(pack, keep_ref, send_ref, sems)


def stage_eight(side_ref, g_ref, halo_ref, conv_ref, out_ref, ext):
    rows = g_ref.shape[1]
    load_rows(g_ref, halo_ref, side_ref[0], ext)
    kernel = taps(conv_ref, 0)

    @pl.loop(0, rows, unroll=ROW_UNROLL)
    def _(r):
        out_ref[r, :, pl.ds(pl.program_id(0), 1), :] = conv_row_back(ext, r, kernel)[:COLS].reshape(COLS, 1, D)


VMEM_LIMIT = 60 * 1024 * 1024


def per_image(shape):
    return pl.BlockSpec((1,) + tuple(shape[1:]), lambda i: (i,) + (0,) * (len(shape) - 1))


def whole(shape):
    return pl.BlockSpec(tuple(shape), lambda i: (0,) * len(shape))


def layer(array, index):
    shape = array.shape
    return pl.BlockSpec((1,) + tuple(shape[1:]), lambda i: (index,) + (0,) * (len(shape) - 1))


def scalar():
    return pl.BlockSpec(memory_space=pltpu.SMEM)


def call(body, images, in_specs, outs, scratch, microseconds, name):
    return pl.pallas_call(
        body,
        name=name,
        grid=(images,),
        in_specs=in_specs,
        out_specs=[pl.BlockSpec(memory_space=pl.ANY) if own is None else per_image(shape) if own else whole(shape) for shape, _, own in outs],
        out_shape=[jax.ShapeDtypeStruct(shape, dtype) for shape, dtype, _ in outs],
        scratch_shapes=scratch,
        compiler_params=pltpu.CompilerParams(dimension_semantics=("arbitrary",), vmem_limit_bytes=VMEM_LIMIT),
        cost_estimate=pl.CostEstimate(flops=microseconds * 1_150_000_000, bytes_accessed=1_000_000, transcendentals=0),
    )


def exchange(array):
    return lax.ppermute(array, "win", [(0, 1), (1, 0)])


def shards(images, valid_mask, cotangent, conv, gain, shift, qkv_w, bias, out_w, up_w, up_b, down_w, down_b):
    n, rows = images.shape[0], images.shape[1]
    side = lax.axis_index("win")
    side_arr = side.astype(jnp.int32).reshape(1)
    core_arr = (lax.axis_index("batch") % 2).astype(jnp.int32).reshape(1)
    perm, back, heads_w, heads_c = constants()
    wide = (n, rows, WIDE, D)
    inner = (rows, COLS, n, D)
    flat = rows * WIDE
    wflat = rows // WIN * WROWS
    border = (n, WIDE, D)
    valid = jnp.pad(valid_mask.astype(F32), ((0, 0), (0, 0), (0, WIDE - COLS))).reshape(n, flat, 1)
    ext = pltpu.VMEM((rows + 2, WIDE, D), F32)

    def vm(shape, dtype=F32):
        return pltpu.VMEM(shape, dtype)

    edge = jnp.where(side == 0, images[:, rows - 1], images[:, 0])
    img_halo = exchange(edge)
    small_params = [whole(conv.shape), whole(gain.shape)]

    turned = (n, rows // WIN, D, WROWS)
    pos_one, nw, qkv_one, kt, att, mix_one, res_one, edge = call(
        stage_one, n,
        [scalar(), per_image(images.shape), per_image(img_halo.shape), *small_params, whole(shift.shape), layer(qkv_w, 0),
         whole(bias.shape), layer(out_w, 0), whole(perm.shape), whole(back.shape),
         whole(heads_w.shape)],
        [(wide, F32, True), ((n, wflat, D), BF16, True), ((n, wflat, 3 * D), BF16, True), (turned, BF16, True),
         ((n, wflat, GROUPS * WROWS), F32, True), (turned, BF16, True), (wide, F32, True), (border, BF16, True)],
        [ext, vm((flat, D), BF16), vm((D, WROWS), BF16), vm((2 * D, D), BF16), vm((D, LANES))], 23, "window_forward",
    )(side_arr, images, img_halo, conv, gain, shift, qkv_w, bias, out_w, perm, back, heads_w)

    halo = exchange(edge)
    pos_two, nrm_two, hid_one, der_one, res_two, edge = call(
        stage_two, n,
        [scalar(), per_image(wide), per_image(border), *small_params, whole(shift.shape), layer(up_w, 0), whole(up_b.shape),
         layer(down_w, 0), whole(down_b.shape)],
        [(wide, F32, True), ((n, flat, D), BF16, True), ((n, flat, FF), BF16, True), ((n, flat, FF), BF16, True), (wide, F32, True),
         (border, BF16, True)],
        [ext], 20, "mlp_one_forward",
    )(side_arr, res_one, halo, conv, gain, shift, up_w, up_b, down_w, down_b)

    halo = exchange(edge)
    gram_shape = (n, GROUPS * HD, LANES)
    pos_three, nrm_three, qkv_two, gram = call(
        stage_three, n,
        [scalar(), per_image(wide), per_image(border), *small_params, whole(shift.shape), layer(qkv_w, 1), whole(bias.shape),
         per_image(valid.shape), whole(heads_c.shape)],
        [(wide, F32, True), ((n, flat, D), BF16, True), ((n, flat, 3 * D), BF16, True), (gram_shape, F32, True)],
        [ext], 11, "channel_gram",
    )(side_arr, res_two, halo, conv, gain, shift, qkv_w, bias, valid, heads_c)

    gram_other = exchange(gram)

    devices = 2 * lax.axis_size("batch")
    four_rows = -(-MLP_PACK // devices) * devices

    def pack_outs(rows_in_pack):
        return [((rows_in_pack // 2, LANES), BF16, None)] * 2

    def pack_scratch(rows_in_pack):
        return [vm((2, rows_in_pack // 2, LANES), BF16), pltpu.SemaphoreType.DMA((2,))]

    output, gres_three, gm_two, gchan, *four, small_four = call(
        stage_four, n,
        [scalar(), per_image(wide), per_image(qkv_two.shape), per_image(gram_shape), per_image(gram_shape),
         per_image(cotangent.shape), layer(out_w, 1), whole(bias.shape), whole(gain.shape), whole(shift.shape), layer(up_w, 1),
         whole(up_b.shape), layer(down_w, 1), whole(down_b.shape), whole(heads_c.shape)],
        [(inner, F32, False), (wide, F32, True), ((n, flat, D), BF16, True), (gram_shape, F32, True),
         *pack_outs(four_rows), ((8, D), F32, False)],
        [*pack_scratch(four_rows), vm((flat, D), BF16), vm((rows, WIDE, D)), vm((flat, D), BF16), vm((rows, WIDE, D)),
         vm((flat, D), BF16), vm((flat, FF), BF16), vm((flat, FF), BF16), vm((rows, WIDE, D)), vm((flat, D), BF16),
         vm((D, FF)), vm((D, FF)), vm((D, D)), vm((8, FF + 4 * D))],
        36, "mlp_two",
    )(core_arr, pos_three, qkv_two, gram, gram_other, cotangent, out_w, bias, gain, shift, up_w, up_b, down_w, down_b,
      heads_c)

    trade = Trade()
    gchan_other = exchange(gchan)
    four = start_sum(trade, four)
    far = range(2, len(trade.order))
    gpos_three, edge, *five, small_five = call(
        stage_five, n,
        [scalar(), scalar(), per_image(wide), per_image(wide), per_image(nrm_three.shape), per_image(qkv_two.shape),
         per_image(gm_two.shape), per_image(gram_shape), per_image(gram_shape), per_image(gram_shape), per_image(gram_shape),
         per_image(valid.shape), layer(qkv_w, 1), whole(gain.shape), whole(heads_c.shape)],
        [(wide, F32, True), (border, BF16, True), *pack_outs(PIECES[0]), ((8, D), F32, False)],
        [*pack_scratch(PIECES[0]), vm((flat, 3 * D), BF16), vm((rows, WIDE, D)), vm((D, 3 * D)), vm((8, 5 * D))],
        13, "channel_backward",
    )(side_arr, core_arr, gres_three, pos_three, nrm_three, qkv_two, gm_two, gram, gram_other, gchan, gchan_other, valid, qkv_w,
      gain, heads_c)

    halo, four = lax.optimization_barrier((exchange(edge), four))
    four = trade.halve(four, far[0])
    five = start_sum(trade, five)
    gpos_two, edge, *six, small_six = call(
        stage_six, n,
        [scalar(), scalar(), per_image(wide), per_image(border), per_image(wide), per_image(wide), per_image(nrm_two.shape),
         per_image(hid_one.shape), per_image(der_one.shape), *small_params, layer(up_w, 0), layer(down_w, 0)],
        [(wide, F32, True), (border, BF16, True), *pack_outs(PIECES[1]), ((24, D), F32, False)],
        [*pack_scratch(PIECES[1]), ext, vm((rows, WIDE, D)), vm((flat, D), BF16), vm((flat, FF), BF16), vm((rows, WIDE, D)),
         vm((D, FF)), vm((D, FF)), vm((8, FF + 3 * D)), vm((10, 8, D))], 23, "mlp_one_backward",
    )(side_arr, core_arr, gpos_three, halo, res_two, pos_two, nrm_two, hid_one, der_one, conv, gain, up_w, down_w)

    halo, four, five = lax.optimization_barrier((exchange(edge), four, five))
    for step in far[1:]:
        four = trade.halve(four, step)
    five = trade.halve(five, 0)
    six = start_sum(trade, six)
    gpos_one, edge, *seven = call(
        stage_seven, n,
        [scalar(), scalar(), whole((8, D)), whole((8, D)), whole((24, D)), per_image(wide), per_image(border), per_image(wide),
         per_image(wide), per_image(images.shape), per_image(img_halo.shape), per_image(nw.shape), per_image(qkv_one.shape),
         per_image(turned), per_image(att.shape), per_image(mix_one.shape), *small_params, layer(qkv_w, 0), layer(out_w, 0), whole(perm.shape),
         whole(back.shape), whole(heads_w.shape)],
        [(wide, F32, True), (border, BF16, True), *pack_outs(PIECES[2])],
        [*pack_scratch(PIECES[2]), ext, vm((rows, WIDE, D)), vm((flat, D), BF16), vm((WROWS, 2 * D), BF16), vm((D, WROWS), BF16),
         vm((rows, WIDE, D)), vm((D, D)), vm((D, 2 * D)), vm((D, D)), vm((8, 5 * D)), vm((10, 8, D)), vm((10, 8, D)), vm((80, D))],
        35, "window_backward",
    )(side_arr, core_arr, small_four, small_five, small_six, gpos_two, halo, res_one, pos_one, images, img_halo, nw, qkv_one, kt, att,
      mix_one, conv, gain, qkv_w, out_w, perm, back, heads_w)

    four, five, six, gpos_one, edge, *seven = lax.optimization_barrier((four, five, six, gpos_one, edge, *seven))
    halo = exchange(edge)
    (images_grad,) = call(
        stage_eight, n, [scalar(), per_image(wide), per_image(border), whole(conv.shape)], [(inner, F32, False)], [ext],
        5, "images_backward",
    )(side_arr, gpos_one, halo, conv)

    seven = start_sum(trade, seven)
    five = trade.halve(five, 1)
    six, seven = (trade.halve(trade.halve(x, 0), 1) for x in (six, seven))
    x, four = lax.optimization_barrier((jnp.concatenate([five, six, seven], axis=0), four))
    x = trade.halve(x, far[0])
    x, images_grad = lax.optimization_barrier((x, images_grad))
    for step in far[1:]:
        x = trade.halve(x, step)
    for step in far[::-1]:
        x = trade.join(x, step)
    for step in (0, 1):
        four = trade.halve(four, step)
    for step in (1, 0):
        four = trade.join(four, step)
    x, four = lax.optimization_barrier((x, four))
    output, images_grad = (jnp.transpose(x, (2, 0, 1, 3)) for x in (output, images_grad))
    return (output, images_grad, *finish_sum(trade, x, four))


MATRIX = {"up": FF // LANES * D, "down": FF // LANES * D, "out": D // LANES * D, "qkv": 3 * D // LANES * D}
PIECES = (
    MATRIX["qkv"],
    MATRIX["up"] + MATRIX["down"],
    MATRIX["qkv"] + MATRIX["out"] + 640,
)
STARTS = tuple(sum(PIECES[:i]) for i in range(len(PIECES)))
TOTAL = sum(PIECES)
MLP_PACK = MATRIX["up"] + MATRIX["down"] + MATRIX["out"]
ROW_UNROLL = 14


class Trade:
    def __init__(self):
        self.batch = lax.axis_size("batch")
        self.place, self.win = lax.axis_index("batch"), lax.axis_index("win")
        self.core = self.place % 2
        bits = list(range((self.batch // 2).bit_length() - 1))
        one, two = ["w", *bits], [*bits[:1], "w", *bits[1:]]
        self.order = list(zip(one, two))
        self.bits = [self.bit(axes, self.core) for axes in self.order]

    def __call__(self, value, axes):
        pairs = []
        for b in range(self.batch):
            for w in range(2):
                axis = axes[b % 2]
                to = (b ^ 1, w) if axis == "c" else (b, 1 - w) if axis == "w" else (b ^ (2 << axis), w)
                pairs.append((2 * b + w, 2 * to[0] + to[1]))
        return lax.ppermute(value, ("batch", "win"), pairs)

    def of(self, axis):
        return self.win if axis == "w" else (self.place // (2 << axis)) % 2

    def bit(self, axes, core):
        return jnp.where(core == 0, self.of(axes[0]), self.of(axes[1]))

    def halve(self, x, step):
        half = x.shape[0] // 2
        sent = lax.dynamic_slice_in_dim(x, (1 - self.bits[step]) * half, half, 0)
        kept = lax.dynamic_slice_in_dim(x, self.bits[step] * half, half, 0)
        return added(kept, self(sent, self.order[step]))

    def join(self, x, step):
        got, lower = self(x, self.order[step]), self.bits[step] == 0
        return jnp.concatenate([jnp.where(lower, x, got), jnp.where(lower, got, x)], axis=0)


def added(left, right):
    return (left.astype(F32) + right.astype(F32)).astype(BF16)


def start_sum(trade, pack):
    keep, send = pack
    return added(keep, trade(send, ("c", "c")))


def finish_sum(trade, x, four):
    far = range(2, len(trade.order))
    one = [x, trade(x, trade.order[1])]
    mine = one + [trade(block, trade.order[0]) for block in one]
    theirs = [trade(block, ("c", "c")) for block in mine]
    where = []
    for core in (trade.core, 1 - trade.core):
        first, second = (trade.bit(trade.order[step], core) for step in range(2))
        for flip_first in range(2):
            for flip_second in range(2):
                where.append(core * 4 + (first ^ flip_first) * 2 + (second ^ flip_second))
    for step in far[:0:-1]:
        four = trade.join(four, step)
    pair = [four, trade(four, trade.order[far[0]])]
    fours = pair + [trade(block, ("c", "c")) for block in pair]
    bit = trade.bits[far[0]]
    where_four = [core * 2 + (bit ^ flip) for core in (trade.core, 1 - trade.core) for flip in range(2)]
    rest = unpack_rest(jnp.stack(where).astype(jnp.int32), mine + theirs)
    return unpack_four(jnp.stack(where_four).astype(jnp.int32), fours, rest)


UP, DOWN, OUT, QKV = (2, D, FF), (2, FF, D), (2, D, D), (2, D, 3 * D)


def unpack_four_kernel(where_ref, *refs):
    blocks, (up_out, down_out, out_out), (buf, sems) = refs[:4], refs[7:10], refs[10:]
    size = blocks[0].shape[0]
    copies = []
    for t, block in enumerate(blocks):
        target = pl.ds(pl.multiple_of(where_ref[t] * size, 16), size)
        copies.append(pltpu.make_async_copy(block, buf.at[target], sems.at[t]))
    for copy in copies:
        copy.start()
    for copy in copies:
        copy.wait()
    start = 0
    for ref in (up_out, down_out, out_out):
        height, width = ref.shape[1:]
        for j in range(width // LANES):
            ref[0, :, j * LANES : (j + 1) * LANES] = buf[start : start + height, :].astype(F32)
            start += height


def unpack_four(where, blocks, rest):
    conv, gain, shift, qkv, bias, out, up, up_bias, down, down_bias = rest
    shapes = (UP, DOWN, OUT)
    hbm = pl.BlockSpec(memory_space=pl.ANY)
    up, down, out = pl.pallas_call(
        unpack_four_kernel,
        name="unpack_four",
        grid=(1,),
        in_specs=[scalar()] + [hbm] * 7,
        out_specs=[pl.BlockSpec((1,) + shape[1:], lambda i: (1, 0, 0)) for shape in shapes],
        out_shape=[jax.ShapeDtypeStruct(shape, F32) for shape in shapes],
        input_output_aliases={5: 0, 6: 1, 7: 2},
        scratch_shapes=[pltpu.VMEM((4 * blocks[0].shape[0], LANES), BF16), pltpu.SemaphoreType.DMA((4,))],
        compiler_params=pltpu.CompilerParams(vmem_limit_bytes=VMEM_LIMIT),
    )(where, *blocks, up, down, out)
    return conv, gain, shift, qkv, bias, out, up, up_bias, down, down_bias


def unpack_rest_kernel(where_ref, *refs):
    blocks, outs, (buf, up_buf, down_buf, out_buf, sems, out_sems) = refs[:8], refs[8:18], refs[18:]
    up_out, down_out, out_out, conv_out, gain_out, shift_out, qkv_out, bias_out, upb_out, downb_out = outs
    copies = []
    for p, piece in enumerate(PIECES):
        size, source = piece // 8, STARTS[p] // 8
        for t, block in enumerate(blocks):
            target = pl.ds(pl.multiple_of(STARTS[p] + where_ref[t] * size, 16), size)
            copies.append(pltpu.make_async_copy(block.at[source : source + size], buf.at[target], sems.at[t, p]))
    order = (1, 2, 0)
    for p in order:
        for copy in copies[8 * p : 8 * p + 8]:
            copy.start()

    def arrived(p):
        for copy in copies[8 * p : 8 * p + 8]:
            copy.wait()

    def matrix(store, height, width, start):
        for j in range(width // LANES):
            low = start + j * height
            store(slice(j * LANES, (j + 1) * LANES), buf[low : low + height, :].astype(F32))

    def into(ref, *index):
        def store(lanes, value):
            ref[(*index, slice(None), lanes)] = value

        return store

    sent = []

    def send(source, target):
        copy = pltpu.make_async_copy(source, target.at[0], out_sems.at[len(sent)])
        copy.start()
        sent.append(copy)

    arrived(1)
    matrix(into(up_buf), D, FF, STARTS[1])
    send(up_buf, up_out)
    matrix(into(down_buf), FF, D, STARTS[1] + MATRIX["up"])
    send(down_buf, down_out)
    arrived(2)
    matrix(into(out_buf), D, D, STARTS[2] + MATRIX["qkv"])
    send(out_buf, out_out)
    matrix(into(qkv_out, 0), D, 3 * D, STARTS[2])
    base = STARTS[2] + MATRIX["qkv"] + MATRIX["out"]
    for j in range(GROUPS):
        lanes = slice(j * LANES, (j + 1) * LANES)
        small = buf[base + j * 80 : base + (j + 1) * 80, :].astype(F32)
        for index, first in enumerate((58, 48, 24)):
            conv_out[index, :, lanes] = small[first : first + 10]
        for ref, rows in ((gain_out, (41, 21, 11, 5)), (shift_out, (44, 22, 12, 6)), (bias_out, (40, 42, 43, 8, 9, 10, 7)),
                          (downb_out, (20, 4))):
            for index, row in enumerate(rows):
                ref[index : index + 1, lanes] = small[row : row + 1]
        for index, first in enumerate((16, 0)):
            for r in range(FF // D):
                low = r * D + j * LANES
                upb_out[index : index + 1, low : low + LANES] = small[first + r : first + r + 1]
    arrived(0)
    matrix(into(qkv_out, 1), D, 3 * D, STARTS[0])
    for copy in sent:
        copy.wait()


def unpack_rest(where, blocks):
    shapes = [UP, DOWN, OUT, (3, 10, D), (4, D), (4, D), QKV, (7, D), (2, FF), (2, D)]
    hbm, vmem = pl.BlockSpec(memory_space=pl.ANY), pl.BlockSpec(memory_space=pltpu.VMEM)
    up, down, out, conv, gain, shift, qkv, bias, up_bias, down_bias = pl.pallas_call(
        unpack_rest_kernel,
        name="unpack_rest",
        in_specs=[pl.BlockSpec(memory_space=pltpu.SMEM)] + [hbm] * 8,
        out_specs=[hbm] * 3 + [vmem] * 7,
        out_shape=[jax.ShapeDtypeStruct(shape, F32) for shape in shapes],
        scratch_shapes=[pltpu.VMEM((TOTAL, LANES), BF16), pltpu.VMEM((D, FF), F32), pltpu.VMEM((FF, D), F32), pltpu.VMEM((D, D), F32),
                        pltpu.SemaphoreType.DMA((8, len(PIECES))), pltpu.SemaphoreType.DMA((3,))],
        compiler_params=pltpu.CompilerParams(vmem_limit_bytes=VMEM_LIMIT),
    )(where, *blocks)
    return conv, gain, shift, qkv, bias, out, up, up_bias, down, down_bias


def solution(mesh):
    split = P("batch", "win", None, None)
    in_specs = (split, P("batch", "win", None), split) + (P(),) * 10
    out_specs = (split, split) + (P(),) * 10
    return jax.shard_map(shards, mesh=mesh, in_specs=in_specs, out_specs=out_specs, check_vma=False)
```

```python
import functools

import jax
import jax.numpy as jnp
import numpy as np
from jax import lax
from jax.experimental import pallas as pl
from jax.experimental.pallas import tpu as pltpu
from jax.sharding import PartitionSpec as P

D = 384
HEADS = 12
HD = 32
FF = 1536
WIN = 7
COLS = 28
WIDE = 32
SLOT = 64
GROUPS = 3
LANES = 128
SIDE = 28
CHUNK = 256
EPS = 1e-05
SCALE = HD ** (-0.5)
F32 = jnp.float32
BF16 = jnp.bfloat16

STRIP = WIN * WIDE
WROWS = 4 * SLOT


def constants():
    perm = np.zeros((WROWS, STRIP), np.float32)
    for window in range(4):
        for r in range(WIN):
            for c in range(WIN):
                perm[window * SLOT + r * WIN + c, r * WIDE + window * WIN + c] = 1.0
    heads_window = np.zeros((4 * SLOT, LANES), np.float32)
    heads_channel = np.zeros((LANES, LANES), np.float32)
    for head in range(4):
        heads_window[head * SLOT : (head + 1) * SLOT, head * HD : (head + 1) * HD] = 1.0
        heads_channel[head * HD : (head + 1) * HD, head * HD : (head + 1) * HD] = 1.0
    return (
        jnp.asarray(perm, BF16),
        jnp.asarray(perm.T, BF16),
        jnp.asarray(heads_window, BF16),
        jnp.asarray(heads_channel, BF16),
    )


def dot(left, right):
    return jnp.dot(left, right, preferred_element_type=F32)


def dot_nt(left, right):
    return lax.dot_general(left, right, (((1,), (1,)), ((), ())), preferred_element_type=F32)


def dot_tn(left, right):
    return lax.dot_general(left, right, (((0,), (0,)), ((), ())), preferred_element_type=F32)


def normalized(z):
    center = z - jnp.sum(z, axis=-1, keepdims=True) * (1.0 / D)
    spread = jnp.sum(center * center, axis=-1, keepdims=True) * (1.0 / D)
    scale = lax.rsqrt(spread + EPS)
    return center * scale, scale


def normalized_back(grad, z, gain):
    xhat, scale = normalized(z)
    scaled = grad * gain
    mean_one = jnp.sum(scaled, axis=-1, keepdims=True) * (1.0 / D)
    mean_two = jnp.sum(scaled * xhat, axis=-1, keepdims=True) * (1.0 / D)
    return (scaled - mean_one - xhat * mean_two) * scale, grad * xhat


TAIL = 0.39 * 0.5**0.5
ERFC = tuple(
    0.5 * c
    for c in (
        0.2353252479818039,
        0.091388231495776,
        0.6495598567387839,
        -0.6354008448449706,
        0.886664715384384,
        -0.2275372084398586,
    )
)


def gelu_pair(x):
    bell = jnp.exp(x * x * -0.5)
    t = 1.0 / (1.0 + TAIL * jnp.abs(x))
    poly = ERFC[5] * t + ERFC[4]
    for c in (ERFC[3], ERFC[2], ERFC[1], ERFC[0]):
        poly = poly * t + c
    tail = poly * t * bell
    below = jnp.where(x >= 0, 1.0 - tail, tail)
    return x * below, below + x * bell * ((2.0 * np.pi) ** -0.5)


def column_mask(rows):
    return lax.broadcasted_iota(jnp.int32, (rows, 1), 0) % WIDE < COLS


def folded(block):
    return jnp.sum(block.reshape(block.shape[0] // 8, 8, block.shape[1]), axis=0)


def conv_row(ext, row, kernel):
    above, here, below = ext[row], ext[row + 1], ext[row + 2]
    left = kernel[0] * above + kernel[3] * here + kernel[6] * below
    center = kernel[1] * above + (1.0 + kernel[4]) * here + kernel[7] * below + kernel[9]
    right = kernel[2] * above + kernel[5] * here + kernel[8] * below
    return center + pltpu.roll(left, 1, 0) + pltpu.roll(right, WIDE - 1, 0)


def conv_row_back(ext, row, kernel):
    above, here, below = ext[row], ext[row + 1], ext[row + 2]
    left = kernel[0] * below + kernel[3] * here + kernel[6] * above
    center = kernel[1] * below + (1.0 + kernel[4]) * here + kernel[7] * above
    right = kernel[2] * below + kernel[5] * here + kernel[8] * above
    return center + pltpu.roll(left, WIDE - 1, 0) + pltpu.roll(right, 1, 0)


def tap_sums(z, ext, row, taps_ref):
    shifted = (pltpu.roll(z, 1, 0), z, pltpu.roll(z, WIDE - 1, 0))
    for a in range(3):
        grad = ext[row + 2 - a]
        for b in range(3):
            taps_ref[3 * a + b] += folded(shifted[b] * grad)
    taps_ref[9] += folded(ext[row + 1])


def taps(ref, layer):
    return [ref[layer, j : j + 1, :] for j in range(10)]


def put_halo(ext, side, halo, rows):
    ext[0] = jnp.where(side == 1, halo, 0.0)
    ext[rows + 1] = jnp.where(side == 0, halo, 0.0)


def put_border(border_ref, side, first, last):
    border_ref[0] = jnp.where(side == 0, last, first).astype(BF16)


def first_step():
    return pl.program_id(0) == 0


def last_step():
    return pl.program_id(0) == pl.num_programs(0) - 1


def clear(*refs):
    @pl.when(first_step())
    def _():
        for ref in refs:
            ref[...] = jnp.zeros_like(ref)


def column_sum(block):
    return jnp.sum(block.astype(F32), axis=0, keepdims=True)


def pack_tiles(pack, core, start, value):
    rows, half = value.shape[0], pack.shape[1]
    for j in range(value.shape[1] // LANES):
        tile = value[:, j * LANES : (j + 1) * LANES].astype(BF16)
        low, high = start + j * rows, start + (j + 1) * rows
        for h in range(2):
            a, b = max(low, h * half), min(high, (h + 1) * half)
            if a < b:
                pack[core ^ h, a - h * half : b - h * half, :] = tile[a - low : b - low]


def hand_out(pack, keep_ref, send_ref, sems):
    copies = [pltpu.make_async_copy(pack.at[slot], ref, sems.at[slot]) for slot, ref in enumerate((keep_ref, send_ref))]
    for copy in copies:
        copy.start()
    for copy in copies:
        copy.wait()


def window_scores(q, k, heads, group):
    lanes = slice(group * LANES, (group + 1) * LANES)
    spread_q = jnp.concatenate([q[:, lanes]] * 4, axis=0) * heads
    return dot_nt(k[:, lanes], spread_q), spread_q


def own_heads(pair):
    first = lax.broadcasted_iota(jnp.int32, (HD, LANES), 1) < SLOT
    blocks = []
    for head in range(4):
        rows, lanes = slice(head * HD, (head + 1) * HD), slice(head // 2 * LANES, (head // 2 + 1) * LANES)
        one, two = (block[rows, lanes] for block in pair)
        if head % 2:
            one = pltpu.roll(one, SLOT, 1)
        else:
            two = pltpu.roll(two, SLOT, 1)
        blocks.append(jnp.where(first, one, two))
    return jnp.concatenate(blocks, axis=0)


def over_keys(left, right, odd):
    empty = jnp.zeros_like(right)
    return dot(left, jnp.concatenate([empty, right] if odd else [right, empty], axis=0))


def stage_one(side_ref, img_ref, halo_ref, conv_ref, gain_ref, shift_ref, qkv_w, bias_ref, out_w, perm_ref, back_ref, heads_ref,
              pos_ref, nw_ref, qkv_ref, kt_ref, att_ref, mix_ref, res_ref, border_ref, ext, nrm, vt, kv_t, bias_t):
    rows = img_ref.shape[1]
    side = side_ref[0]

    @pl.when(first_step())
    def _():
        kv_t[...] = qkv_w[0, :, D:].T
        bias_t[...] = jnp.broadcast_to(bias_ref[1:2, :], (LANES, D)).T

    load_image(img_ref, halo_ref, side, ext)
    kernel = taps(conv_ref, 0)
    gain, shift = gain_ref[0:1, :], shift_ref[0:1, :]

    @pl.loop(0, rows, unroll=ROW_UNROLL)
    def _(r):
        z = conv_row(ext, r, kernel)
        pos_ref[0, r] = z
        xhat, _ = normalized(z)
        nrm[pl.ds(pl.multiple_of(r * WIDE, WIDE), WIDE), :] = (xhat * gain + shift).astype(BF16)

    heads = heads_ref[...]
    real = lax.broadcasted_iota(jnp.int32, (16, 1), 0) < WIN * WIN - 48
    mask = column_mask(STRIP)

    @pl.loop(0, rows // WIN)
    def _(s):
        image_rows = pl.ds(pl.multiple_of(s * STRIP, STRIP), STRIP)
        window_rows = pl.ds(pl.multiple_of(s * WROWS, WROWS), WROWS)
        nw = dot(perm_ref[...], nrm[image_rows, :]).astype(BF16)
        nw_ref[0, window_rows, :] = nw
        for part in range(3):
            cols = slice(part * D, (part + 1) * D)
            value = dot(nw, qkv_w[0, :, cols])
            if part != 1:
                value = value + bias_ref[part // 2 : part // 2 + 1, :]
            qkv_ref[0, window_rows, cols] = value.astype(BF16)
        kt_ref[0, s] = dot_nt(kv_t[:D, :], nw).astype(BF16)
        vt[...] = (dot_nt(kv_t[D:, :], nw) + bias_t[:, :1]).astype(BF16)
        for pair in range(2):
            columns = slice(pair * LANES, (pair + 1) * LANES)
            for group in range(GROUPS):
                lanes = slice(group * LANES, (group + 1) * LANES)
                mixed = []
                for odd in range(2):
                    slot = pl.ds(pl.multiple_of(s * WROWS + (2 * pair + odd) * SLOT, SLOT), SLOT)
                    q, k = qkv_ref[0, slot, :D], qkv_ref[0, slot, D : 2 * D]
                    scores, _ = window_scores(q, k, heads, group)
                    scores = jnp.concatenate([scores[:48], jnp.where(real, scores[48:], -1e30)], axis=0)
                    raised = jnp.exp((scores - jnp.max(scores, axis=0, keepdims=True)) * SCALE)
                    attend = raised * (1.0 / jnp.sum(raised, axis=0, keepdims=True))
                    attend = attend.astype(BF16)
                    att_ref[0, slot, group * WROWS : (group + 1) * WROWS] = attend
                    mixed.append(over_keys(vt[lanes, columns], attend, odd))
                mix_ref[0, s, lanes, columns] = own_heads(mixed).astype(BF16)
        mixed = dot_nt(back_ref[...], mix_ref[0, s]).astype(BF16)
        attn = (dot(mixed, out_w[0]) + bias_ref[2:3, :]).reshape(WIN, WIDE, D)
        strip = pl.ds(s * WIN, WIN)
        value = (pos_ref[0, strip] + attn).reshape(STRIP, D)
        res_ref[0, strip] = jnp.where(mask, value, 0.0).reshape(WIN, WIDE, D)

    put_border(border_ref, side, res_ref[0, 0], res_ref[0, rows - 1])


def load_image(img_ref, halo_ref, side, ext):
    rows = img_ref.shape[1]
    ext[...] = jnp.zeros_like(ext)

    @pl.loop(0, rows, unroll=ROW_UNROLL)
    def _(r):
        ext[r + 1, :COLS, :] = img_ref[0, r].astype(F32)

    halo = halo_ref[0].astype(F32)
    ext[0, :COLS, :] = jnp.where(side == 1, halo, 0.0)
    ext[rows + 1, :COLS, :] = jnp.where(side == 0, halo, 0.0)


def load_rows(x_ref, halo_ref, side, ext):
    rows = x_ref.shape[1]

    @pl.loop(0, rows, unroll=ROW_UNROLL)
    def _(r):
        ext[r + 1] = x_ref[0, r]

    put_halo(ext, side, halo_ref[0].astype(F32), rows)


def stage_two(side_ref, x_ref, halo_ref, conv_ref, gain_ref, shift_ref, up_w, upb_ref, down_w, downb_ref,
              pos_ref, nrm_ref, hid_ref, der_ref, res_ref, border_ref, ext):
    rows = x_ref.shape[1]
    side = side_ref[0]
    load_rows(x_ref, halo_ref, side, ext)
    kernel = taps(conv_ref, 1)
    gain, shift = gain_ref[1:2, :], shift_ref[1:2, :]

    @pl.loop(0, rows, unroll=ROW_UNROLL)
    def _(r):
        z = conv_row(ext, r, kernel)
        pos_ref[0, r] = z
        xhat, _ = normalized(z)
        nrm_ref[0, pl.ds(pl.multiple_of(r * WIDE, WIDE), WIDE), :] = (xhat * gain + shift).astype(BF16)

    mask = column_mask(rows * WIDE)

    @pl.loop(0, 1)
    def _(s):
        part = slice(0, rows * WIDE)
        nrm = nrm_ref[0, part, :]
        for c in range(FF // CHUNK):
            cols = slice(c * CHUNK, (c + 1) * CHUNK)
            hidden, slope = gelu_pair(dot(nrm, up_w[0, :, cols]) + upb_ref[0:1, cols])
            hid_ref[0, part, cols] = hidden.astype(BF16)
            der_ref[0, part, cols] = slope.astype(BF16)
        out = (dot(hid_ref[0, part, :], down_w[0]) + downb_ref[0:1, :]).reshape(rows, WIDE, D)
        strip = slice(0, rows)
        value = (pos_ref[0, strip] + out).reshape(rows * WIDE, D)
        res_ref[0, strip] = jnp.where(mask, value, 0.0).reshape(rows, WIDE, D)

    put_border(border_ref, side, res_ref[0, 0], res_ref[0, rows - 1])


def gram_fold(left, right, heads_f):
    full = dot_tn(left, right) * heads_f
    return full[:HD] + full[HD : 2 * HD] + full[2 * HD : 3 * HD] + full[3 * HD :]


def stage_three(side_ref, x_ref, halo_ref, conv_ref, gain_ref, shift_ref, qkv_w, bias_ref, valid_ref, heads_ref,
                pos_ref, nrm_ref, qkv_ref, gram_ref, ext):
    rows = x_ref.shape[1]
    load_rows(x_ref, halo_ref, side_ref[0], ext)
    kernel = taps(conv_ref, 2)
    gain, shift = gain_ref[2:3, :], shift_ref[2:3, :]

    @pl.loop(0, rows, unroll=ROW_UNROLL)
    def _(r):
        z = conv_row(ext, r, kernel)
        pos_ref[0, r] = z
        xhat, _ = normalized(z)
        nrm_ref[0, pl.ds(pl.multiple_of(r * WIDE, WIDE), WIDE), :] = (xhat * gain + shift).astype(BF16)

    @pl.loop(0, rows // WIN)
    def _(s):
        part = pl.ds(pl.multiple_of(s * STRIP, STRIP), STRIP)
        nrm = nrm_ref[0, part, :]
        valid = valid_ref[0, part, :]
        for third in range(3):
            cols = slice(third * D, (third + 1) * D)
            value = (dot(nrm, qkv_w[0, :, cols]) + bias_ref[3 + third : 4 + third, :]).astype(BF16)
            if third == 0:
                value = (value.astype(F32) * valid).astype(BF16)
            qkv_ref[0, part, cols] = value

    heads_f = heads_ref[...].astype(F32)
    for group in range(GROUPS):
        low = group * LANES
        gram_ref[0, group * HD : (group + 1) * HD, :] = gram_fold(
            qkv_ref[0, :, D + low : D + low + LANES], qkv_ref[0, :, low : low + LANES], heads_f
        )


def channel_weights(gram):
    gram = gram * (1.0 / SIDE)
    raised = jnp.exp(gram - jnp.max(gram, axis=0, keepdims=True))
    return raised / jnp.sum(raised, axis=0, keepdims=True)


def block_diagonal(block, heads):
    return jnp.concatenate([block.astype(BF16)] * 4, axis=0) * heads


def stage_four(core_ref, pos_ref, qkv_ref, gram_a, gram_b, cot_ref, out_w, bias_ref, gain_ref, shift_ref, up_w, upb_ref, down_w, downb_ref,
               heads_ref,
               out_ref, gres_ref, gm_ref, gchan_ref, keep_ref, send_ref, small_ref,
               pack, sems, mix, cotf, cotb, res, nrm, hid, gpre, gn, gb, up_acc, down_acc, out_acc, sums):
    rows = pos_ref.shape[1]
    clear(up_acc, down_acc, out_acc, sums)
    heads = heads_ref[...]
    for group in range(GROUPS):
        low = group * LANES
        gram_rows = slice(group * HD, (group + 1) * HD)
        chan = block_diagonal(channel_weights(gram_a[0, gram_rows] + gram_b[0, gram_rows]), heads)
        mix[:, low : low + LANES] = dot(qkv_ref[0, :, 2 * D + low : 2 * D + low + LANES], chan).astype(BF16)

    cotf[...] = jnp.zeros_like(cotf)

    @pl.loop(0, rows, unroll=ROW_UNROLL)
    def _(r):
        cotf[r, :COLS, :] = cot_ref[0, r].astype(F32)
        cotb[pl.ds(pl.multiple_of(r * WIDE, WIDE), WIDE), :] = cotf[r].astype(BF16)

    gain, shift = gain_ref[3:4, :], shift_ref[3:4, :]

    @pl.loop(0, 1)
    def _(s):
        part = slice(0, rows * WIDE)
        strip = slice(0, rows)
        attn = (dot(mix[part, :], out_w[0]) + bias_ref[6:7, :]).reshape(rows, WIDE, D)
        res[strip] = pos_ref[0, strip] + attn

    @pl.loop(0, rows, unroll=ROW_UNROLL)
    def _(r):
        xhat, _ = normalized(res[r])
        nrm[pl.ds(pl.multiple_of(r * WIDE, WIDE), WIDE), :] = (xhat * gain + shift).astype(BF16)

    @pl.loop(0, 1)
    def _(s):
        part = slice(0, rows * WIDE)
        strip = slice(0, rows)
        normed, cot = nrm[part, :], cotb[part, :]
        for c in range(FF // CHUNK):
            cols = slice(c * CHUNK, (c + 1) * CHUNK)
            hidden, slope = gelu_pair(dot(normed, up_w[0, :, cols]) + upb_ref[1:2, cols])
            hid[part, cols] = hidden.astype(BF16)
            grad = (slope * dot_nt(cot, down_w[0, cols, :])).astype(BF16)
            gpre[part, cols] = grad
            sums[:, cols] += folded(grad.astype(F32))
        value = (dot(hid[part, :], down_w[0]) + downb_ref[1:2, :]).reshape(rows, WIDE, D) + res[strip]
        for r in range(rows):
            out_ref[r, :, pl.ds(pl.program_id(0), 1), :] = value[r, :COLS, :].reshape(COLS, 1, D)
        gn[strip] = dot_nt(gpre[part, :], up_w[0]).reshape(rows, WIDE, D)

    @pl.loop(0, rows, unroll=ROW_UNROLL)
    def _(r):
        grad = gn[r]
        back, gain_term = normalized_back(grad, res[r], gain)
        cot = cotf[r]
        total = cot + back
        gres_ref[0, r] = total
        low = total.astype(BF16)
        gb[pl.ds(pl.multiple_of(r * WIDE, WIDE), WIDE), :] = low
        sums[:, FF : FF + D] += folded(cot)
        sums[:, FF + D : FF + 2 * D] += folded(gain_term)
        sums[:, FF + 2 * D : FF + 3 * D] += folded(grad)
        sums[:, FF + 3 * D : FF + 4 * D] += folded(low.astype(F32))

    up_acc[...] += dot_tn(nrm[...], gpre[...])
    down_acc[...] += dot_tn(cotb[...], hid[...])
    out_acc[...] += dot_tn(mix[...], gb[...])
    gm = dot_nt(gb[...], out_w[0]).astype(BF16)
    gm_ref[0] = gm
    heads_f = heads.astype(F32)
    for group in range(GROUPS):
        low = group * LANES
        gchan_ref[0, group * HD : (group + 1) * HD, :] = gram_fold(
            qkv_ref[0, :, 2 * D + low : 2 * D + low + LANES], gm[:, low : low + LANES], heads_f
        )

    @pl.when(last_step())
    def _():
        core = core_ref[0]
        pack_tiles(pack, core, 0, up_acc[...])
        pack_tiles(pack, core, MATRIX["up"], down_acc[...].T)
        pack_tiles(pack, core, 2 * MATRIX["up"], out_acc[...])
        hand_out(pack, keep_ref, send_ref, sems)
        for j in range(FF // D + 4):
            small_ref[j : j + 1, :] = jnp.sum(sums[:, j * D : (j + 1) * D], axis=0, keepdims=True)


def stage_five(side_ref, core_ref, gres_ref, pos_ref, nrm_ref, qkv_ref, gm_ref, gram_a, gram_b, gchan_a, gchan_b, valid_ref, qkv_w, gain_ref,
               heads_ref,
               gpos_ref, border_ref, keep_ref, send_ref, small_ref,
               pack, sems, joined, gn, qkv_acc, sums):
    rows = pos_ref.shape[1]
    clear(qkv_acc, sums)
    heads = heads_ref[...]
    valid = valid_ref[0]
    for group in range(GROUPS):
        low = group * LANES
        gram_rows = slice(group * HD, (group + 1) * HD)
        chan = channel_weights(gram_a[0, gram_rows] + gram_b[0, gram_rows])
        grad_chan = gchan_a[0, gram_rows] + gchan_b[0, gram_rows]
        grad_gram = chan * (grad_chan - jnp.sum(grad_chan * chan, axis=0, keepdims=True))
        chan, grad_gram = block_diagonal(chan, heads), block_diagonal(grad_gram, heads)
        lanes = slice(low, low + LANES)
        q, k = qkv_ref[0, :, lanes], qkv_ref[0, :, D + low : D + low + LANES]
        joined[:, lanes] = (dot(k, grad_gram) * (1.0 / SIDE) * valid).astype(BF16)
        joined[:, D + low : D + low + LANES] = (dot_nt(q, grad_gram) * (1.0 / SIDE)).astype(BF16)
        joined[:, 2 * D + low : 2 * D + low + LANES] = dot_nt(gm_ref[0, :, lanes], chan).astype(BF16)
    for third in range(3):
        cols = slice(third * D, (third + 1) * D)
        block = joined[:, cols]
        sums[:, cols] += folded(block.astype(F32))
        qkv_acc[:, cols] += dot_tn(nrm_ref[0], block)
    gn[...] = dot_nt(joined[...], qkv_w[0]).reshape(gn.shape)
    gain = gain_ref[2:3, :]

    @pl.loop(0, rows, unroll=ROW_UNROLL)
    def _(r):
        grad = gn[r]
        back, gain_term = normalized_back(grad, pos_ref[0, r], gain)
        gpos_ref[0, r] = gres_ref[0, r] + back
        sums[:, 3 * D : 4 * D] += folded(gain_term)
        sums[:, 4 * D : 5 * D] += folded(grad)

    put_border(border_ref, side_ref[0], gpos_ref[0, 0], gpos_ref[0, rows - 1])

    @pl.when(last_step())
    def _():
        pack_tiles(pack, core_ref[0], 0, qkv_acc[...])
        hand_out(pack, keep_ref, send_ref, sems)
        for j in range(5):
            small_ref[j : j + 1, :] = jnp.sum(sums[:, j * D : (j + 1) * D], axis=0, keepdims=True)


def stage_six(side_ref, core_ref, g_ref, halo_ref, x_ref, pos_ref, nrm_ref, hid_ref, der_ref, conv_ref, gain_ref, up_w, down_w,
              gpos_ref, border_ref, keep_ref, send_ref, small_ref,
              pack, sems, ext, gres, gb, gpre, gn, up_acc, down_acc, sums, tap_acc):
    rows = pos_ref.shape[1]
    clear(up_acc, down_acc, sums, tap_acc)
    load_rows(g_ref, halo_ref, side_ref[0], ext)
    kernel = taps(conv_ref, 2)
    mask = column_mask(WIDE)

    @pl.loop(0, rows, unroll=ROW_UNROLL)
    def _(r):
        back = jnp.where(mask, conv_row_back(ext, r, kernel), 0.0)
        gres[r] = back
        low = back.astype(BF16)
        gb[pl.ds(pl.multiple_of(r * WIDE, WIDE), WIDE), :] = low
        sums[:, FF : FF + D] += folded(low.astype(F32))
        tap_sums(x_ref[0, r], ext, r, tap_acc)

    @pl.loop(0, 1)
    def _(s):
        part = slice(0, rows * WIDE)
        grad = gb[part, :]
        for c in range(FF // CHUNK):
            cols = slice(c * CHUNK, (c + 1) * CHUNK)
            block = (der_ref[0, part, cols].astype(F32) * dot_nt(grad, down_w[0, cols, :])).astype(BF16)
            gpre[part, cols] = block
            sums[:, cols] += folded(block.astype(F32))
        gn[slice(0, rows)] = dot_nt(gpre[part, :], up_w[0]).reshape(rows, WIDE, D)

    gain = gain_ref[1:2, :]

    @pl.loop(0, rows, unroll=ROW_UNROLL)
    def _(r):
        grad = gn[r]
        back, gain_term = normalized_back(grad, pos_ref[0, r], gain)
        gpos_ref[0, r] = gres[r] + back
        sums[:, FF + D : FF + 2 * D] += folded(gain_term)
        sums[:, FF + 2 * D : FF + 3 * D] += folded(grad)

    put_border(border_ref, side_ref[0], gpos_ref[0, 0], gpos_ref[0, rows - 1])
    up_acc[...] += dot_tn(nrm_ref[0], gpre[...])
    down_acc[...] += dot_tn(gb[...], hid_ref[0])

    @pl.when(last_step())
    def _():
        pack_tiles(pack, core_ref[0], 0, up_acc[...])
        pack_tiles(pack, core_ref[0], FF // LANES * D, down_acc[...].T)
        hand_out(pack, keep_ref, send_ref, sems)
        for j in range(FF // D + 3):
            small_ref[j : j + 1, :] = jnp.sum(sums[:, j * D : (j + 1) * D], axis=0, keepdims=True)
        for j in range(10):
            small_ref[8 + j : 9 + j, :] = jnp.sum(tap_acc[j], axis=0, keepdims=True)


def stage_seven(side_ref, core_ref, small_four, small_five, small_six, g_ref, halo_ref, x_ref, pos_ref, img_ref, imghalo_ref, nw_ref, qkv_ref, kt_ref, att_ref, mix_ref, conv_ref,
                gain_ref, qkv_w, out_w, perm_ref, back_ref, heads_ref,
                gpos_ref, border_ref, keep_ref, send_ref,
                pack, sems, ext, gres, gb, joined, gqt, gn, q_acc, kv_acc, out_acc, sums, tap_acc, tap_one, small):
    rows = pos_ref.shape[1]
    side = side_ref[0]
    clear(q_acc, kv_acc, out_acc, sums, tap_acc, tap_one)
    load_rows(g_ref, halo_ref, side, ext)
    kernel = taps(conv_ref, 1)
    mask = column_mask(WIDE)

    @pl.loop(0, rows, unroll=ROW_UNROLL)
    def _(r):
        back = jnp.where(mask, conv_row_back(ext, r, kernel), 0.0)
        gres[r] = back
        low = back.astype(BF16)
        gb[pl.ds(pl.multiple_of(r * WIDE, WIDE), WIDE), :] = low
        sums[:, 3 * D : 4 * D] += folded(low.astype(F32))
        tap_sums(x_ref[0, r], ext, r, tap_acc)

    heads = heads_ref[...]

    @pl.loop(0, rows // WIN)
    def _(s):
        image_rows = pl.ds(pl.multiple_of(s * STRIP, STRIP), STRIP)
        window_rows = pl.ds(pl.multiple_of(s * WROWS, WROWS), WROWS)
        gbw = dot(perm_ref[...], gb[image_rows, :]).astype(BF16)
        out_acc[...] += dot(mix_ref[0, s], gbw)
        gm_all = dot_nt(gbw, out_w[0]).astype(BF16)
        for pair in range(2):
            columns = slice(pair * LANES, (pair + 1) * LANES)
            for group in range(GROUPS):
                low = group * LANES
                lanes = slice(low, low + LANES)
                queries = []
                for odd in range(2):
                    window = 2 * pair + odd
                    slot = pl.ds(pl.multiple_of(s * WROWS + window * SLOT, SLOT), SLOT)
                    out_rows = slice(window * SLOT, (window + 1) * SLOT)
                    q, v = qkv_ref[0, slot, :D], qkv_ref[0, slot, 2 * D :]
                    attend_b = att_ref[0, slot, group * WROWS : (group + 1) * WROWS]
                    attend = attend_b.astype(F32)
                    grad_att, spread_gm = window_scores(gm_all[out_rows], v, heads, group)
                    spread_q = jnp.concatenate([q[:, lanes]] * 4, axis=0) * heads
                    weighted = grad_att * attend
                    grad_s = (weighted - attend * jnp.sum(weighted, axis=0, keepdims=True)).astype(BF16)
                    joined[out_rows, lanes] = (dot(grad_s, spread_q) * SCALE).astype(BF16)
                    joined[out_rows, D + low : D + low + LANES] = dot(attend_b, spread_gm).astype(BF16)
                    queries.append(over_keys(kt_ref[0, s, lanes, columns], grad_s, odd))
                gqt[lanes, columns] = (own_heads(queries) * SCALE).astype(BF16)
        nw = nw_ref[0, window_rows, :]
        q_acc[...] += dot(gqt[...], nw)
        kv_acc[...] += dot_tn(nw, joined[...])
        unwound = dot_nt(back_ref[...], gqt[...]).astype(BF16)
        sums[:, :D] += folded(unwound.astype(F32))
        total = dot_nt(unwound, qkv_w[0, :, :D])
        unwound = dot(back_ref[...], joined[...]).astype(BF16)
        sums[:, 2 * D : 3 * D] += folded(unwound[:, D:].astype(F32))
        gn[pl.ds(s * WIN, WIN)] = (total + dot_nt(unwound, qkv_w[0, :, D:])).reshape(WIN, WIDE, D)

    gain = gain_ref[0:1, :]

    @pl.loop(0, rows, unroll=ROW_UNROLL)
    def _(r):
        grad = gn[r]
        back, gain_term = normalized_back(grad, pos_ref[0, r], gain)
        gpos_ref[0, r] = gres[r] + back
        sums[:, D : 2 * D] += folded(gain_term)
        sums[:, 4 * D : 5 * D] += folded(grad)

    put_border(border_ref, side, gpos_ref[0, 0], gpos_ref[0, rows - 1])
    load_image(img_ref, imghalo_ref, side, ext)

    @pl.loop(0, rows, unroll=ROW_UNROLL)
    def _(r):
        grad = gpos_ref[0, r]
        shifted = (pltpu.roll(grad, WIDE - 1, 0), grad, pltpu.roll(grad, 1, 0))
        for a in range(3):
            z = ext[r + a]
            for b in range(3):
                tap_one[3 * a + b] += folded(shifted[b] * z)
        tap_one[9] += folded(grad)

    @pl.when(last_step())
    def _():
        core = core_ref[0]
        pack_tiles(pack, core, 0, q_acc[...].T)
        pack_tiles(pack, core, D // LANES * D, kv_acc[...])
        pack_tiles(pack, core, 3 * D // LANES * D, out_acc[...])
        small[...] = jnp.zeros_like(small)
        small[0:8] = small_four[...]
        small[8:16] = small_five[...]
        small[16:40] = small_six[...]
        for j in range(5):
            small[40 + j : 41 + j, :] = jnp.sum(sums[:, j * D : (j + 1) * D], axis=0, keepdims=True)
        for j in range(10):
            small[48 + j : 49 + j, :] = jnp.sum(tap_acc[j], axis=0, keepdims=True)
            small[58 + j : 59 + j, :] = jnp.sum(tap_one[j], axis=0, keepdims=True)
        pack_tiles(pack, core, 4 * D // LANES * D, small[...])
        hand_out(pack, keep_ref, send_ref, sems)


def stage_eight(side_ref, g_ref, halo_ref, conv_ref, out_ref, ext):
    rows = g_ref.shape[1]
    load_rows(g_ref, halo_ref, side_ref[0], ext)
    kernel = taps(conv_ref, 0)

    @pl.loop(0, rows, unroll=ROW_UNROLL)
    def _(r):
        out_ref[r, :, pl.ds(pl.program_id(0), 1), :] = conv_row_back(ext, r, kernel)[:COLS].reshape(COLS, 1, D)


VMEM_LIMIT = 40 * 1024 * 1024


def per_image(shape):
    return pl.BlockSpec((1,) + tuple(shape[1:]), lambda i: (i,) + (0,) * (len(shape) - 1))


def whole(shape):
    return pl.BlockSpec(tuple(shape), lambda i: (0,) * len(shape))


def layer(array, index):
    shape = array.shape
    return pl.BlockSpec((1,) + tuple(shape[1:]), lambda i: (index,) + (0,) * (len(shape) - 1))


def scalar():
    return pl.BlockSpec(memory_space=pltpu.SMEM)


def call(body, images, in_specs, outs, scratch, microseconds, name):
    run = pl.pallas_call(
        body,
        name=name,
        grid=(images,),
        in_specs=in_specs,
        out_specs=[pl.BlockSpec(memory_space=pl.ANY) if own is None else per_image(shape) if own else whole(shape) for shape, _, own in outs],
        out_shape=[pltpu.HBM(shape, dtype) if large(shape) else jax.ShapeDtypeStruct(shape, dtype) for shape, dtype, _ in outs],
        scratch_shapes=scratch,
        compiler_params=pltpu.CompilerParams(dimension_semantics=("arbitrary",), vmem_limit_bytes=VMEM_LIMIT),
        cost_estimate=pl.CostEstimate(flops=microseconds * 1_150_000_000, bytes_accessed=1_000_000, transcendentals=0),
    )

    def placed(*arrays):
        return run(*(pltpu.with_memory_space_constraint(x, pltpu.HBM) if large(x.shape) and x.shape[0] == images else x for x in arrays))

    return placed


def large(shape):
    return np.prod(shape) > 1 << 18


def exchange(array):
    return lax.ppermute(array, "win", [(0, 1), (1, 0)])


def shards(images, valid_mask, cotangent, conv, gain, shift, qkv_w, bias, out_w, up_w, up_b, down_w, down_b):
    n, rows = images.shape[0], images.shape[1]
    side = lax.axis_index("win")
    side_arr = side.astype(jnp.int32).reshape(1)
    core_arr = (lax.axis_index("batch") % 2).astype(jnp.int32).reshape(1)
    perm, back, heads_w, heads_c = constants()
    wide = (n, rows, WIDE, D)
    inner = (rows, COLS, n, D)
    flat = rows * WIDE
    wflat = rows // WIN * WROWS
    border = (n, WIDE, D)
    valid = jnp.pad(valid_mask.astype(F32), ((0, 0), (0, 0), (0, WIDE - COLS))).reshape(n, flat, 1)
    ext = pltpu.VMEM((rows + 2, WIDE, D), F32)

    def vm(shape, dtype=F32):
        return pltpu.VMEM(shape, dtype)

    edge = jnp.where(side == 0, images[:, rows - 1], images[:, 0])
    img_halo = exchange(edge)
    small_params = [whole(conv.shape), whole(gain.shape)]

    turned = (n, rows // WIN, D, WROWS)
    pos_one, nw, qkv_one, kt, att, mix_one, res_one, edge = call(
        stage_one, n,
        [scalar(), per_image(images.shape), per_image(img_halo.shape), *small_params, whole(shift.shape), layer(qkv_w, 0),
         whole(bias.shape), layer(out_w, 0), whole(perm.shape), whole(back.shape),
         whole(heads_w.shape)],
        [(wide, F32, True), ((n, wflat, D), BF16, True), ((n, wflat, 3 * D), BF16, True), (turned, BF16, True),
         ((n, wflat, GROUPS * WROWS), BF16, True), (turned, BF16, True), (wide, F32, True), (border, BF16, True)],
        [ext, vm((flat, D), BF16), vm((D, WROWS), BF16), vm((2 * D, D), BF16), vm((D, LANES))], 23, "window_forward",
    )(side_arr, images, img_halo, conv, gain, shift, qkv_w, bias, out_w, perm, back, heads_w)

    halo = exchange(edge)
    pos_two, nrm_two, hid_one, der_one, res_two, edge = call(
        stage_two, n,
        [scalar(), per_image(wide), per_image(border), *small_params, whole(shift.shape), layer(up_w, 0), whole(up_b.shape),
         layer(down_w, 0), whole(down_b.shape)],
        [(wide, F32, True), ((n, flat, D), BF16, True), ((n, flat, FF), BF16, True), ((n, flat, FF), BF16, True), (wide, F32, True),
         (border, BF16, True)],
        [ext], 20, "mlp_one_forward",
    )(side_arr, res_one, halo, conv, gain, shift, up_w, up_b, down_w, down_b)

    halo = exchange(edge)
    gram_shape = (n, GROUPS * HD, LANES)
    pos_three, nrm_three, qkv_two, gram = call(
        stage_three, n,
        [scalar(), per_image(wide), per_image(border), *small_params, whole(shift.shape), layer(qkv_w, 1), whole(bias.shape),
         per_image(valid.shape), whole(heads_c.shape)],
        [(wide, F32, True), ((n, flat, D), BF16, True), ((n, flat, 3 * D), BF16, True), (gram_shape, F32, True)],
        [ext], 11, "channel_gram",
    )(side_arr, res_two, halo, conv, gain, shift, qkv_w, bias, valid, heads_c)

    gram_other = exchange(gram)

    devices = 2 * lax.axis_size("batch")
    four_rows = -(-MLP_PACK // devices) * devices

    def pack_outs(rows_in_pack):
        return [((rows_in_pack // 2, LANES), BF16, None)] * 2

    def pack_scratch(rows_in_pack):
        return [vm((2, rows_in_pack // 2, LANES), BF16), pltpu.SemaphoreType.DMA((2,))]

    output, gres_three, gm_two, gchan, *four, small_four = call(
        stage_four, n,
        [scalar(), per_image(wide), per_image(qkv_two.shape), per_image(gram_shape), per_image(gram_shape),
         per_image(cotangent.shape), layer(out_w, 1), whole(bias.shape), whole(gain.shape), whole(shift.shape), layer(up_w, 1),
         whole(up_b.shape), layer(down_w, 1), whole(down_b.shape), whole(heads_c.shape)],
        [(inner, F32, False), (wide, F32, True), ((n, flat, D), BF16, True), (gram_shape, F32, True),
         *pack_outs(four_rows), ((8, D), F32, False)],
        [*pack_scratch(four_rows), vm((flat, D), BF16), vm((rows, WIDE, D)), vm((flat, D), BF16), vm((rows, WIDE, D)),
         vm((flat, D), BF16), vm((flat, FF), BF16), vm((flat, FF), BF16), vm((rows, WIDE, D)), vm((flat, D), BF16),
         vm((D, FF)), vm((D, FF)), vm((D, D)), vm((8, FF + 4 * D))],
        36, "mlp_two",
    )(core_arr, pos_three, qkv_two, gram, gram_other, cotangent, out_w, bias, gain, shift, up_w, up_b, down_w, down_b,
      heads_c)

    trade = Trade()
    gchan_other = exchange(gchan)
    four = start_sum(trade, four)
    far = range(2, len(trade.order))
    gpos_three, edge, *five, small_five = call(
        stage_five, n,
        [scalar(), scalar(), per_image(wide), per_image(wide), per_image(nrm_three.shape), per_image(qkv_two.shape),
         per_image(gm_two.shape), per_image(gram_shape), per_image(gram_shape), per_image(gram_shape), per_image(gram_shape),
         per_image(valid.shape), layer(qkv_w, 1), whole(gain.shape), whole(heads_c.shape)],
        [(wide, F32, True), (border, BF16, True), *pack_outs(PIECES[0]), ((8, D), F32, False)],
        [*pack_scratch(PIECES[0]), vm((flat, 3 * D), BF16), vm((rows, WIDE, D)), vm((D, 3 * D)), vm((8, 5 * D))],
        13, "channel_backward",
    )(side_arr, core_arr, gres_three, pos_three, nrm_three, qkv_two, gm_two, gram, gram_other, gchan, gchan_other, valid, qkv_w,
      gain, heads_c)

    halo, four = lax.optimization_barrier((exchange(edge), four))
    four = trade.halve(four, far[0])
    five = start_sum(trade, five)
    gpos_two, edge, *six, small_six = call(
        stage_six, n,
        [scalar(), scalar(), per_image(wide), per_image(border), per_image(wide), per_image(wide), per_image(nrm_two.shape),
         per_image(hid_one.shape), per_image(der_one.shape), *small_params, layer(up_w, 0), layer(down_w, 0)],
        [(wide, F32, True), (border, BF16, True), *pack_outs(PIECES[1]), ((24, D), F32, False)],
        [*pack_scratch(PIECES[1]), ext, vm((rows, WIDE, D)), vm((flat, D), BF16), vm((flat, FF), BF16), vm((rows, WIDE, D)),
         vm((D, FF)), vm((D, FF)), vm((8, FF + 3 * D)), vm((10, 8, D))], 23, "mlp_one_backward",
    )(side_arr, core_arr, gpos_three, halo, res_two, pos_two, nrm_two, hid_one, der_one, conv, gain, up_w, down_w)

    halo, four, five = lax.optimization_barrier((exchange(edge), four, five))
    for step in far[1:]:
        four = trade.halve(four, step)
    five = trade.halve(five, 0)
    six = start_sum(trade, six)
    gpos_one, edge, *seven = call(
        stage_seven, n,
        [scalar(), scalar(), whole((8, D)), whole((8, D)), whole((24, D)), per_image(wide), per_image(border), per_image(wide),
         per_image(wide), per_image(images.shape), per_image(img_halo.shape), per_image(nw.shape), per_image(qkv_one.shape),
         per_image(turned), per_image(att.shape), per_image(mix_one.shape), *small_params, layer(qkv_w, 0), layer(out_w, 0), whole(perm.shape),
         whole(back.shape), whole(heads_w.shape)],
        [(wide, F32, True), (border, BF16, True), *pack_outs(PIECES[2])],
        [*pack_scratch(PIECES[2]), ext, vm((rows, WIDE, D)), vm((flat, D), BF16), vm((WROWS, 2 * D), BF16), vm((D, WROWS), BF16),
         vm((rows, WIDE, D)), vm((D, D)), vm((D, 2 * D)), vm((D, D)), vm((8, 5 * D)), vm((10, 8, D)), vm((10, 8, D)), vm((80, D))],
        35, "window_backward",
    )(side_arr, core_arr, small_four, small_five, small_six, gpos_two, halo, res_one, pos_one, images, img_halo, nw, qkv_one, kt, att,
      mix_one, conv, gain, qkv_w, out_w, perm, back, heads_w)

    four, five, six, gpos_one, edge, *seven = lax.optimization_barrier((four, five, six, gpos_one, edge, *seven))
    halo, five, six, seven = lax.optimization_barrier((exchange(edge), five, six, start_sum(trade, seven)))
    (images_grad,) = call(
        stage_eight, n, [scalar(), per_image(wide), per_image(border), whole(conv.shape)], [(inner, F32, False)], [ext],
        5, "images_backward",
    )(side_arr, gpos_one, halo, conv)

    five = trade.halve(five, 1)
    six, seven = (trade.halve(trade.halve(x, 0), 1) for x in (six, seven))
    x, four = lax.optimization_barrier((jnp.concatenate([five, six, seven], axis=0), four))
    x = trade.halve(x, far[0])
    x, images_grad = lax.optimization_barrier((x, images_grad))
    for step in far[1:]:
        x = trade.halve(x, step)
    for step in far[::-1]:
        x = trade.join(x, step)
    for step in (0, 1):
        four = trade.halve(four, step)
    for step in (1, 0):
        four = trade.join(four, step)
    x, four = lax.optimization_barrier((x, four))
    output, images_grad = (jnp.transpose(x, (2, 0, 1, 3)) for x in (output, images_grad))
    return (output, images_grad, *finish_sum(trade, x, four))


MATRIX = {"up": FF // LANES * D, "down": FF // LANES * D, "out": D // LANES * D, "qkv": 3 * D // LANES * D}
PIECES = (
    MATRIX["qkv"],
    MATRIX["up"] + MATRIX["down"],
    MATRIX["qkv"] + MATRIX["out"] + 640,
)
STARTS = tuple(sum(PIECES[:i]) for i in range(len(PIECES)))
TOTAL = sum(PIECES)
MLP_PACK = MATRIX["up"] + MATRIX["down"] + MATRIX["out"]
ROW_UNROLL = 14


class Trade:
    def __init__(self):
        self.batch = lax.axis_size("batch")
        self.place, self.win = lax.axis_index("batch"), lax.axis_index("win")
        self.core = self.place % 2
        bits = list(range((self.batch // 2).bit_length() - 1))
        one, two = ["w", *bits], [*bits[:1], "w", *bits[1:]]
        self.order = list(zip(one, two))
        self.bits = [self.bit(axes, self.core) for axes in self.order]

    def __call__(self, value, axes):
        pairs = []
        for b in range(self.batch):
            for w in range(2):
                axis = axes[b % 2]
                to = (b ^ 1, w) if axis == "c" else (b, 1 - w) if axis == "w" else (b ^ (2 << axis), w)
                pairs.append((2 * b + w, 2 * to[0] + to[1]))
        return lax.ppermute(value, ("batch", "win"), pairs)

    def of(self, axis):
        return self.win if axis == "w" else (self.place // (2 << axis)) % 2

    def bit(self, axes, core):
        return jnp.where(core == 0, self.of(axes[0]), self.of(axes[1]))

    def halve(self, x, step):
        half = x.shape[0] // 2
        sent = lax.dynamic_slice_in_dim(x, (1 - self.bits[step]) * half, half, 0)
        kept = lax.dynamic_slice_in_dim(x, self.bits[step] * half, half, 0)
        return added(kept, self(sent, self.order[step]))

    def join(self, x, step):
        got, lower = self(x, self.order[step]), self.bits[step] == 0
        return jnp.concatenate([jnp.where(lower, x, got), jnp.where(lower, got, x)], axis=0)


def added(left, right):
    return (left.astype(F32) + right.astype(F32)).astype(BF16)


def start_sum(trade, pack):
    keep, send = pack
    return added(keep, trade(send, ("c", "c")))


def finish_sum(trade, x, four):
    far = range(2, len(trade.order))
    one = [x, trade(x, trade.order[1])]
    mine = one + [trade(block, trade.order[0]) for block in one]
    theirs = [trade(block, ("c", "c")) for block in mine]
    where = []
    for core in (trade.core, 1 - trade.core):
        first, second = (trade.bit(trade.order[step], core) for step in range(2))
        for flip_first in range(2):
            for flip_second in range(2):
                where.append(core * 4 + (first ^ flip_first) * 2 + (second ^ flip_second))
    for step in far[:0:-1]:
        four = trade.join(four, step)
    pair = [four, trade(four, trade.order[far[0]])]
    fours = pair + [trade(block, ("c", "c")) for block in pair]
    bit = trade.bits[far[0]]
    where_four = [core * 2 + (bit ^ flip) for core in (trade.core, 1 - trade.core) for flip in range(2)]
    first = unpack_four(jnp.stack(where_four).astype(jnp.int32), fours)
    return unpack_rest(jnp.stack(where).astype(jnp.int32), mine + theirs, first)


UP, DOWN, OUT, QKV = (2, D, FF), (2, FF, D), (2, D, D), (2, D, 3 * D)


def unpack_four_kernel(where_ref, *refs):
    blocks, (up_out, down_out, out_out), (buf, sems) = refs[:4], refs[4:7], refs[7:]
    size = blocks[0].shape[0]
    copies = []
    for t, block in enumerate(blocks):
        target = pl.ds(pl.multiple_of(where_ref[t] * size, 16), size)
        copies.append(pltpu.make_async_copy(block, buf.at[target], sems.at[t]))
    for copy in copies:
        copy.start()
    for copy in copies:
        copy.wait()
    start = 0
    for ref in (up_out, down_out, out_out):
        height, width = ref.shape[1:]
        for j in range(width // LANES):
            ref[0, :, j * LANES : (j + 1) * LANES] = buf[start : start + height, :].astype(F32)
            start += height


def unpack_four(where, blocks):
    shapes = (UP, DOWN, OUT)
    return pl.pallas_call(
        unpack_four_kernel,
        name="unpack_four",
        grid=(1,),
        in_specs=[scalar()] + [pl.BlockSpec(memory_space=pl.ANY)] * 4,
        out_specs=[pl.BlockSpec((1,) + shape[1:], lambda i: (1, 0, 0)) for shape in shapes],
        out_shape=[jax.ShapeDtypeStruct(shape, F32) for shape in shapes],
        scratch_shapes=[pltpu.VMEM((4 * blocks[0].shape[0], LANES), BF16), pltpu.SemaphoreType.DMA((4,))],
        compiler_params=pltpu.CompilerParams(vmem_limit_bytes=VMEM_LIMIT),
    )(where, *blocks)


def unpack_rest_kernel(where_ref, *refs):
    blocks, outs, (buf, up_buf, down_buf, out_buf, sems, out_sems) = refs[:8], refs[11:21], refs[21:]
    up_out, down_out, out_out, conv_out, gain_out, shift_out, qkv_out, bias_out, upb_out, downb_out = outs
    copies = []
    for p, piece in enumerate(PIECES):
        size, source = piece // 8, STARTS[p] // 8
        for t, block in enumerate(blocks):
            target = pl.ds(pl.multiple_of(STARTS[p] + where_ref[t] * size, 16), size)
            copies.append(pltpu.make_async_copy(block.at[source : source + size], buf.at[target], sems.at[t, p]))
    order = (1, 2, 0)
    for p in order:
        for copy in copies[8 * p : 8 * p + 8]:
            copy.start()

    def arrived(p):
        for copy in copies[8 * p : 8 * p + 8]:
            copy.wait()

    def matrix(store, height, width, start):
        for j in range(width // LANES):
            low = start + j * height
            store(slice(j * LANES, (j + 1) * LANES), buf[low : low + height, :].astype(F32))

    def into(ref, *index):
        def store(lanes, value):
            ref[(*index, slice(None), lanes)] = value

        return store

    sent = []

    def send(source, target):
        copy = pltpu.make_async_copy(source, target.at[0], out_sems.at[len(sent)])
        copy.start()
        sent.append(copy)

    arrived(1)
    matrix(into(up_buf), D, FF, STARTS[1])
    send(up_buf, up_out)
    matrix(into(down_buf), FF, D, STARTS[1] + MATRIX["up"])
    send(down_buf, down_out)
    arrived(2)
    matrix(into(out_buf), D, D, STARTS[2] + MATRIX["qkv"])
    send(out_buf, out_out)
    matrix(into(qkv_out, 0), D, 3 * D, STARTS[2])
    base = STARTS[2] + MATRIX["qkv"] + MATRIX["out"]
    for j in range(GROUPS):
        lanes = slice(j * LANES, (j + 1) * LANES)
        small = buf[base + j * 80 : base + (j + 1) * 80, :].astype(F32)
        for index, first in enumerate((58, 48, 24)):
            conv_out[:, index : index + 1, lanes] = small[first : first + 10].reshape(10, 1, LANES)
        for ref, rows in ((gain_out, (41, 21, 11, 5)), (shift_out, (44, 22, 12, 6)), (bias_out, (40, 42, 43, 8, 9, 10, 7)),
                          (downb_out, (20, 4))):
            for index, row in enumerate(rows):
                ref[index : index + 1, lanes] = small[row : row + 1]
        for index, first in enumerate((16, 0)):
            for r in range(FF // D):
                low = r * D + j * LANES
                upb_out[index : index + 1, low : low + LANES] = small[first + r : first + r + 1]
    arrived(0)
    matrix(into(qkv_out, 1), D, 3 * D, STARTS[0])
    for copy in sent:
        copy.wait()


def unpack_rest(where, blocks, first):
    shapes = [UP, DOWN, OUT, (10, 3, D), (4, D), (4, D), QKV, (7, D), (2, FF), (2, D)]
    hbm, vmem = pl.BlockSpec(memory_space=pl.ANY), pl.BlockSpec(memory_space=pltpu.VMEM)
    up, down, out, conv, gain, shift, qkv, bias, up_bias, down_bias = pl.pallas_call(
        unpack_rest_kernel,
        name="unpack_rest",
        in_specs=[pl.BlockSpec(memory_space=pltpu.SMEM)] + [hbm] * 11,
        out_specs=[hbm] * 3 + [vmem] * 7,
        out_shape=[jax.ShapeDtypeStruct(shape, F32) for shape in shapes],
        input_output_aliases={9: 0, 10: 1, 11: 2},
        scratch_shapes=[pltpu.VMEM((TOTAL, LANES), BF16), pltpu.VMEM((D, FF), F32), pltpu.VMEM((FF, D), F32), pltpu.VMEM((D, D), F32),
                        pltpu.SemaphoreType.DMA((8, len(PIECES))), pltpu.SemaphoreType.DMA((3,))],
        compiler_params=pltpu.CompilerParams(vmem_limit_bytes=VMEM_LIMIT),
    )(where, *blocks, *first)
    return conv.transpose(1, 0, 2), gain, shift, qkv, bias, out, up, up_bias, down, down_bias


def solution(mesh):
    split = P("batch", "win", None, None)
    in_specs = (split, P("batch", "win", None), split) + (P(),) * 10
    out_specs = (split, split) + (P(),) * 10
    return jax.shard_map(shards, mesh=mesh, in_specs=in_specs, out_specs=out_specs, check_vma=False)
```

```python
import functools

import jax
import jax.numpy as jnp
import numpy as np
from jax import lax
from jax.experimental import pallas as pl
from jax.experimental.pallas import tpu as pltpu
from jax.sharding import PartitionSpec as P

D = 384
HEADS = 12
HD = 32
FF = 1536
WIN = 7
COLS = 28
WIDE = 32
SLOT = 64
GROUPS = 3
LANES = 128
SIDE = 28
CHUNK = 256
EPS = 1e-05
SCALE = HD ** (-0.5)
F32 = jnp.float32
BF16 = jnp.bfloat16

STRIP = WIN * WIDE
WROWS = 4 * SLOT


def constants():
    perm = np.zeros((WROWS, STRIP), np.float32)
    for window in range(4):
        for r in range(WIN):
            for c in range(WIN):
                perm[window * SLOT + r * WIN + c, r * WIDE + window * WIN + c] = 1.0
    heads_window = np.zeros((4 * SLOT, LANES), np.float32)
    heads_channel = np.zeros((LANES, LANES), np.float32)
    for head in range(4):
        heads_window[head * SLOT : (head + 1) * SLOT, head * HD : (head + 1) * HD] = 1.0
        heads_channel[head * HD : (head + 1) * HD, head * HD : (head + 1) * HD] = 1.0
    return (
        jnp.asarray(perm, BF16),
        jnp.asarray(perm.T, BF16),
        jnp.asarray(heads_window, BF16),
        jnp.asarray(heads_channel, BF16),
    )


def dot(left, right):
    return jnp.dot(left, right, preferred_element_type=F32)


def dot_nt(left, right):
    return lax.dot_general(left, right, (((1,), (1,)), ((), ())), preferred_element_type=F32)


def dot_tn(left, right):
    return lax.dot_general(left, right, (((0,), (0,)), ((), ())), preferred_element_type=F32)


def normalized(z):
    center = z - jnp.sum(z, axis=-1, keepdims=True) * (1.0 / D)
    spread = jnp.sum(center * center, axis=-1, keepdims=True) * (1.0 / D)
    scale = lax.rsqrt(spread + EPS)
    return center * scale, scale


def normalized_back(grad, z, gain):
    xhat, scale = normalized(z)
    scaled = grad * gain
    mean_one = jnp.sum(scaled, axis=-1, keepdims=True) * (1.0 / D)
    mean_two = jnp.sum(scaled * xhat, axis=-1, keepdims=True) * (1.0 / D)
    return (scaled - mean_one - xhat * mean_two) * scale, grad * xhat


TAIL = 0.39 * 0.5**0.5
ERFC = tuple(
    0.5 * c
    for c in (
        0.2353252479818039,
        0.091388231495776,
        0.6495598567387839,
        -0.6354008448449706,
        0.886664715384384,
        -0.2275372084398586,
    )
)


def gelu_pair(x):
    bell = jnp.exp2(x * x * (-0.5 * np.log2(np.e)))
    t = pl.reciprocal(1.0 + TAIL * jnp.abs(x))
    poly = ERFC[5] * t + ERFC[4]
    for c in (ERFC[3], ERFC[2], ERFC[1], ERFC[0]):
        poly = poly * t + c
    tail = poly * t * bell
    below = jnp.where(x >= 0, 1.0 - tail, tail)
    return x * below, below + x * bell * ((2.0 * np.pi) ** -0.5)


def column_mask(rows):
    return lax.broadcasted_iota(jnp.int32, (rows, 1), 0) % WIDE < COLS


def folded(block):
    return jnp.sum(block.reshape(block.shape[0] // 8, 8, block.shape[1]), axis=0)


def conv_row(ext, row, kernel):
    above, here, below = ext[row], ext[row + 1], ext[row + 2]
    left = kernel[0] * above + kernel[3] * here + kernel[6] * below
    center = kernel[1] * above + (1.0 + kernel[4]) * here + kernel[7] * below + kernel[9]
    right = kernel[2] * above + kernel[5] * here + kernel[8] * below
    return center + pltpu.roll(left, 1, 0) + pltpu.roll(right, WIDE - 1, 0)


def conv_row_back(ext, row, kernel):
    above, here, below = ext[row], ext[row + 1], ext[row + 2]
    left = kernel[0] * below + kernel[3] * here + kernel[6] * above
    center = kernel[1] * below + (1.0 + kernel[4]) * here + kernel[7] * above
    right = kernel[2] * below + kernel[5] * here + kernel[8] * above
    return center + pltpu.roll(left, WIDE - 1, 0) + pltpu.roll(right, 1, 0)


def tap_sums(z, ext, row, taps_ref):
    shifted = (pltpu.roll(z, 1, 0), z, pltpu.roll(z, WIDE - 1, 0))
    for a in range(3):
        grad = ext[row + 2 - a]
        for b in range(3):
            taps_ref[3 * a + b] += folded(shifted[b] * grad)
    taps_ref[9] += folded(ext[row + 1])


def taps(ref, layer):
    return [ref[layer, j : j + 1, :] for j in range(10)]


def put_halo(ext, side, halo, rows):
    ext[0] = jnp.where(side == 1, halo, 0.0)
    ext[rows + 1] = jnp.where(side == 0, halo, 0.0)


def put_border(border_ref, side, first, last):
    border_ref[0] = jnp.where(side == 0, last, first).astype(BF16)


def first_step():
    return pl.program_id(0) == 0


def last_step():
    return pl.program_id(0) == pl.num_programs(0) - 1


def clear(*refs):
    @pl.when(first_step())
    def _():
        for ref in refs:
            ref[...] = jnp.zeros_like(ref)


def column_sum(block):
    return jnp.sum(block.astype(F32), axis=0, keepdims=True)


def pack_tiles(pack, core, start, value):
    rows, half = value.shape[0], pack.shape[1]
    for j in range(value.shape[1] // LANES):
        tile = value[:, j * LANES : (j + 1) * LANES].astype(BF16)
        low, high = start + j * rows, start + (j + 1) * rows
        for h in range(2):
            a, b = max(low, h * half), min(high, (h + 1) * half)
            if a < b:
                pack[core ^ h, a - h * half : b - h * half, :] = tile[a - low : b - low]


def hand_out(pack, keep_ref, send_ref, sems):
    copies = [pltpu.make_async_copy(pack.at[slot], ref, sems.at[slot]) for slot, ref in enumerate((keep_ref, send_ref))]
    for copy in copies:
        copy.start()
    for copy in copies:
        copy.wait()


def window_scores(q, k, heads, group):
    lanes = slice(group * LANES, (group + 1) * LANES)
    spread_q = jnp.concatenate([q[:, lanes]] * 4, axis=0) * heads
    return dot_nt(k[:, lanes], spread_q), spread_q


def own_heads(pair):
    first = lax.broadcasted_iota(jnp.int32, (HD, LANES), 1) < SLOT
    blocks = []
    for head in range(4):
        rows, lanes = slice(head * HD, (head + 1) * HD), slice(head // 2 * LANES, (head // 2 + 1) * LANES)
        one, two = (block[rows, lanes] for block in pair)
        if head % 2:
            one = pltpu.roll(one, SLOT, 1)
        else:
            two = pltpu.roll(two, SLOT, 1)
        blocks.append(jnp.where(first, one, two))
    return jnp.concatenate(blocks, axis=0)


def over_keys(left, right, odd):
    empty = jnp.zeros_like(right)
    return dot(left, jnp.concatenate([empty, right] if odd else [right, empty], axis=0))


def stage_one(side_ref, img_ref, halo_ref, conv_ref, gain_ref, shift_ref, qkv_w, bias_ref, out_w, perm_ref, back_ref, heads_ref,
              pos_ref, nw_ref, qkv_ref, kt_ref, att_ref, mix_ref, res_ref, border_ref, ext, nrm, vt, kv_t, bias_t):
    rows = img_ref.shape[1]
    side = side_ref[0]

    @pl.when(first_step())
    def _():
        kv_t[...] = qkv_w[0, :, D:].T
        bias_t[...] = jnp.broadcast_to(bias_ref[1:2, :], (LANES, D)).T

    load_image(img_ref, halo_ref, side, ext)
    kernel = taps(conv_ref, 0)
    gain, shift = gain_ref[0:1, :], shift_ref[0:1, :]

    @pl.loop(0, rows, unroll=ROW_UNROLL)
    def _(r):
        z = conv_row(ext, r, kernel)
        pos_ref[0, r] = z
        xhat, _ = normalized(z)
        nrm[pl.ds(pl.multiple_of(r * WIDE, WIDE), WIDE), :] = (xhat * gain + shift).astype(BF16)

    heads = heads_ref[...]
    real = lax.broadcasted_iota(jnp.int32, (16, 1), 0) < WIN * WIN - 48
    mask = column_mask(STRIP)

    @pl.loop(0, rows // WIN)
    def _(s):
        image_rows = pl.ds(pl.multiple_of(s * STRIP, STRIP), STRIP)
        window_rows = pl.ds(pl.multiple_of(s * WROWS, WROWS), WROWS)
        nw = dot(perm_ref[...], nrm[image_rows, :]).astype(BF16)
        nw_ref[0, window_rows, :] = nw
        for part in range(3):
            cols = slice(part * D, (part + 1) * D)
            value = dot(nw, qkv_w[0, :, cols])
            if part != 1:
                value = value + bias_ref[part // 2 : part // 2 + 1, :]
            qkv_ref[0, window_rows, cols] = value.astype(BF16)
        kt_ref[0, s] = dot_nt(kv_t[:D, :], nw).astype(BF16)
        vt[...] = (dot_nt(kv_t[D:, :], nw) + bias_t[:, :1]).astype(BF16)
        for pair in range(2):
            columns = slice(pair * LANES, (pair + 1) * LANES)
            for group in range(GROUPS):
                lanes = slice(group * LANES, (group + 1) * LANES)
                mixed = []
                for odd in range(2):
                    slot = pl.ds(pl.multiple_of(s * WROWS + (2 * pair + odd) * SLOT, SLOT), SLOT)
                    q, k = qkv_ref[0, slot, :D], qkv_ref[0, slot, D : 2 * D]
                    scores, _ = window_scores(q, k, heads, group)
                    scores = jnp.concatenate([scores[:48], jnp.where(real, scores[48:], -1e30)], axis=0)
                    raised = jnp.exp((scores - jnp.max(scores, axis=0, keepdims=True)) * SCALE)
                    attend = raised * (1.0 / jnp.sum(raised, axis=0, keepdims=True))
                    attend = attend.astype(BF16)
                    att_ref[0, slot, group * WROWS : (group + 1) * WROWS] = attend
                    mixed.append(over_keys(vt[lanes, columns], attend, odd))
                mix_ref[0, s, lanes, columns] = own_heads(mixed).astype(BF16)
        mixed = dot_nt(back_ref[...], mix_ref[0, s]).astype(BF16)
        attn = (dot(mixed, out_w[0]) + bias_ref[2:3, :]).reshape(WIN, WIDE, D)
        strip = pl.ds(s * WIN, WIN)
        value = (pos_ref[0, strip] + attn).reshape(STRIP, D)
        res_ref[0, strip] = jnp.where(mask, value, 0.0).reshape(WIN, WIDE, D)

    put_border(border_ref, side, res_ref[0, 0], res_ref[0, rows - 1])


def load_image(img_ref, halo_ref, side, ext):
    rows = img_ref.shape[1]
    ext[...] = jnp.zeros_like(ext)

    @pl.loop(0, rows, unroll=ROW_UNROLL)
    def _(r):
        ext[r + 1, :COLS, :] = img_ref[0, r].astype(F32)

    halo = halo_ref[0].astype(F32)
    ext[0, :COLS, :] = jnp.where(side == 1, halo, 0.0)
    ext[rows + 1, :COLS, :] = jnp.where(side == 0, halo, 0.0)


def load_rows(x_ref, halo_ref, side, ext):
    rows = x_ref.shape[1]

    @pl.loop(0, rows, unroll=ROW_UNROLL)
    def _(r):
        ext[r + 1] = x_ref[0, r]

    put_halo(ext, side, halo_ref[0].astype(F32), rows)


def stage_two(side_ref, x_ref, halo_ref, conv_ref, gain_ref, shift_ref, up_w, upb_ref, down_w, downb_ref,
              pos_ref, nrm_ref, hid_ref, der_ref, res_ref, border_ref, ext):
    rows = x_ref.shape[1]
    side = side_ref[0]
    load_rows(x_ref, halo_ref, side, ext)
    kernel = taps(conv_ref, 1)
    gain, shift = gain_ref[1:2, :], shift_ref[1:2, :]

    @pl.loop(0, rows, unroll=ROW_UNROLL)
    def _(r):
        z = conv_row(ext, r, kernel)
        pos_ref[0, r] = z
        xhat, _ = normalized(z)
        nrm_ref[0, pl.ds(pl.multiple_of(r * WIDE, WIDE), WIDE), :] = (xhat * gain + shift).astype(BF16)

    mask = column_mask(rows * WIDE)

    @pl.loop(0, 1)
    def _(s):
        part = slice(0, rows * WIDE)
        nrm = nrm_ref[0, part, :]
        for c in range(FF // CHUNK):
            cols = slice(c * CHUNK, (c + 1) * CHUNK)
            hidden, slope = gelu_pair(dot(nrm, up_w[0, :, cols]) + upb_ref[0:1, cols])
            hid_ref[0, part, cols] = hidden.astype(BF16)
            der_ref[0, part, cols] = slope.astype(BF16)
        out = (dot(hid_ref[0, part, :], down_w[0]) + downb_ref[0:1, :]).reshape(rows, WIDE, D)
        strip = slice(0, rows)
        value = (pos_ref[0, strip] + out).reshape(rows * WIDE, D)
        res_ref[0, strip] = jnp.where(mask, value, 0.0).reshape(rows, WIDE, D)

    put_border(border_ref, side, res_ref[0, 0], res_ref[0, rows - 1])


def gram_fold(left, right, heads_f):
    full = dot_tn(left, right) * heads_f
    return full[:HD] + full[HD : 2 * HD] + full[2 * HD : 3 * HD] + full[3 * HD :]


def stage_three(side_ref, x_ref, halo_ref, conv_ref, gain_ref, shift_ref, qkv_w, bias_ref, valid_ref, heads_ref,
                pos_ref, nrm_ref, qkv_ref, gram_ref, ext):
    rows = x_ref.shape[1]
    load_rows(x_ref, halo_ref, side_ref[0], ext)
    kernel = taps(conv_ref, 2)
    gain, shift = gain_ref[2:3, :], shift_ref[2:3, :]

    @pl.loop(0, rows, unroll=ROW_UNROLL)
    def _(r):
        z = conv_row(ext, r, kernel)
        pos_ref[0, r] = z
        xhat, _ = normalized(z)
        nrm_ref[0, pl.ds(pl.multiple_of(r * WIDE, WIDE), WIDE), :] = (xhat * gain + shift).astype(BF16)

    @pl.loop(0, rows // WIN)
    def _(s):
        part = pl.ds(pl.multiple_of(s * STRIP, STRIP), STRIP)
        nrm = nrm_ref[0, part, :]
        valid = valid_ref[0, part, :]
        for third in range(3):
            cols = slice(third * D, (third + 1) * D)
            value = (dot(nrm, qkv_w[0, :, cols]) + bias_ref[3 + third : 4 + third, :]).astype(BF16)
            if third == 0:
                value = (value.astype(F32) * valid).astype(BF16)
            qkv_ref[0, part, cols] = value

    heads_f = heads_ref[...].astype(F32)
    for group in range(GROUPS):
        low = group * LANES
        gram_ref[0, group * HD : (group + 1) * HD, :] = gram_fold(
            qkv_ref[0, :, D + low : D + low + LANES], qkv_ref[0, :, low : low + LANES], heads_f
        )


def channel_weights(gram):
    gram = gram * (1.0 / SIDE)
    raised = jnp.exp(gram - jnp.max(gram, axis=0, keepdims=True))
    return raised / jnp.sum(raised, axis=0, keepdims=True)


def block_diagonal(block, heads):
    return jnp.concatenate([block.astype(BF16)] * 4, axis=0) * heads


def stage_four(core_ref, pos_ref, qkv_ref, gram_a, gram_b, cot_ref, out_w, bias_ref, gain_ref, shift_ref, up_w, upb_ref, down_w, downb_ref,
               heads_ref,
               out_ref, gres_ref, gm_ref, gchan_ref, keep_ref, send_ref, small_ref,
               pack, sems, mix, cotf, cotb, res, nrm, hid, gpre, gn, gb, up_acc, down_acc, out_acc, sums):
    rows = pos_ref.shape[1]
    clear(up_acc, down_acc, out_acc, sums)
    heads = heads_ref[...]
    for group in range(GROUPS):
        low = group * LANES
        gram_rows = slice(group * HD, (group + 1) * HD)
        chan = block_diagonal(channel_weights(gram_a[0, gram_rows] + gram_b[0, gram_rows]), heads)
        mix[:, low : low + LANES] = dot(qkv_ref[0, :, 2 * D + low : 2 * D + low + LANES], chan).astype(BF16)

    cotf[...] = jnp.zeros_like(cotf)

    @pl.loop(0, rows, unroll=ROW_UNROLL)
    def _(r):
        cotf[r, :COLS, :] = cot_ref[0, r].astype(F32)
        cotb[pl.ds(pl.multiple_of(r * WIDE, WIDE), WIDE), :] = cotf[r].astype(BF16)

    gain, shift = gain_ref[3:4, :], shift_ref[3:4, :]

    @pl.loop(0, 1)
    def _(s):
        part = slice(0, rows * WIDE)
        strip = slice(0, rows)
        attn = (dot(mix[part, :], out_w[0]) + bias_ref[6:7, :]).reshape(rows, WIDE, D)
        res[strip] = pos_ref[0, strip] + attn

    @pl.loop(0, rows, unroll=ROW_UNROLL)
    def _(r):
        xhat, _ = normalized(res[r])
        nrm[pl.ds(pl.multiple_of(r * WIDE, WIDE), WIDE), :] = (xhat * gain + shift).astype(BF16)

    @pl.loop(0, 1)
    def _(s):
        part = slice(0, rows * WIDE)
        strip = slice(0, rows)
        normed, cot = nrm[part, :], cotb[part, :]
        for c in range(FF // CHUNK):
            cols = slice(c * CHUNK, (c + 1) * CHUNK)
            hidden, slope = gelu_pair(dot(normed, up_w[0, :, cols]) + upb_ref[1:2, cols])
            hid[part, cols] = hidden.astype(BF16)
            grad = (slope * dot_nt(cot, down_w[0, cols, :])).astype(BF16)
            gpre[part, cols] = grad
            sums[:, cols] += folded(grad.astype(F32))
        value = (dot(hid[part, :], down_w[0]) + downb_ref[1:2, :]).reshape(rows, WIDE, D) + res[strip]
        for r in range(rows):
            out_ref[r, :, pl.ds(pl.program_id(0), 1), :] = value[r, :COLS, :].reshape(COLS, 1, D)
        gn[strip] = dot_nt(gpre[part, :], up_w[0]).reshape(rows, WIDE, D)

    @pl.loop(0, rows, unroll=ROW_UNROLL)
    def _(r):
        grad = gn[r]
        back, gain_term = normalized_back(grad, res[r], gain)
        cot = cotf[r]
        total = cot + back
        gres_ref[0, r] = total
        low = total.astype(BF16)
        gb[pl.ds(pl.multiple_of(r * WIDE, WIDE), WIDE), :] = low
        sums[:, FF : FF + D] += folded(cot)
        sums[:, FF + D : FF + 2 * D] += folded(gain_term)
        sums[:, FF + 2 * D : FF + 3 * D] += folded(grad)
        sums[:, FF + 3 * D : FF + 4 * D] += folded(low.astype(F32))

    up_acc[...] += dot_tn(nrm[...], gpre[...])
    down_acc[...] += dot_tn(cotb[...], hid[...])
    out_acc[...] += dot_tn(mix[...], gb[...])
    gm = dot_nt(gb[...], out_w[0]).astype(BF16)
    gm_ref[0] = gm
    heads_f = heads.astype(F32)
    for group in range(GROUPS):
        low = group * LANES
        gchan_ref[0, group * HD : (group + 1) * HD, :] = gram_fold(
            qkv_ref[0, :, 2 * D + low : 2 * D + low + LANES], gm[:, low : low + LANES], heads_f
        )

    @pl.when(last_step())
    def _():
        core = core_ref[0]
        pack_tiles(pack, core, 0, up_acc[...])
        pack_tiles(pack, core, MATRIX["up"], down_acc[...].T)
        pack_tiles(pack, core, 2 * MATRIX["up"], out_acc[...])
        hand_out(pack, keep_ref, send_ref, sems)
        for j in range(FF // D + 4):
            small_ref[j : j + 1, :] = jnp.sum(sums[:, j * D : (j + 1) * D], axis=0, keepdims=True)


def stage_five(side_ref, core_ref, gres_ref, pos_ref, nrm_ref, qkv_ref, gm_ref, gram_a, gram_b, gchan_a, gchan_b, valid_ref, qkv_w, gain_ref,
               heads_ref,
               gpos_ref, border_ref, keep_ref, send_ref, small_ref,
               pack, sems, joined, gn, qkv_acc, sums):
    rows = pos_ref.shape[1]
    clear(qkv_acc, sums)
    heads = heads_ref[...]
    valid = valid_ref[0]
    for group in range(GROUPS):
        low = group * LANES
        gram_rows = slice(group * HD, (group + 1) * HD)
        chan = channel_weights(gram_a[0, gram_rows] + gram_b[0, gram_rows])
        grad_chan = gchan_a[0, gram_rows] + gchan_b[0, gram_rows]
        grad_gram = chan * (grad_chan - jnp.sum(grad_chan * chan, axis=0, keepdims=True))
        chan, grad_gram = block_diagonal(chan, heads), block_diagonal(grad_gram, heads)
        lanes = slice(low, low + LANES)
        q, k = qkv_ref[0, :, lanes], qkv_ref[0, :, D + low : D + low + LANES]
        joined[:, lanes] = (dot(k, grad_gram) * (1.0 / SIDE) * valid).astype(BF16)
        joined[:, D + low : D + low + LANES] = (dot_nt(q, grad_gram) * (1.0 / SIDE)).astype(BF16)
        joined[:, 2 * D + low : 2 * D + low + LANES] = dot_nt(gm_ref[0, :, lanes], chan).astype(BF16)
    for third in range(3):
        cols = slice(third * D, (third + 1) * D)
        block = joined[:, cols]
        sums[:, cols] += folded(block.astype(F32))
        qkv_acc[:, cols] += dot_tn(nrm_ref[0], block)
    gn[...] = dot_nt(joined[...], qkv_w[0]).reshape(gn.shape)
    gain = gain_ref[2:3, :]

    @pl.loop(0, rows, unroll=ROW_UNROLL)
    def _(r):
        grad = gn[r]
        back, gain_term = normalized_back(grad, pos_ref[0, r], gain)
        gpos_ref[0, r] = gres_ref[0, r] + back
        sums[:, 3 * D : 4 * D] += folded(gain_term)
        sums[:, 4 * D : 5 * D] += folded(grad)

    put_border(border_ref, side_ref[0], gpos_ref[0, 0], gpos_ref[0, rows - 1])

    @pl.when(last_step())
    def _():
        pack_tiles(pack, core_ref[0], 0, qkv_acc[...])
        hand_out(pack, keep_ref, send_ref, sems)
        for j in range(5):
            small_ref[j : j + 1, :] = jnp.sum(sums[:, j * D : (j + 1) * D], axis=0, keepdims=True)


def stage_six(side_ref, core_ref, g_ref, halo_ref, x_ref, pos_ref, nrm_ref, hid_ref, der_ref, conv_ref, gain_ref, up_w, down_w,
              gpos_ref, border_ref, keep_ref, send_ref, small_ref,
              pack, sems, ext, gres, gb, gpre, gn, up_acc, down_acc, sums, tap_acc):
    rows = pos_ref.shape[1]
    clear(up_acc, down_acc, sums, tap_acc)
    load_rows(g_ref, halo_ref, side_ref[0], ext)
    kernel = taps(conv_ref, 2)
    mask = column_mask(WIDE)

    @pl.loop(0, rows, unroll=ROW_UNROLL)
    def _(r):
        back = jnp.where(mask, conv_row_back(ext, r, kernel), 0.0)
        gres[r] = back
        low = back.astype(BF16)
        gb[pl.ds(pl.multiple_of(r * WIDE, WIDE), WIDE), :] = low
        sums[:, FF : FF + D] += folded(low.astype(F32))
        tap_sums(x_ref[0, r], ext, r, tap_acc)

    @pl.loop(0, 1)
    def _(s):
        part = slice(0, rows * WIDE)
        grad = gb[part, :]
        for c in range(FF // CHUNK):
            cols = slice(c * CHUNK, (c + 1) * CHUNK)
            block = (der_ref[0, part, cols].astype(F32) * dot_nt(grad, down_w[0, cols, :])).astype(BF16)
            gpre[part, cols] = block
            sums[:, cols] += folded(block.astype(F32))
        gn[slice(0, rows)] = dot_nt(gpre[part, :], up_w[0]).reshape(rows, WIDE, D)

    gain = gain_ref[1:2, :]

    @pl.loop(0, rows, unroll=ROW_UNROLL)
    def _(r):
        grad = gn[r]
        back, gain_term = normalized_back(grad, pos_ref[0, r], gain)
        gpos_ref[0, r] = gres[r] + back
        sums[:, FF + D : FF + 2 * D] += folded(gain_term)
        sums[:, FF + 2 * D : FF + 3 * D] += folded(grad)

    put_border(border_ref, side_ref[0], gpos_ref[0, 0], gpos_ref[0, rows - 1])
    up_acc[...] += dot_tn(nrm_ref[0], gpre[...])
    down_acc[...] += dot_tn(gb[...], hid_ref[0])

    @pl.when(last_step())
    def _():
        pack_tiles(pack, core_ref[0], 0, up_acc[...])
        pack_tiles(pack, core_ref[0], FF // LANES * D, down_acc[...].T)
        hand_out(pack, keep_ref, send_ref, sems)
        for j in range(FF // D + 3):
            small_ref[j : j + 1, :] = jnp.sum(sums[:, j * D : (j + 1) * D], axis=0, keepdims=True)
        for j in range(10):
            small_ref[8 + j : 9 + j, :] = jnp.sum(tap_acc[j], axis=0, keepdims=True)


def stage_seven(side_ref, core_ref, small_four, small_five, small_six, g_ref, halo_ref, x_ref, pos_ref, img_ref, imghalo_ref, nw_ref, qkv_ref, kt_ref, att_ref, mix_ref, conv_ref,
                gain_ref, qkv_w, out_w, perm_ref, back_ref, heads_ref,
                gpos_ref, border_ref, keep_ref, send_ref,
                pack, sems, ext, gres, gb, joined, gqt, gn, q_acc, kv_acc, out_acc, sums, tap_acc, tap_one, small):
    rows = pos_ref.shape[1]
    side = side_ref[0]
    clear(q_acc, kv_acc, out_acc, sums, tap_acc, tap_one)
    load_rows(g_ref, halo_ref, side, ext)
    kernel = taps(conv_ref, 1)
    mask = column_mask(WIDE)

    @pl.loop(0, rows, unroll=ROW_UNROLL)
    def _(r):
        back = jnp.where(mask, conv_row_back(ext, r, kernel), 0.0)
        gres[r] = back
        low = back.astype(BF16)
        gb[pl.ds(pl.multiple_of(r * WIDE, WIDE), WIDE), :] = low
        sums[:, 3 * D : 4 * D] += folded(low.astype(F32))
        tap_sums(x_ref[0, r], ext, r, tap_acc)

    heads = heads_ref[...]

    @pl.loop(0, rows // WIN)
    def _(s):
        image_rows = pl.ds(pl.multiple_of(s * STRIP, STRIP), STRIP)
        window_rows = pl.ds(pl.multiple_of(s * WROWS, WROWS), WROWS)
        gbw = dot(perm_ref[...], gb[image_rows, :]).astype(BF16)
        out_acc[...] += dot(mix_ref[0, s], gbw)
        gm_all = dot_nt(gbw, out_w[0]).astype(BF16)
        for pair in range(2):
            columns = slice(pair * LANES, (pair + 1) * LANES)
            for group in range(GROUPS):
                low = group * LANES
                lanes = slice(low, low + LANES)
                queries = []
                for odd in range(2):
                    window = 2 * pair + odd
                    slot = pl.ds(pl.multiple_of(s * WROWS + window * SLOT, SLOT), SLOT)
                    out_rows = slice(window * SLOT, (window + 1) * SLOT)
                    q, v = qkv_ref[0, slot, :D], qkv_ref[0, slot, 2 * D :]
                    attend_b = att_ref[0, slot, group * WROWS : (group + 1) * WROWS]
                    attend = attend_b.astype(F32)
                    grad_att, spread_gm = window_scores(gm_all[out_rows], v, heads, group)
                    spread_q = jnp.concatenate([q[:, lanes]] * 4, axis=0) * heads
                    weighted = grad_att * attend
                    grad_s = (weighted - attend * jnp.sum(weighted, axis=0, keepdims=True)).astype(BF16)
                    joined[out_rows, lanes] = (dot(grad_s, spread_q) * SCALE).astype(BF16)
                    joined[out_rows, D + low : D + low + LANES] = dot(attend_b, spread_gm).astype(BF16)
                    queries.append(over_keys(kt_ref[0, s, lanes, columns], grad_s, odd))
                gqt[lanes, columns] = (own_heads(queries) * SCALE).astype(BF16)
        nw = nw_ref[0, window_rows, :]
        q_acc[...] += dot(gqt[...], nw)
        kv_acc[...] += dot_tn(nw, joined[...])
        unwound = dot_nt(back_ref[...], gqt[...]).astype(BF16)
        sums[:, :D] += folded(unwound.astype(F32))
        total = dot_nt(unwound, qkv_w[0, :, :D])
        unwound = dot(back_ref[...], joined[...]).astype(BF16)
        sums[:, 2 * D : 3 * D] += folded(unwound[:, D:].astype(F32))
        gn[pl.ds(s * WIN, WIN)] = (total + dot_nt(unwound, qkv_w[0, :, D:])).reshape(WIN, WIDE, D)

    gain = gain_ref[0:1, :]
    load_image(img_ref, imghalo_ref, side, ext)

    @pl.loop(0, rows, unroll=ROW_UNROLL)
    def _(r):
        grad = gn[r]
        back, gain_term = normalized_back(grad, pos_ref[0, r], gain)
        total = gres[r] + back
        gpos_ref[0, r] = total
        sums[:, D : 2 * D] += folded(gain_term)
        sums[:, 4 * D : 5 * D] += folded(grad)
        grad = total
        shifted = (pltpu.roll(grad, WIDE - 1, 0), grad, pltpu.roll(grad, 1, 0))
        for a in range(3):
            z = ext[r + a]
            for b in range(3):
                tap_one[3 * a + b] += folded(shifted[b] * z)
        tap_one[9] += folded(grad)

    put_border(border_ref, side, gpos_ref[0, 0], gpos_ref[0, rows - 1])

    @pl.when(last_step())
    def _():
        core = core_ref[0]
        pack_tiles(pack, core, 0, q_acc[...].T)
        pack_tiles(pack, core, D // LANES * D, kv_acc[...])
        pack_tiles(pack, core, 3 * D // LANES * D, out_acc[...])
        small[...] = jnp.zeros_like(small)
        small[0:8] = small_four[...]
        small[8:16] = small_five[...]
        small[16:40] = small_six[...]
        for j in range(5):
            small[40 + j : 41 + j, :] = jnp.sum(sums[:, j * D : (j + 1) * D], axis=0, keepdims=True)
        for j in range(10):
            small[48 + j : 49 + j, :] = jnp.sum(tap_acc[j], axis=0, keepdims=True)
            small[58 + j : 59 + j, :] = jnp.sum(tap_one[j], axis=0, keepdims=True)
        pack_tiles(pack, core, 4 * D // LANES * D, small[...])
        hand_out(pack, keep_ref, send_ref, sems)


def stage_eight(side_ref, g_ref, halo_ref, conv_ref, out_ref, ext):
    rows = g_ref.shape[1]
    load_rows(g_ref, halo_ref, side_ref[0], ext)
    kernel = taps(conv_ref, 0)

    @pl.loop(0, rows, unroll=ROW_UNROLL)
    def _(r):
        out_ref[r, :, pl.ds(pl.program_id(0), 1), :] = conv_row_back(ext, r, kernel)[:COLS].reshape(COLS, 1, D)


VMEM_LIMIT = 48 * 1024 * 1024


def per_image(shape):
    return pl.BlockSpec((1,) + tuple(shape[1:]), lambda i: (i,) + (0,) * (len(shape) - 1))


def whole(shape):
    return pl.BlockSpec(tuple(shape), lambda i: (0,) * len(shape))


def layer(array, index):
    shape = array.shape
    return pl.BlockSpec((1,) + tuple(shape[1:]), lambda i: (index,) + (0,) * (len(shape) - 1))


def scalar():
    return pl.BlockSpec(memory_space=pltpu.SMEM)


def call(body, images, in_specs, outs, scratch, microseconds, name):
    run = pl.pallas_call(
        body,
        name=name,
        grid=(images,),
        in_specs=in_specs,
        out_specs=[pl.BlockSpec(memory_space=pl.ANY) if own is None else per_image(shape) if own else whole(shape) for shape, _, own in outs],
        out_shape=[pltpu.HBM(shape, dtype) if large(shape) else jax.ShapeDtypeStruct(shape, dtype) for shape, dtype, _ in outs],
        scratch_shapes=scratch,
        compiler_params=pltpu.CompilerParams(dimension_semantics=("arbitrary",), vmem_limit_bytes=VMEM_LIMIT),
        cost_estimate=pl.CostEstimate(flops=microseconds * 1_150_000_000, bytes_accessed=1_000_000, transcendentals=0),
    )

    def placed(*arrays):
        return run(*(pltpu.with_memory_space_constraint(x, pltpu.HBM) if large(x.shape) and x.shape[0] == images else x for x in arrays))

    return placed


def large(shape):
    return np.prod(shape) > 1 << 18


def exchange(array):
    return lax.ppermute(array, "win", [(0, 1), (1, 0)])


def shards(images, valid_mask, cotangent, conv, gain, shift, qkv_w, bias, out_w, up_w, up_b, down_w, down_b):
    n, rows = images.shape[0], images.shape[1]
    side = lax.axis_index("win")
    side_arr = side.astype(jnp.int32).reshape(1)
    core_arr = (lax.axis_index("batch") % 2).astype(jnp.int32).reshape(1)
    perm, back, heads_w, heads_c = constants()
    wide = (n, rows, WIDE, D)
    inner = (rows, COLS, n, D)
    flat = rows * WIDE
    wflat = rows // WIN * WROWS
    border = (n, WIDE, D)
    valid = jnp.pad(valid_mask.astype(F32), ((0, 0), (0, 0), (0, WIDE - COLS))).reshape(n, flat, 1)
    ext = pltpu.VMEM((rows + 2, WIDE, D), F32)

    def vm(shape, dtype=F32):
        return pltpu.VMEM(shape, dtype)

    edge = jnp.where(side == 0, images[:, rows - 1], images[:, 0])
    img_halo = exchange(edge)
    small_params = [whole(conv.shape), whole(gain.shape)]

    turned = (n, rows // WIN, D, WROWS)
    pos_one, nw, qkv_one, kt, att, mix_one, res_one, edge = call(
        stage_one, n,
        [scalar(), per_image(images.shape), per_image(img_halo.shape), *small_params, whole(shift.shape), layer(qkv_w, 0),
         whole(bias.shape), layer(out_w, 0), whole(perm.shape), whole(back.shape),
         whole(heads_w.shape)],
        [(wide, F32, True), ((n, wflat, D), BF16, True), ((n, wflat, 3 * D), BF16, True), (turned, BF16, True),
         ((n, wflat, GROUPS * WROWS), BF16, True), (turned, BF16, True), (wide, F32, True), (border, BF16, True)],
        [ext, vm((flat, D), BF16), vm((D, WROWS), BF16), vm((2 * D, D), BF16), vm((D, LANES))], 23, "window_forward",
    )(side_arr, images, img_halo, conv, gain, shift, qkv_w, bias, out_w, perm, back, heads_w)

    halo = exchange(edge)
    pos_two, nrm_two, hid_one, der_one, res_two, edge = call(
        stage_two, n,
        [scalar(), per_image(wide), per_image(border), *small_params, whole(shift.shape), layer(up_w, 0), whole(up_b.shape),
         layer(down_w, 0), whole(down_b.shape)],
        [(wide, F32, True), ((n, flat, D), BF16, True), ((n, flat, FF), BF16, True), ((n, flat, FF), BF16, True), (wide, F32, True),
         (border, BF16, True)],
        [ext], 20, "mlp_one_forward",
    )(side_arr, res_one, halo, conv, gain, shift, up_w, up_b, down_w, down_b)

    halo = exchange(edge)
    gram_shape = (n, GROUPS * HD, LANES)
    pos_three, nrm_three, qkv_two, gram = call(
        stage_three, n,
        [scalar(), per_image(wide), per_image(border), *small_params, whole(shift.shape), layer(qkv_w, 1), whole(bias.shape),
         per_image(valid.shape), whole(heads_c.shape)],
        [(wide, F32, True), ((n, flat, D), BF16, True), ((n, flat, 3 * D), BF16, True), (gram_shape, F32, True)],
        [ext], 11, "channel_gram",
    )(side_arr, res_two, halo, conv, gain, shift, qkv_w, bias, valid, heads_c)

    gram_other = exchange(gram)

    devices = 2 * lax.axis_size("batch")
    four_rows = -(-MLP_PACK // devices) * devices

    def pack_outs(rows_in_pack):
        return [((rows_in_pack // 2, LANES), BF16, None)] * 2

    def pack_scratch(rows_in_pack):
        return [vm((2, rows_in_pack // 2, LANES), BF16), pltpu.SemaphoreType.DMA((2,))]

    output, gres_three, gm_two, gchan, *four, small_four = call(
        stage_four, n,
        [scalar(), per_image(wide), per_image(qkv_two.shape), per_image(gram_shape), per_image(gram_shape),
         per_image(cotangent.shape), layer(out_w, 1), whole(bias.shape), whole(gain.shape), whole(shift.shape), layer(up_w, 1),
         whole(up_b.shape), layer(down_w, 1), whole(down_b.shape), whole(heads_c.shape)],
        [(inner, F32, False), (wide, F32, True), ((n, flat, D), BF16, True), (gram_shape, F32, True),
         *pack_outs(four_rows), ((8, D), F32, False)],
        [*pack_scratch(four_rows), vm((flat, D), BF16), vm((rows, WIDE, D)), vm((flat, D), BF16), vm((rows, WIDE, D)),
         vm((flat, D), BF16), vm((flat, FF), BF16), vm((flat, FF), BF16), vm((rows, WIDE, D)), vm((flat, D), BF16),
         vm((D, FF)), vm((D, FF)), vm((D, D)), vm((8, FF + 4 * D))],
        36, "mlp_two",
    )(core_arr, pos_three, qkv_two, gram, gram_other, cotangent, out_w, bias, gain, shift, up_w, up_b, down_w, down_b,
      heads_c)

    trade = Trade()
    gchan_other = exchange(gchan)
    four = start_sum(trade, four)
    far = range(2, len(trade.order))
    gpos_three, edge, *five, small_five = call(
        stage_five, n,
        [scalar(), scalar(), per_image(wide), per_image(wide), per_image(nrm_three.shape), per_image(qkv_two.shape),
         per_image(gm_two.shape), per_image(gram_shape), per_image(gram_shape), per_image(gram_shape), per_image(gram_shape),
         per_image(valid.shape), layer(qkv_w, 1), whole(gain.shape), whole(heads_c.shape)],
        [(wide, F32, True), (border, BF16, True), *pack_outs(PIECES[0]), ((8, D), F32, False)],
        [*pack_scratch(PIECES[0]), vm((flat, 3 * D), BF16), vm((rows, WIDE, D)), vm((D, 3 * D)), vm((8, 5 * D))],
        13, "channel_backward",
    )(side_arr, core_arr, gres_three, pos_three, nrm_three, qkv_two, gm_two, gram, gram_other, gchan, gchan_other, valid, qkv_w,
      gain, heads_c)

    halo, four = lax.optimization_barrier((exchange(edge), four))
    four = trade.halve(four, far[0])
    five = start_sum(trade, five)
    gpos_two, edge, *six, small_six = call(
        stage_six, n,
        [scalar(), scalar(), per_image(wide), per_image(border), per_image(wide), per_image(wide), per_image(nrm_two.shape),
         per_image(hid_one.shape), per_image(der_one.shape), *small_params, layer(up_w, 0), layer(down_w, 0)],
        [(wide, F32, True), (border, BF16, True), *pack_outs(PIECES[1]), ((24, D), F32, False)],
        [*pack_scratch(PIECES[1]), ext, vm((rows, WIDE, D)), vm((flat, D), BF16), vm((flat, FF), BF16), vm((rows, WIDE, D)),
         vm((D, FF)), vm((D, FF)), vm((8, FF + 3 * D)), vm((10, 8, D))], 23, "mlp_one_backward",
    )(side_arr, core_arr, gpos_three, halo, res_two, pos_two, nrm_two, hid_one, der_one, conv, gain, up_w, down_w)

    halo, four, five = lax.optimization_barrier((exchange(edge), four, five))
    for step in far[1:]:
        four = trade.halve(four, step)
    five = trade.halve(five, 0)
    six = start_sum(trade, six)
    gpos_one, edge, *seven = call(
        stage_seven, n,
        [scalar(), scalar(), whole((8, D)), whole((8, D)), whole((24, D)), per_image(wide), per_image(border), per_image(wide),
         per_image(wide), per_image(images.shape), per_image(img_halo.shape), per_image(nw.shape), per_image(qkv_one.shape),
         per_image(turned), per_image(att.shape), per_image(mix_one.shape), *small_params, layer(qkv_w, 0), layer(out_w, 0), whole(perm.shape),
         whole(back.shape), whole(heads_w.shape)],
        [(wide, F32, True), (border, BF16, True), *pack_outs(PIECES[2])],
        [*pack_scratch(PIECES[2]), ext, vm((rows, WIDE, D)), vm((flat, D), BF16), vm((WROWS, 2 * D), BF16), vm((D, WROWS), BF16),
         vm((rows, WIDE, D)), vm((D, D)), vm((D, 2 * D)), vm((D, D)), vm((8, 5 * D)), vm((10, 8, D)), vm((10, 8, D)), vm((80, D))],
        35, "window_backward",
    )(side_arr, core_arr, small_four, small_five, small_six, gpos_two, halo, res_one, pos_one, images, img_halo, nw, qkv_one, kt, att,
      mix_one, conv, gain, qkv_w, out_w, perm, back, heads_w)

    four, five, six, gpos_one, edge, *seven = lax.optimization_barrier((four, five, six, gpos_one, edge, *seven))
    halo, five, six, seven = lax.optimization_barrier((exchange(edge), five, six, start_sum(trade, seven)))
    (images_grad,) = call(
        stage_eight, n, [scalar(), per_image(wide), per_image(border), whole(conv.shape)], [(inner, F32, False)], [ext],
        5, "images_backward",
    )(side_arr, gpos_one, halo, conv)

    five = trade.halve(five, 1)
    six, seven = (trade.halve(trade.halve(x, 0), 1) for x in (six, seven))
    x, four = lax.optimization_barrier((jnp.concatenate([five, six, seven], axis=0), four))
    x = trade.halve(x, far[0])
    x, images_grad = lax.optimization_barrier((x, images_grad))
    for step in far[1:]:
        x = trade.halve(x, step)
    for step in far[::-1]:
        x = trade.join(x, step)
    for step in (0, 1):
        four = trade.halve(four, step)
    for step in (1, 0):
        four = trade.join(four, step)
    x, four = lax.optimization_barrier((x, four))
    output, images_grad = (jnp.transpose(x, (2, 0, 1, 3)) for x in (output, images_grad))
    return (output, images_grad, *finish_sum(trade, x, four))


MATRIX = {"up": FF // LANES * D, "down": FF // LANES * D, "out": D // LANES * D, "qkv": 3 * D // LANES * D}
PIECES = (
    MATRIX["qkv"],
    MATRIX["up"] + MATRIX["down"],
    MATRIX["qkv"] + MATRIX["out"] + 640,
)
STARTS = tuple(sum(PIECES[:i]) for i in range(len(PIECES)))
TOTAL = sum(PIECES)
MLP_PACK = MATRIX["up"] + MATRIX["down"] + MATRIX["out"]
ROW_UNROLL = 14


class Trade:
    def __init__(self):
        self.batch = lax.axis_size("batch")
        self.place, self.win = lax.axis_index("batch"), lax.axis_index("win")
        self.core = self.place % 2
        bits = list(range((self.batch // 2).bit_length() - 1))
        one, two = ["w", *bits], [*bits[:1], "w", *bits[1:]]
        self.order = list(zip(one, two))
        self.bits = [self.bit(axes, self.core) for axes in self.order]

    def __call__(self, value, axes):
        pairs = []
        for b in range(self.batch):
            for w in range(2):
                axis = axes[b % 2]
                to = (b ^ 1, w) if axis == "c" else (b, 1 - w) if axis == "w" else (b ^ (2 << axis), w)
                pairs.append((2 * b + w, 2 * to[0] + to[1]))
        return lax.ppermute(value, ("batch", "win"), pairs)

    def of(self, axis):
        return self.win if axis == "w" else (self.place // (2 << axis)) % 2

    def bit(self, axes, core):
        return jnp.where(core == 0, self.of(axes[0]), self.of(axes[1]))

    def halve(self, x, step):
        half = x.shape[0] // 2
        sent = lax.dynamic_slice_in_dim(x, (1 - self.bits[step]) * half, half, 0)
        kept = lax.dynamic_slice_in_dim(x, self.bits[step] * half, half, 0)
        return added(kept, self(sent, self.order[step]))

    def join(self, x, step):
        got, lower = self(x, self.order[step]), self.bits[step] == 0
        return jnp.concatenate([jnp.where(lower, x, got), jnp.where(lower, got, x)], axis=0)


def added(left, right):
    return (left.astype(F32) + right.astype(F32)).astype(BF16)


def start_sum(trade, pack):
    keep, send = pack
    return added(keep, trade(send, ("c", "c")))


def finish_sum(trade, x, four):
    far = range(2, len(trade.order))
    one = [x, trade(x, trade.order[1])]
    mine = one + [trade(block, trade.order[0]) for block in one]
    theirs = [trade(block, ("c", "c")) for block in mine]
    where = []
    for core in (trade.core, 1 - trade.core):
        first, second = (trade.bit(trade.order[step], core) for step in range(2))
        for flip_first in range(2):
            for flip_second in range(2):
                where.append(core * 4 + (first ^ flip_first) * 2 + (second ^ flip_second))
    for step in far[:0:-1]:
        four = trade.join(four, step)
    pair = [four, trade(four, trade.order[far[0]])]
    fours = pair + [trade(block, ("c", "c")) for block in pair]
    bit = trade.bits[far[0]]
    where_four = [core * 2 + (bit ^ flip) for core in (trade.core, 1 - trade.core) for flip in range(2)]
    first = unpack_four(jnp.stack(where_four).astype(jnp.int32), fours)
    return unpack_rest(jnp.stack(where).astype(jnp.int32), mine + theirs, first)


UP, DOWN, OUT, QKV = (2, D, FF), (2, FF, D), (2, D, D), (2, D, 3 * D)


def unpack_four_kernel(where_ref, *refs):
    blocks, (up_out, down_out, out_out), (buf, sems) = refs[:4], refs[4:7], refs[7:]
    size = blocks[0].shape[0]
    copies = []
    for t, block in enumerate(blocks):
        target = pl.ds(pl.multiple_of(where_ref[t] * size, 16), size)
        copies.append(pltpu.make_async_copy(block, buf.at[target], sems.at[t]))
    for copy in copies:
        copy.start()
    for copy in copies:
        copy.wait()
    start = 0
    for ref in (up_out, down_out, out_out):
        height, width = ref.shape[1:]
        for j in range(width // LANES):
            ref[0, :, j * LANES : (j + 1) * LANES] = buf[start : start + height, :].astype(F32)
            start += height


def unpack_four(where, blocks):
    shapes = (UP, DOWN, OUT)
    return pl.pallas_call(
        unpack_four_kernel,
        name="unpack_four",
        grid=(1,),
        in_specs=[scalar()] + [pl.BlockSpec(memory_space=pl.ANY)] * 4,
        out_specs=[pl.BlockSpec((1,) + shape[1:], lambda i: (1, 0, 0)) for shape in shapes],
        out_shape=[jax.ShapeDtypeStruct(shape, F32) for shape in shapes],
        scratch_shapes=[pltpu.VMEM((4 * blocks[0].shape[0], LANES), BF16), pltpu.SemaphoreType.DMA((4,))],
        compiler_params=pltpu.CompilerParams(vmem_limit_bytes=VMEM_LIMIT),
    )(where, *blocks)


def unpack_rest_kernel(where_ref, *refs):
    blocks, outs, (buf, up_buf, down_buf, out_buf, sems, out_sems) = refs[:8], refs[11:21], refs[21:]
    up_out, down_out, out_out, conv_out, gain_out, shift_out, qkv_out, bias_out, upb_out, downb_out = outs
    copies = []
    for p, piece in enumerate(PIECES):
        size, source = piece // 8, STARTS[p] // 8
        for t, block in enumerate(blocks):
            target = pl.ds(pl.multiple_of(STARTS[p] + where_ref[t] * size, 16), size)
            copies.append(pltpu.make_async_copy(block.at[source : source + size], buf.at[target], sems.at[t, p]))
    order = (1, 2, 0)
    for p in order:
        for copy in copies[8 * p : 8 * p + 8]:
            copy.start()

    def arrived(p):
        for copy in copies[8 * p : 8 * p + 8]:
            copy.wait()

    def matrix(store, height, width, start):
        for j in range(width // LANES):
            low = start + j * height
            store(slice(j * LANES, (j + 1) * LANES), buf[low : low + height, :].astype(F32))

    def into(ref, *index):
        def store(lanes, value):
            ref[(*index, slice(None), lanes)] = value

        return store

    sent = []

    def send(source, target):
        copy = pltpu.make_async_copy(source, target.at[0], out_sems.at[len(sent)])
        copy.start()
        sent.append(copy)

    arrived(1)
    matrix(into(up_buf), D, FF, STARTS[1])
    send(up_buf, up_out)
    matrix(into(down_buf), FF, D, STARTS[1] + MATRIX["up"])
    send(down_buf, down_out)
    arrived(2)
    matrix(into(out_buf), D, D, STARTS[2] + MATRIX["qkv"])
    send(out_buf, out_out)
    matrix(into(qkv_out, 0), D, 3 * D, STARTS[2])
    base = STARTS[2] + MATRIX["qkv"] + MATRIX["out"]
    for j in range(GROUPS):
        lanes = slice(j * LANES, (j + 1) * LANES)
        small = buf[base + j * 80 : base + (j + 1) * 80, :].astype(F32)
        for index, first in enumerate((58, 48, 24)):
            conv_out[:, index : index + 1, lanes] = small[first : first + 10].reshape(10, 1, LANES)
        for ref, rows in ((gain_out, (41, 21, 11, 5)), (shift_out, (44, 22, 12, 6)), (bias_out, (40, 42, 43, 8, 9, 10, 7)),
                          (downb_out, (20, 4))):
            for index, row in enumerate(rows):
                ref[index : index + 1, lanes] = small[row : row + 1]
        for index, first in enumerate((16, 0)):
            for r in range(FF // D):
                low = r * D + j * LANES
                upb_out[index : index + 1, low : low + LANES] = small[first + r : first + r + 1]
    arrived(0)
    matrix(into(qkv_out, 1), D, 3 * D, STARTS[0])
    for copy in sent:
        copy.wait()


def unpack_rest(where, blocks, first):
    shapes = [UP, DOWN, OUT, (10, 3, D), (4, D), (4, D), QKV, (7, D), (2, FF), (2, D)]
    hbm, vmem = pl.BlockSpec(memory_space=pl.ANY), pl.BlockSpec(memory_space=pltpu.VMEM)
    up, down, out, conv, gain, shift, qkv, bias, up_bias, down_bias = pl.pallas_call(
        unpack_rest_kernel,
        name="unpack_rest",
        in_specs=[pl.BlockSpec(memory_space=pltpu.SMEM)] + [hbm] * 11,
        out_specs=[hbm] * 3 + [vmem] * 7,
        out_shape=[jax.ShapeDtypeStruct(shape, F32) for shape in shapes],
        input_output_aliases={9: 0, 10: 1, 11: 2},
        scratch_shapes=[pltpu.VMEM((TOTAL, LANES), BF16), pltpu.VMEM((D, FF), F32), pltpu.VMEM((FF, D), F32), pltpu.VMEM((D, D), F32),
                        pltpu.SemaphoreType.DMA((8, len(PIECES))), pltpu.SemaphoreType.DMA((3,))],
        compiler_params=pltpu.CompilerParams(vmem_limit_bytes=VMEM_LIMIT),
    )(where, *blocks, *first)
    return conv.transpose(1, 0, 2), gain, shift, qkv, bias, out, up, up_bias, down, down_bias


def solution(mesh):
    split = P("batch", "win", None, None)
    in_specs = (split, P("batch", "win", None), split) + (P(),) * 10
    out_specs = (split, split) + (P(),) * 10
    return jax.shard_map(shards, mesh=mesh, in_specs=in_specs, out_specs=out_specs, check_vma=False)
```
